32 devices in a mesh: dp: 4 (over y, x), ctx: 8 (over z, core).
Axes of the slice: x: 2, y: 2, z: 4, core: 2. Of those that a mesh axis runs over, the one named last changes fastest.
Arguments:
- tokens: bfloat16 [8, 4096, 768], P('dp', 'ctx'), may hold values from -6 to 6
- cotangent: bfloat16 [8, 4096, 768], P('dp', 'ctx'), may hold values from -6 to 6
- lengths: int32 [8], P('dp'), may hold values from 1024 to 4096, as said below
- block_order: int32 [8, 8], P('dp'), may hold values from 0 to 7, each once within a row
- qkv_weight: bfloat16 [768, 2304], P('dp'), may hold values from -0.21875 to 0.21875
- query_bias: bfloat16 [768], P('dp'), may hold values from -4 to 4
- value_bias: bfloat16 [768], P('dp'), may hold values from -0.15625 to 0.15625
- out_weight: bfloat16 [768, 768], P('dp'), may hold values from -6 to 6
- out_bias: bfloat16 [768], P('dp'), may hold values from -4 to 4
- attn_gain: bfloat16 [768], P('dp'), may hold values from 0.5 to 1.5
- attn_shift: bfloat16 [768], P('dp'), may hold values from -1.5 to 1.5
- up_weight: bfloat16 [768, 3072], P('dp'), may hold values from -0.21875 to 0.21875
- up_bias: bfloat16 [3072], P('dp'), may hold values from -1.5 to 1.5
- down_weight: bfloat16 [3072, 768], P('dp'), may hold values from -0.15625 to 0.15625
- down_bias: bfloat16 [768], P('dp'), may hold values from -1.5 to 1.5
- ffn_gain: bfloat16 [768], P('dp'), may hold values from 0.5 to 1.5
- ffn_shift: bfloat16 [768], P('dp'), may hold values from -1.5 to 1.5
Outputs:
- output: bfloat16 [8, 4096, 768], P('dp', 'ctx')
- grad_tokens: bfloat16 [8, 4096, 768], P('dp', 'ctx')
- grad_qkv_weight: float32 [768, 2304], P('dp')
- grad_query_bias: float32 [768], P('dp')
- grad_value_bias: float32 [768], P('dp')
- grad_out_weight: float32 [768, 768], P('dp')
- grad_out_bias: float32 [768], P('dp')
- grad_attn_gain: float32 [768], P('dp')
- grad_attn_shift: float32 [768], P('dp')
- grad_up_weight: float32 [768, 3072], P('dp')
- grad_up_bias: float32 [3072], P('dp')
- grad_down_weight: float32 [3072, 768], P('dp')
- grad_down_bias: float32 [768], P('dp')
- grad_ffn_gain: float32 [768], P('dp')
- grad_ffn_shift: float32 [768], P('dp')
- branch_rms: float32 [8, 3], P('dp')
The draws below stay inside these ranges and needn't reach their ends.
Inputs may be any that keep to these rules, and one draw needn't show every extreme that they name: `lengths`: some sequence has exactly 4096 valid slots and some exactly 1024. Each row is a permutation: index c of ctx holds positions block_order[s, c] * 512 to block_order[s, c] * 512 + 511 of sequence s.
All inputs are finite; a program needn't handle non-finite values.
Results may differ from the reference program's by a relative error of at most 0.02.
Values may be sent and summed in bfloat16 or wider, within the bound.
A program may use at most 256 MiB of HBM per device.

```python
import jax
import jax.numpy as jnp
from jax import lax

HEADS = 12
D = 768
FF = 3072
SEQ_LEN = 4096
SEQS = 8
N_CTX = 8


def draw_lengths(key, part):
    least = SEQ_LEN // 4
    values = jax.random.randint(key, (SEQS,), least, SEQ_LEN + 1, dtype=jnp.int32)
    first = jax.random.randint(jax.random.fold_in(key, 7), (), 0, SEQS, dtype=jnp.int32)
    values = values.at[first].set(SEQ_LEN)
    return values.at[(first + 1) % SEQS].set(least)


def spiked(array, own_key, source, target, shards_of, factor):
    owner, partner = [(jnp.arange(array.shape[position]) // (array.shape[position] // shards_of)).reshape([-1 if axis == position else 1 for axis in range(array.ndim)]) for position in (source, target)]
    chosen = jax.random.permutation(own_key, shards_of)[partner]
    strong = (owner == chosen) | (owner == (partner + shards_of // 2) % shards_of)
    return jnp.where(strong, factor * array, array)


def level_of(stream_key, extent, split, smallest, largest):
    def one(dim, parts):
        draws = jax.random.uniform(jax.random.fold_in(jax.random.fold_in(stream_key, 6), dim), (parts,), jnp.float32, smallest / len(split), largest / len(split))
        return jnp.repeat(jnp.exp(draws), extent[dim] // parts).reshape((-1,) + (1,) * (len(extent) - dim - 1))

    loudness = one(*split[0])
    for cut in split[1:]:
        loudness = loudness * one(*cut)
    return loudness


def gaussian(key, dims, deviation, most, shards=(), kind=jnp.bfloat16):
    level = level_of(key, dims, shards, -0.22, 0.18) if shards else 1.0
    array = jax.random.normal(key, dims, jnp.float32) * deviation * level
    return jnp.minimum(jnp.maximum(array, -most), most).astype(kind)


def noise_with(stream_key, dims, scale, reach, shards, heavy, kind=jnp.bfloat16):
    values = scale * jax.random.normal(stream_key, dims, jnp.float32)
    if shards:
        values = values * level_of(stream_key, dims, shards, -0.22, 0.18)
    return jnp.clip(spiked(values, jax.random.fold_in(stream_key, 3), *heavy), -reach, reach).astype(kind)


def setup_inputs(seed: int = 0) -> dict:
    splits = jax.random.split(jax.random.key(seed), 18)
    tokens = gaussian(splits[0], (SEQS, SEQ_LEN, D), 1.0, 6.0, ((0, 4), (1, 8)))
    cotangent = noise_with(splits[1], (SEQS, SEQ_LEN, D), 1.0, 6.0, ((0, 4), (1, 8)), (0, 2, 4, 2.0))
    lengths = draw_lengths(jax.random.fold_in(splits[17], 71), 0)
    block_order = jax.vmap(lambda own: jax.random.permutation(own, N_CTX))(jax.random.split(splits[3], SEQS)).reshape((SEQS, N_CTX)).astype(jnp.int32)
    qkv_weight = gaussian(splits[4], (D, 3 * D), D ** -0.5, 0.21875, ((0, 4),))
    query_bias = gaussian(splits[5], (D,), 0.3, 4.0, ((0, 4),))
    value_bias = gaussian(splits[6], (D,), 0.01, 0.15625, ((0, 4),))
    out_weight = gaussian(splits[7], (D, D), 1 ** -0.5, 6.0, ((0, 4),))
    out_bias = gaussian(splits[8], (D,), 0.3, 4.0, ((0, 4),))
    attn_gain = jnp.clip(1.0 + 0.1 * jax.random.normal(splits[9], (D,), jnp.float32), 0.5, 1.5).astype(jnp.bfloat16)
    attn_shift = gaussian(splits[10], (D,), 0.1, 1.5, ((0, 4),))
    up_weight = gaussian(splits[11], (D, FF), D ** -0.5, 0.21875, ((0, 4),))
    up_bias = gaussian(splits[12], (FF,), 0.1, 1.5, ((0, 4),))
    down_weight = gaussian(splits[13], (FF, D), (FF // 2) ** -0.5, 0.15625, ((0, 4),))
    down_bias = gaussian(splits[14], (D,), 0.1, 1.5, ((0, 4),))
    ffn_gain = jnp.clip(1.0 + 0.1 * jax.random.normal(splits[15], (D,), jnp.float32), 0.5, 1.5).astype(jnp.bfloat16)
    ffn_shift = gaussian(splits[16], (D,), 0.1, 1.5, ((0, 4),))
    return {"tokens": tokens, "cotangent": cotangent, "lengths": lengths, "block_order": block_order, "qkv_weight": qkv_weight, "query_bias": query_bias, "value_bias": value_bias, "out_weight": out_weight, "out_bias": out_bias, "attn_gain": attn_gain, "attn_shift": attn_shift, "up_weight": up_weight, "up_bias": up_bias, "down_weight": down_weight, "down_bias": down_bias, "ffn_gain": ffn_gain, "ffn_shift": ffn_shift}


norm_eps = 1e-12
rms_eps = 1e-06
highest = lax.Precision.HIGHEST

@jax.custom_vjp
def low(v):
    return lax.optimization_barrier(v.astype(jnp.bfloat16)).astype(jnp.float32)

@jax.custom_vjp
def low_back(v):
    return v

def low_keep(v):
    return (low(v), None)

def low_pass(kept, grad):
    return (grad,)

def back_keep(v):
    return (v, None)

def back_low(kept, grad):
    return (low(grad),)
low.defvjp(low_keep, low_pass)
low_back.defvjp(back_keep, back_low)

def layer_norm(total, gain, shift):
    mean = lax.optimization_barrier(jnp.mean(total, axis=-1, keepdims=True))
    centred = total - mean
    spread = lax.optimization_barrier(jnp.mean(centred * centred, axis=-1, keepdims=True))
    return centred * lax.rsqrt(spread + norm_eps) * gain + shift

def product(left, right):
    return jnp.dot(left, right, precision=highest)

def layer(params, rows, live):
    qkv_weight, query_bias, value_bias, out_weight, out_bias, attn_gain, attn_shift, up_weight, up_bias, down_weight, down_bias, ffn_gain, ffn_shift = params
    width = rows.shape[1]
    head_dim = width // HEADS
    scale = head_dim ** (-0.5)
    projected = product(rows, qkv_weight)
    queries = low_back(low(projected[:, :width] + query_bias))
    keys = low_back(low(projected[:, width:2 * width]))
    values = low_back(low(projected[:, 2 * width:] + value_bias))
    key_heads = keys.reshape(SEQ_LEN, HEADS, head_dim)
    value_heads = values.reshape(SEQ_LEN, HEADS, head_dim)
    step = min(512, SEQ_LEN)

    def attend(query_block):
        scores = jnp.einsum('qhd,khd->hqk', query_block, key_heads, precision=highest) * scale
        scores = jnp.where(live[None, None, :], low_back(scores), -1e+30)
        totals = jax.nn.logsumexp(scores, axis=2, keepdims=True)
        weights = low(jnp.exp(scores - totals))
        return jnp.einsum('hqk,khd->qhd', weights, value_heads, precision=highest)
    mixed = lax.map(jax.checkpoint(attend), queries.reshape(SEQ_LEN // step, step, HEADS, head_dim))
    mixed = low_back(low(mixed.reshape(SEQ_LEN, width)))
    attn = low_back(product(mixed, out_weight) + out_bias)
    hidden = layer_norm(rows + attn, attn_gain, attn_shift)
    upper = low_back(product(low(hidden), up_weight) + up_bias)
    active = low(jax.nn.gelu(upper, approximate=False))
    branch = low_back(product(active, down_weight) + down_bias)
    keep_rows = jnp.where(live[:, None], 1.0, 0.0).astype(rows.dtype)
    result = layer_norm(hidden + branch, ffn_gain, ffn_shift) * keep_rows
    squares = jnp.stack([jnp.sum(result * result), jnp.sum(attn * attn * keep_rows), jnp.sum(branch * branch * keep_rows)])
    return (result, squares)

def reference(tokens, cotangent, lengths, block_order, qkv_weight, query_bias, value_bias, out_weight, out_bias, attn_gain, attn_shift, up_weight, up_bias, down_weight, down_bias, ffn_gain, ffn_shift):
    params = tuple((item.astype(jnp.float32) for item in (qkv_weight, query_bias, value_bias, out_weight, out_bias, attn_gain, attn_shift, up_weight, up_bias, down_weight, down_bias, ffn_gain, ffn_shift)))
    block = SEQ_LEN // N_CTX
    slots = jnp.arange(SEQ_LEN, dtype=jnp.int32)

    def one_sequence(carry, item):
        rows, grads_out, length, order = item
        places = order[slots // block] * block + slots % block
        live = places < length

        def run(weights, inputs):
            return layer(weights, inputs, live)
        result, pull, squares = jax.vjp(run, params, rows.astype(jnp.float32), has_aux=True)
        grads, grad_rows = pull(grads_out.astype(jnp.float32))
        carry = jax.tree.map(jnp.add, carry, grads)
        rms = jnp.sqrt(squares / (length.astype(jnp.float32) * rows.shape[1]) + rms_eps)
        return (carry, (result.astype(jnp.bfloat16), grad_rows.astype(jnp.bfloat16), rms))
    zeros = tuple((jnp.zeros_like(item) for item in params))
    totals, (output, grad_tokens, branch_rms) = lax.scan(one_sequence, zeros, (tokens, cotangent, lengths, block_order))
    return (output, grad_tokens, totals[0], totals[1], totals[2], totals[3], totals[4], totals[5], totals[6], totals[7], totals[8], totals[9], totals[10], totals[11], totals[12], branch_rms)
```

```python
import functools

import jax
import jax.numpy as jnp
from jax import lax
from jax.experimental import pallas as pl
from jax.experimental.pallas import tpu as pltpu
from jax.sharding import PartitionSpec as P

HEADS = 12

norm_eps = 1e-12
rms_eps = 1e-06
masked_bias = -1e30
log2_e = 1.4426950408889634
lanes = 128
vmem_grant = 56 << 20
f32 = jnp.float32
bf16 = jnp.bfloat16


def norm_parts(total, gain, shift):
    mean = jnp.mean(total, axis=-1, keepdims=True)
    centred = total - mean
    inverse = lax.rsqrt(jnp.mean(centred * centred, axis=-1, keepdims=True) + norm_eps)
    unit = centred * inverse
    return (unit * gain + shift, unit, inverse)


def norm_back(grad_unit, unit, inverse):
    mean_grad = jnp.mean(grad_unit, axis=-1, keepdims=True)
    mean_cross = jnp.mean(grad_unit * unit, axis=-1, keepdims=True)
    return inverse * (grad_unit - mean_grad - unit * mean_cross)


def dot(left, right, left_dim, right_dim):
    return lax.dot_general(
        left, right, (((left_dim,), (right_dim,)), ((), ())), preferred_element_type=f32
    )


def head_lanes(head, head_dim):
    lane = lax.broadcasted_iota(jnp.int32, (1, lanes), 1)
    return (lane // head_dim) == head


def spread_lanes(first_head, second_head, unit, head_dim):
    rows = first_head.shape[0]
    lane = lax.broadcasted_iota(jnp.int32, (rows, lanes), 1)
    place = lane % head_dim
    value = -jnp.where(lane < head_dim, second_head, first_head)
    high = value.astype(bf16).astype(f32)
    rest = value - high
    mid = rest.astype(bf16).astype(f32)
    low = rest - mid
    out = jnp.where(place == 1, high, jnp.where(place == 2, mid, jnp.where(place == 3, low, 0.0)))
    return jnp.where(place == 0, unit, out).astype(bf16)


def attend_kernel(scale, head_dim, step, q_ref, k_ref, v_ref, extra_ref, o_ref, stat_ref, kb, vb):
    keys = k_ref.shape[0]

    @pl.when(pl.program_id(1) == 0)
    def _():
        for h in range(2):
            kb[h] = jnp.where(head_lanes(h, head_dim), k_ref[...], extra_ref[...])
            vb[h] = jnp.where(head_lanes(h, head_dim), v_ref[...], extra_ref[...])

    factor = scale * log2_e
    queries = q_ref[...]
    lane = lax.broadcasted_iota(jnp.int32, (1, lanes), 1)
    bias_lane = jnp.where(lane % head_dim == 0, 1.0, 0.0).astype(bf16)
    outs, logs = ([], [])
    for h in range(2):
        own = jnp.where(head_lanes(h, head_dim), queries, bias_lane)
        best, acc = (None, None)
        for first in range(0, keys, step):
            scores = dot(own, kb[h, first : first + step, :], 1, 1)
            high = jnp.max(scores, axis=1, keepdims=True)
            new_best = high if best is None else jnp.maximum(best, high)
            weights = jnp.exp2((scores - new_best) * factor).astype(bf16)
            part = dot(weights, vb[h, first : first + step, :], 1, 0)
            acc = part if best is None else acc * jnp.exp2((best - new_best) * factor) + part
            best = new_best
        free = (1 - h) * head_dim + 1
        total = acc[:, free : free + 1]
        outs.append(acc / total)
        logs.append(best + jnp.log2(total) * (1.0 / factor))
    o_ref[...] = jnp.where(head_lanes(0, head_dim), outs[0], outs[1]).astype(bf16)
    stat_ref[...] = spread_lanes(logs[0], logs[1], 1.0, head_dim)


def attend(queries, both, extra, head_dim):
    rows, width = queries.shape
    keys = both.shape[0]
    pairs = width // lanes
    row_step = min(512, rows)
    step = min(2048, keys)
    scale = head_dim ** (-0.5)
    return pl.pallas_call(
        functools.partial(attend_kernel, scale, head_dim, step),
        grid=(pairs, rows // row_step),
        in_specs=[
            pl.BlockSpec((row_step, lanes), lambda h, i: (i, h)),
            pl.BlockSpec((keys, lanes), lambda h, i: (0, h)),
            pl.BlockSpec((keys, lanes), lambda h, i: (0, h + pairs)),
            pl.BlockSpec((keys, lanes), lambda h, i: (0, 0)),
        ],
        out_specs=[
            pl.BlockSpec((row_step, lanes), lambda h, i: (i, h)),
            pl.BlockSpec((None, row_step, lanes), lambda h, i: (h, i, 0)),
        ],
        out_shape=[
            jax.ShapeDtypeStruct((rows, width), bf16),
            jax.ShapeDtypeStruct((pairs, rows, lanes), bf16),
        ],
        scratch_shapes=[pltpu.VMEM((2, keys, lanes), bf16), pltpu.VMEM((2, keys, lanes), bf16)],
        compiler_params=pltpu.CompilerParams(vmem_limit_bytes=vmem_grant),
        cost_estimate=pl.CostEstimate(
            flops=4 * rows * keys * width * 4,
            bytes_accessed=keys * width * 4 + rows * width * 6,
            transcendentals=rows * keys * width // head_dim,
        ),
        name="attend",
    )(queries, both, both, extra)


def attend_back_kernel(scale, head_dim, row_step, resumed, *refs):
    q_ref, da_ref, qx_ref, dax_ref, k_ref, v_ref, extra_ref = refs[:7]
    start_ref = refs[7] if resumed else None
    dq_ref, dkv_ref = refs[-2:]
    j = pl.program_id(1)
    rows = q_ref.shape[0]
    factor = scale * log2_e
    keys, values, extra = (k_ref[...], v_ref[...], extra_ref[...])
    dk, dv = (None, None)
    for first in range(0, rows, row_step):
        part = slice(first, first + row_step)
        queries, grads = (q_ref[part, :], da_ref[part, :])
        queries_extra, grads_extra = (qx_ref[part, :], dax_ref[part, :])
        dq = None
        for h in range(2):
            sel = head_lanes(h, head_dim)
            scores = dot(
                jnp.where(sel, queries, queries_extra), jnp.where(sel, keys, extra), 1, 1
            )
            weights = jnp.exp2(scores * factor)
            grad_weights = dot(
                jnp.where(sel, grads, grads_extra), jnp.where(sel, values, extra), 1, 1
            )
            grad_scores = (weights * grad_weights).astype(bf16)
            none = jnp.zeros_like(queries)
            part_dv = dot(jnp.where(sel, grads, none), weights.astype(bf16), 0, 0)
            part_dk = dot(jnp.where(sel, queries, none), grad_scores, 0, 0)
            part_dq = dot(grad_scores, jnp.where(sel, keys, jnp.zeros_like(keys)), 1, 0)
            dv = part_dv if dv is None else dv + part_dv
            dk = part_dk if dk is None else dk + part_dk
            dq = part_dq if dq is None else dq + part_dq
        dq = dq * scale

        @pl.when(j == 0)
        def _():
            dq_ref[part, :] = dq + start_ref[part, :] if resumed else dq

        @pl.when(j > 0)
        def _():
            dq_ref[part, :] += dq

    dkv_ref[0] = (dk * scale).astype(bf16)
    dkv_ref[1] = dv.astype(bf16)


def attend_back(queries, grads, stats, deltas, both, extra, head_dim, first, count, start):
    rows, width = queries.shape
    pairs = width // lanes
    row_step = min(1024, rows)
    step = min(512, count)
    skip = first // step
    scale = head_dim ** (-0.5)
    resumed = start is not None
    more = [pl.BlockSpec((rows, lanes), lambda h, j: (0, h))] if resumed else []
    return pl.pallas_call(
        functools.partial(attend_back_kernel, scale, head_dim, row_step, resumed),
        grid=(pairs, count // step),
        in_specs=[
            pl.BlockSpec((rows, lanes), lambda h, j: (0, h)),
            pl.BlockSpec((rows, lanes), lambda h, j: (0, h)),
            pl.BlockSpec((None, rows, lanes), lambda h, j: (h, 0, 0)),
            pl.BlockSpec((None, rows, lanes), lambda h, j: (h, 0, 0)),
            pl.BlockSpec((step, lanes), lambda h, j: (j + skip, h)),
            pl.BlockSpec((step, lanes), lambda h, j: (j + skip, h + pairs)),
            pl.BlockSpec((step, lanes), lambda h, j: (j + skip, 0)),
        ]
        + more,
        out_specs=[
            pl.BlockSpec((rows, lanes), lambda h, j: (0, h)),
            pl.BlockSpec((2, lanes, step), lambda h, j: (0, h, j)),
        ],
        out_shape=[
            jax.ShapeDtypeStruct((rows, width), f32),
            jax.ShapeDtypeStruct((2, width, count), bf16),
        ],
        compiler_params=pltpu.CompilerParams(vmem_limit_bytes=vmem_grant),
        cost_estimate=pl.CostEstimate(
            flops=10 * rows * count * width * 4,
            bytes_accessed=count * width * 8 + rows * width * 12,
            transcendentals=rows * count * width // head_dim,
        ),
        name="attend_back",
    )(queries, grads, stats, deltas, both, both, extra, *([start] if resumed else []))


def key_lanes(live, head_dim):
    lane = jnp.arange(lanes, dtype=jnp.int32) % head_dim
    bias = jnp.where(live, 0.0, masked_bias)[:, None]
    ones = jnp.where((lane >= 1) & (lane <= 3), 1.0, 0.0)[None, :]
    return jnp.where(lane[None, :] == 0, bias, ones).astype(bf16)


def middle_kernel(
    head_dim,
    chunk,
    mixed_ref,
    x_ref,
    cot_ref,
    live_ref,
    out_ref,
    up_ref,
    down_ref,
    vec_ref,
    up_bias_ref,
    y_ref,
    active_ref,
    hidden_ref,
    dbranch_ref,
    dupper_ref,
    dz_ref,
    dattn_ref,
    dmixed_ref,
    delta_ref,
    sums_ref,
    up_sum_ref,
    slope,
):
    width = x_ref.shape[1]
    inner = up_ref.shape[1]
    out_bias, gain_first, shift_first = (vec_ref[0:1, :], vec_ref[1:2, :], vec_ref[2:3, :])
    down_bias, gain_second, shift_second = (vec_ref[3:4, :], vec_ref[4:5, :], vec_ref[5:6, :])
    live = live_ref[...]
    mixed = mixed_ref[...]
    attn = dot(mixed, out_ref[...], 1, 0) + out_bias
    hidden, unit_first, inverse_first = norm_parts(
        x_ref[...].astype(f32) + attn, gain_first, shift_first
    )
    hidden_low = hidden.astype(bf16)
    hidden_ref[...] = hidden_low
    branch = down_bias
    for first in range(0, inner, chunk):
        part = slice(first, first + chunk)
        upper = dot(hidden_low, up_ref[:, part], 1, 0) + up_bias_ref[:, part]
        below = 0.5 + 0.5 * lax.erf(upper * (0.5**0.5))
        active = (upper * below).astype(bf16)
        bell = jnp.exp2(upper * upper * (-0.5 * log2_e)) * 0.3989422804014327
        slope[:, part] = (below + upper * bell).astype(bf16)
        active_ref[:, part] = active
        branch = branch + dot(active, down_ref[part, :], 1, 0)
    normed, unit_second, inverse_second = norm_parts(hidden + branch, gain_second, shift_second)
    result = normed * live
    y_ref[...] = result.astype(bf16)
    grad_out = cot_ref[...].astype(f32) * live
    grad_second = norm_back(grad_out * gain_second, unit_second, inverse_second)
    grad_branch = grad_second.astype(bf16)
    dbranch_ref[...] = grad_branch
    grad_hidden = grad_second
    up_sums = []
    for first in range(0, inner, chunk):
        part = slice(first, first + chunk)
        grad_active = dot(grad_branch, down_ref[part, :], 1, 1)
        grad_upper = (grad_active * slope[:, part].astype(f32)).astype(bf16)
        dupper_ref[:, part] = grad_upper
        up_sums.append(jnp.sum(grad_upper.astype(f32), axis=0, keepdims=True))
        grad_hidden = grad_hidden + dot(grad_upper, up_ref[:, part], 1, 1)
    grad_first = norm_back(grad_hidden * gain_first, unit_first, inverse_first)
    dz_ref[...] = grad_first
    grad_attn = grad_first.astype(bf16)
    dattn_ref[...] = grad_attn
    grad_mixed = dot(grad_attn, out_ref[...], 1, 1).astype(bf16)
    dmixed_ref[...] = grad_mixed
    cross = grad_mixed.astype(f32) * mixed.astype(f32)
    lane = lax.broadcasted_iota(jnp.int32, (1, lanes), 1)
    lower = lane < head_dim
    for p in range(width // lanes):
        pair = cross[:, p * lanes : (p + 1) * lanes]
        first_head = jnp.sum(jnp.where(lower, pair, 0.0), axis=1, keepdims=True)
        second_head = jnp.sum(jnp.where(lower, 0.0, pair), axis=1, keepdims=True)
        delta_ref[p] = spread_lanes(first_head, second_head, 0.0, head_dim)
    sums = [
        grad_attn.astype(f32),
        grad_hidden * unit_first,
        grad_hidden,
        grad_branch.astype(f32),
        grad_out * unit_second,
        grad_out,
        result * result,
        attn * attn * live,
        branch * branch * live,
    ]
    first_step = pl.program_id(0) == 0

    @pl.when(first_step)
    def _():
        sums_ref[...] = jnp.zeros_like(sums_ref)
        up_sum_ref[...] = jnp.zeros_like(up_sum_ref)

    for i, value in enumerate(sums):
        sums_ref[i : i + 1, :] += jnp.sum(value, axis=0, keepdims=True)
    up_sum_ref[0:1, :] += jnp.concatenate(up_sums, axis=1)


def middle(mixed, rows, cot, live, out_all, up_all, down_all, vectors, up_bias, head_dim):
    count, width = rows.shape
    inner = up_all.shape[1]
    pairs = width // lanes
    row_step = min(256, count)
    chunk = min(768, inner)

    def fixed(shape):
        return pl.BlockSpec(shape, lambda i: (0, 0), pipeline_mode=pl.Buffered(1))

    def block(columns):
        return pl.BlockSpec((row_step, columns), lambda i: (i, 0))

    return pl.pallas_call(
        functools.partial(middle_kernel, head_dim, chunk),
        grid=(count // row_step,),
        in_specs=[
            block(width),
            block(width),
            block(width),
            block(1),
            fixed((width, width)),
            fixed((width, inner)),
            fixed((inner, width)),
            fixed(vectors.shape),
            fixed(up_bias.shape),
        ],
        out_specs=[
            block(width),
            block(inner),
            block(width),
            block(width),
            block(inner),
            block(width),
            block(width),
            block(width),
            pl.BlockSpec((pairs, row_step, lanes), lambda i: (0, i, 0)),
            pl.BlockSpec((16, width), lambda i: (0, 0)),
            pl.BlockSpec((8, inner), lambda i: (0, 0)),
        ],
        out_shape=[
            jax.ShapeDtypeStruct((count, width), bf16),
            jax.ShapeDtypeStruct((count, inner), bf16),
            jax.ShapeDtypeStruct((count, width), bf16),
            jax.ShapeDtypeStruct((count, width), bf16),
            jax.ShapeDtypeStruct((count, inner), bf16),
            jax.ShapeDtypeStruct((count, width), f32),
            jax.ShapeDtypeStruct((count, width), bf16),
            jax.ShapeDtypeStruct((count, width), bf16),
            jax.ShapeDtypeStruct((pairs, count, lanes), bf16),
            jax.ShapeDtypeStruct((16, width), f32),
            jax.ShapeDtypeStruct((8, inner), f32),
        ],
        scratch_shapes=[pltpu.VMEM((row_step, inner), bf16)],
        compiler_params=pltpu.CompilerParams(vmem_limit_bytes=vmem_grant),
        cost_estimate=pl.CostEstimate(
            flops=4 * count * width * (2 * inner + width),
            bytes_accessed=4 * width * inner + count * (18 * width + 4 * inner),
            transcendentals=4 * count * inner,
        ),
        name="middle",
    )(mixed, rows, cot, live, out_all, up_all, down_all, vectors, up_bias)


def up_out_kernel(blocks, hidden_ref, dupper_ref, mixed_ref, dattn_ref, o_ref):
    s = pl.program_id(0)

    @pl.when(s < blocks)
    def _():
        o_ref[...] = dot(hidden_ref[...], dupper_ref[...], 0, 0).astype(bf16).reshape(o_ref.shape)

    @pl.when(s == blocks)
    def _():
        o_ref[...] = dot(mixed_ref[...], dattn_ref[...], 0, 0).astype(bf16).reshape(o_ref.shape)


def down_kernel(active_ref, dbranch_ref, held_ref, o_ref):
    del held_ref
    o_ref[...] = dot(active_ref[...], dbranch_ref[...], 0, 0).astype(bf16).reshape(o_ref.shape)


def middle_grads(hidden, dupper, mixed, dattn, active, dbranch, owners, ring):
    count, width = hidden.shape
    inner = dupper.shape[1]
    devices = owners * ring
    share = width // devices
    blocks = inner // width
    tall = inner // devices
    piece = blocks * share + tall + share
    shape = jax.ShapeDtypeStruct((devices, piece, width), bf16)
    params = pltpu.CompilerParams(vmem_limit_bytes=vmem_grant)
    whole = pl.BlockSpec((count, width), lambda s: (0, 0))
    held = pl.pallas_call(
        functools.partial(up_out_kernel, blocks),
        grid=(blocks + 1,),
        in_specs=[
            whole,
            pl.BlockSpec((count, width), lambda s: (0, jnp.minimum(s, blocks - 1))),
            whole,
            whole,
        ],
        out_specs=pl.BlockSpec(
            (devices, share, width),
            lambda s: (0, jnp.where(s < blocks, s, piece // share - 1), 0),
        ),
        out_shape=shape,
        compiler_params=params,
        cost_estimate=pl.CostEstimate(
            flops=2 * count * width * (inner + width),
            bytes_accessed=2 * (count + width) * (inner + 3 * width),
            transcendentals=0,
        ),
        name="up_grads",
    )(hidden, dupper, mixed, dattn)
    return pl.pallas_call(
        down_kernel,
        grid=(owners,),
        in_specs=[
            pl.BlockSpec((count, inner // owners), lambda s: (0, s)),
            whole,
            pl.BlockSpec(memory_space=pl.ANY),
        ],
        out_specs=pl.BlockSpec((ring, tall, width), lambda s: (s, blocks * share // tall, 0)),
        out_shape=shape,
        input_output_aliases={2: 0},
        compiler_params=params,
        cost_estimate=pl.CostEstimate(
            flops=2 * count * width * inner,
            bytes_accessed=2 * (count + width) * (inner + width),
            transcendentals=0,
        ),
        name="down_grads",
    )(active, dbranch, held)


def shards(
    ring,
    tokens,
    cotangent,
    lengths,
    block_order,
    qkv_weight,
    query_bias,
    value_bias,
    out_weight,
    out_bias,
    attn_gain,
    attn_shift,
    up_weight,
    up_bias,
    down_weight,
    down_bias,
    ffn_gain,
    ffn_shift,
):
    seqs, block, width = tokens.shape
    head_dim = width // HEADS
    assert seqs == 2 and ring % 4 == 0
    half = ring // 2
    here = lax.axis_index("ctx")
    side = here // half

    def pick(array, index):
        return lax.dynamic_index_in_dim(array, index, 0, keepdims=False)

    def exchange(array, bit):
        return lax.ppermute(array, "ctx", [(i, i ^ bit) for i in range(ring)])

    def to_home(kept, sent):
        other = exchange(sent, half)
        first = jnp.where(side == 0, kept, other)
        second = jnp.where(side == 0, other, kept)
        return jnp.stack([first, second])

    def gather(array):
        return lax.all_gather(array, "dp", axis=0, tiled=True)

    qkv_all = gather(qkv_weight)
    own = pick(tokens, side)
    moved = exchange(pick(tokens, 1 - side), half)
    bits = []
    bit = half // 2
    while bit:
        bits.append(bit)
        bit //= 2
    ids = jnp.stack([here, here ^ half])
    pieces = [own, moved, exchange(own, bits[0]), exchange(moved, bits[0])]
    ids = jnp.concatenate([ids, ids ^ bits[0]])
    stream = jnp.concatenate(pieces, axis=0)
    for bit in bits[1:]:
        stream = jnp.concatenate([stream, exchange(stream, bit)], axis=0)
        ids = jnp.concatenate([ids, ids ^ bit])
    rows = stream[: 2 * block]
    count_rows = 2 * block

    order = pick(block_order, side)
    length = pick(lengths, side)
    table = jnp.arange(ring, dtype=jnp.int32)
    place_of = jnp.sum(jnp.where(ids[:, None] == table[None, :], order[None, :], 0), axis=1)
    places = place_of[:, None] * block + jnp.arange(block, dtype=jnp.int32)[None, :]
    live_keys = (places < length).reshape(-1)
    live_rows = live_keys[:count_rows, None].astype(f32)
    extra = key_lanes(live_keys, head_dim)

    row = lax.axis_index("dp")
    owners = lax.axis_size("dp")
    singles = [
        query_bias,
        value_bias,
        out_bias,
        attn_gain,
        attn_shift,
        down_bias,
        ffn_gain,
        ffn_shift,
    ]
    share = query_bias.shape[0]
    packed = jnp.concatenate(singles + [up_bias])[None, :]
    held = [packed]
    for k in range(1, owners):
        held.append(lax.ppermute(packed, "dp", [(i, i ^ k) for i in range(owners)]))
    vectors = []
    for d in range(owners):
        found = held[0]
        for k in range(1, owners):
            found = jnp.where((row ^ d) == k, held[k], found)
        vectors.append(found)
    vectors = jnp.concatenate(vectors, axis=0).astype(f32)
    bias = [vectors[:, i * share : (i + 1) * share].reshape(1, width) for i in range(8)]
    up_bias_all = vectors[:, 8 * share :].reshape(1, -1)
    queries = (
        jnp.dot(rows, qkv_all[:, :width], preferred_element_type=f32) + bias[0]
    ).astype(bf16)
    kv_bias = jnp.concatenate([jnp.zeros_like(bias[1]), bias[1]], axis=1)
    both = (jnp.dot(stream, qkv_all[:, width:], preferred_element_type=f32) + kv_bias).astype(bf16)
    out_all = gather(out_weight)
    up_all = gather(up_weight)
    down_all = gather(down_weight)
    held, _ = lax.optimization_barrier((cotangent, stream))
    cot = jnp.concatenate([pick(held, side), exchange(pick(held, 1 - side), half)], axis=0)

    mixed, stats = attend(queries, both, extra, head_dim)
    (
        result,
        active,
        hidden,
        grad_branch,
        grad_upper,
        grad_first,
        grad_attn,
        grad_mixed,
        deltas,
        sums,
        up_sum,
    ) = middle(
        mixed,
        rows,
        cot,
        live_rows,
        out_all,
        up_all,
        down_all,
        jnp.concatenate(bias[2:] + [jnp.zeros((2, width), f32)], axis=0),
        up_bias_all,
        head_dim,
    )
    output = to_home(result[:block], result[block:])

    def scatter(grad):
        return lax.psum_scatter(grad, ("dp", "ctx"), scatter_dimension=0, tiled=True)

    def spread(part):
        return lax.all_gather(part, "ctx", axis=0, tiled=True)

    devices = owners * ring
    inner = up_weight.shape[1]
    laid = width % (8 * devices) == 0 and inner % width == 0
    if laid:
        piece = middle_grads(hidden, grad_upper, mixed, grad_attn, active, grad_branch, owners, ring)
        pieces = spread(scatter(piece)).astype(f32)
        each, tall = (width // devices, inner // devices)
        blocks = inner // width
        cut = blocks * each
        grad_up_weight = jnp.concatenate(
            [pieces[:, i * each : (i + 1) * each, :].reshape(share, width) for i in range(blocks)],
            axis=1,
        )
        grad_down_weight = pieces[:, cut : cut + tall, :].reshape(-1, width)
        grad_out_weight = pieces[:, cut + tall :, :].reshape(share, width)
    else:
        grad_up_weight = spread(scatter(dot(hidden, grad_upper, 0, 0).astype(bf16))).astype(f32)
        grad_down_weight = spread(scatter(dot(active, grad_branch, 0, 0).astype(bf16))).astype(f32)
        grad_out_weight = spread(scatter(dot(mixed, grad_attn, 0, 0).astype(bf16))).astype(f32)

    kv_weight = qkv_all[:, width:]
    total_keys = stream.shape[0]
    grad_queries = None
    grad_kv_weight = None
    grad_value_bias = None
    arrived = []
    last = total_keys
    for bit in list(reversed(bits)) + [0]:
        first = last // 2 if bit else 0
        grad_queries, grad_both = attend_back(
            queries, grad_mixed, stats, deltas, both, extra, head_dim, first, last - first, grad_queries
        )
        kv_grads = grad_both.reshape(2 * width, last - first)
        part = dot(stream[first:last], kv_grads, 0, 1)
        grad_kv_weight = part if grad_kv_weight is None else grad_kv_weight + part
        part = jnp.sum(grad_both[1], axis=1, dtype=f32)
        grad_value_bias = part if grad_value_bias is None else grad_value_bias + part
        grad_stream = dot(kv_grads, kv_weight, 0, 1)
        for other in arrived:
            grad_stream = grad_stream + other[first:last].astype(f32)
        if bit:
            arrived.append(exchange(grad_stream.astype(bf16), bit))
        last = first
    grad_query_low = grad_queries.astype(bf16)
    grad_rows = grad_first + dot(grad_query_low, qkv_all[:, :width], 1, 1) + grad_stream
    grad_rows_low = grad_rows.astype(bf16)
    grad_tokens = to_home(grad_rows_low[:block], grad_rows_low[block:])

    grad_query_bias = jnp.sum(grad_query_low, axis=0, dtype=f32)
    grad_qkv_weight = jnp.concatenate([dot(rows, grad_query_low, 0, 0), grad_kv_weight], axis=1)
    qkv_part = scatter(grad_qkv_weight.astype(bf16))

    small = [grad_query_bias, grad_value_bias] + [sums[i] for i in range(6)] + [up_sum[0]]
    squares = jnp.sum(sums[6:9], axis=1)
    square_sums = jnp.where(jnp.arange(2)[:, None] == side, squares[None, :], 0.0)
    slots = jnp.where(
        jnp.arange(owners)[:, None] == row, square_sums.reshape(1, -1), 0.0
    ).reshape(-1)
    summed = lax.psum(jnp.concatenate(small + [slots]), ("dp", "ctx"))
    totals = []
    start = 0
    for v in small:
        size = v.shape[0] // owners
        totals.append(lax.dynamic_slice_in_dim(summed, start + row * size, size))
        start += v.shape[0]
    seq_squares = lax.dynamic_slice_in_dim(summed, start + row * 6, 6).reshape(2, 3)
    branch_rms = jnp.sqrt(seq_squares / (lengths.astype(f32)[:, None] * width) + rms_eps)
    return (
        output,
        grad_tokens,
        spread(qkv_part).astype(f32),
        totals[0],
        totals[1],
        grad_out_weight,
        totals[2],
        totals[3],
        totals[4],
        grad_up_weight,
        totals[8],
        grad_down_weight,
        totals[5],
        totals[6],
        totals[7],
        branch_rms,
    )


def solution(mesh):
    in_specs = (
        P("dp", "ctx", None),
        P("dp", "ctx", None),
        P("dp"),
        P("dp", None),
        P("dp", None),
        P("dp"),
        P("dp"),
        P("dp", None),
        P("dp"),
        P("dp"),
        P("dp"),
        P("dp", None),
        P("dp"),
        P("dp", None),
        P("dp"),
        P("dp"),
        P("dp"),
    )
    out_specs = (
        P("dp", "ctx", None),
        P("dp", "ctx", None),
        P("dp", None),
        P("dp"),
        P("dp"),
        P("dp", None),
        P("dp"),
        P("dp"),
        P("dp"),
        P("dp", None),
        P("dp"),
        P("dp", None),
        P("dp"),
        P("dp"),
        P("dp"),
        P("dp", None),
    )
    return jax.shard_map(
        functools.partial(shards, mesh.shape["ctx"]),
        mesh=mesh,
        in_specs=in_specs,
        out_specs=out_specs,
        check_vma=False,
    )
```

```python
import functools

import jax
import jax.numpy as jnp
from jax import lax
from jax.experimental import pallas as pl
from jax.experimental.pallas import tpu as pltpu
from jax.sharding import PartitionSpec as P

HEADS = 12

norm_eps = 1e-12
rms_eps = 1e-06
masked_bias = -1e30
log2_e = 1.4426950408889634
lanes = 128
vmem_grant = 56 << 20
f32 = jnp.float32
bf16 = jnp.bfloat16


def norm_parts(total, gain, shift):
    mean = jnp.mean(total, axis=-1, keepdims=True)
    centred = total - mean
    inverse = lax.rsqrt(jnp.mean(centred * centred, axis=-1, keepdims=True) + norm_eps)
    unit = centred * inverse
    return (unit * gain + shift, unit, inverse)


def norm_back(grad_unit, unit, inverse):
    mean_grad = jnp.mean(grad_unit, axis=-1, keepdims=True)
    mean_cross = jnp.mean(grad_unit * unit, axis=-1, keepdims=True)
    return inverse * (grad_unit - mean_grad - unit * mean_cross)


def dot(left, right, left_dim, right_dim):
    return lax.dot_general(
        left, right, (((left_dim,), (right_dim,)), ((), ())), preferred_element_type=f32
    )


def head_lanes(head, head_dim):
    lane = lax.broadcasted_iota(jnp.int32, (1, lanes), 1)
    return (lane // head_dim) == head


def spread_lanes(first_head, second_head, unit, head_dim):
    rows = first_head.shape[0]
    lane = lax.broadcasted_iota(jnp.int32, (rows, lanes), 1)
    place = lane % head_dim
    value = -jnp.where(lane < head_dim, second_head, first_head)
    high = value.astype(bf16).astype(f32)
    rest = value - high
    mid = rest.astype(bf16).astype(f32)
    low = rest - mid
    out = jnp.where(place == 1, high, jnp.where(place == 2, mid, jnp.where(place == 3, low, 0.0)))
    return jnp.where(place == 0, unit, out).astype(bf16)


def attend_kernel(scale, head_dim, step, q_ref, k_ref, v_ref, extra_ref, o_ref, stat_ref, kb, vb):
    keys = k_ref.shape[0]

    @pl.when(pl.program_id(1) == 0)
    def _():
        for h in range(2):
            kb[h] = jnp.where(head_lanes(h, head_dim), k_ref[...], extra_ref[...])
            vb[h] = jnp.where(head_lanes(h, head_dim), v_ref[...], extra_ref[...])

    factor = scale * log2_e
    queries = q_ref[...]
    lane = lax.broadcasted_iota(jnp.int32, (1, lanes), 1)
    bias_lane = jnp.where(lane % head_dim == 0, 1.0, 0.0).astype(bf16)
    outs, logs = ([], [])
    for h in range(2):
        own = jnp.where(head_lanes(h, head_dim), queries, bias_lane)
        best, acc = (None, None)
        for first in range(0, keys, step):
            scores = dot(own, kb[h, first : first + step, :], 1, 1)
            high = jnp.max(scores, axis=1, keepdims=True)
            new_best = high if best is None else jnp.maximum(best, high)
            weights = jnp.exp2((scores - new_best) * factor).astype(bf16)
            part = dot(weights, vb[h, first : first + step, :], 1, 0)
            acc = part if best is None else acc * jnp.exp2((best - new_best) * factor) + part
            best = new_best
        free = (1 - h) * head_dim + 1
        total = acc[:, free : free + 1]
        outs.append(acc / total)
        logs.append(best + jnp.log2(total) * (1.0 / factor))
    o_ref[...] = jnp.where(head_lanes(0, head_dim), outs[0], outs[1]).astype(bf16)
    stat_ref[...] = spread_lanes(logs[0], logs[1], 1.0, head_dim)


def attend(queries, both, extra, head_dim):
    rows, width = queries.shape
    keys = both.shape[0]
    pairs = width // lanes
    row_step = min(512, rows)
    step = min(2048, keys)
    scale = head_dim ** (-0.5)
    return pl.pallas_call(
        functools.partial(attend_kernel, scale, head_dim, step),
        grid=(pairs, rows // row_step),
        in_specs=[
            pl.BlockSpec((row_step, lanes), lambda h, i: (i, h)),
            pl.BlockSpec((keys, lanes), lambda h, i: (0, h)),
            pl.BlockSpec((keys, lanes), lambda h, i: (0, h + pairs)),
            pl.BlockSpec((keys, lanes), lambda h, i: (0, 0)),
        ],
        out_specs=[
            pl.BlockSpec((row_step, lanes), lambda h, i: (i, h)),
            pl.BlockSpec((None, row_step, lanes), lambda h, i: (h, i, 0)),
        ],
        out_shape=[
            jax.ShapeDtypeStruct((rows, width), bf16),
            jax.ShapeDtypeStruct((pairs, rows, lanes), bf16),
        ],
        scratch_shapes=[pltpu.VMEM((2, keys, lanes), bf16), pltpu.VMEM((2, keys, lanes), bf16)],
        compiler_params=pltpu.CompilerParams(vmem_limit_bytes=vmem_grant),
        cost_estimate=pl.CostEstimate(
            flops=4 * rows * keys * width * 4,
            bytes_accessed=keys * width * 4 + rows * width * 6,
            transcendentals=rows * keys * width // head_dim,
        ),
        name="attend",
    )(queries, both, both, extra)


def attend_back_kernel(scale, head_dim, row_step, resumed, *refs):
    q_ref, da_ref, qx_ref, dax_ref, k_ref, v_ref, extra_ref = refs[:7]
    start_ref = refs[7] if resumed else None
    dq_ref, dkv_ref = refs[-2:]
    j = pl.program_id(1)
    rows = q_ref.shape[0]
    factor = scale * log2_e
    keys, values, extra = (k_ref[...], v_ref[...], extra_ref[...])
    dk, dv = (None, None)
    for first in range(0, rows, row_step):
        part = slice(first, first + row_step)
        queries, grads = (q_ref[part, :], da_ref[part, :])
        queries_extra, grads_extra = (qx_ref[part, :], dax_ref[part, :])
        dq = None
        for h in range(2):
            sel = head_lanes(h, head_dim)
            scores = dot(
                jnp.where(sel, queries, queries_extra), jnp.where(sel, keys, extra), 1, 1
            )
            weights = jnp.exp2(scores * factor)
            grad_weights = dot(
                jnp.where(sel, grads, grads_extra), jnp.where(sel, values, extra), 1, 1
            )
            grad_scores = (weights * grad_weights).astype(bf16)
            none = jnp.zeros_like(queries)
            part_dv = dot(jnp.where(sel, grads, none), weights.astype(bf16), 0, 0)
            part_dk = dot(jnp.where(sel, queries, none), grad_scores, 0, 0)
            part_dq = dot(grad_scores, jnp.where(sel, keys, jnp.zeros_like(keys)), 1, 0)
            dv = part_dv if dv is None else dv + part_dv
            dk = part_dk if dk is None else dk + part_dk
            dq = part_dq if dq is None else dq + part_dq
        dq = dq * scale

        @pl.when(j == 0)
        def _():
            dq_ref[part, :] = dq + start_ref[part, :] if resumed else dq

        @pl.when(j > 0)
        def _():
            dq_ref[part, :] += dq

    dkv_ref[0] = (dk * scale).astype(bf16)
    dkv_ref[1] = dv.astype(bf16)


def attend_back(queries, grads, stats, deltas, both, extra, head_dim, first, count, start):
    rows, width = queries.shape
    pairs = width // lanes
    row_step = min(1024, rows)
    step = min(512, count)
    skip = first // step
    scale = head_dim ** (-0.5)
    resumed = start is not None
    more = [pl.BlockSpec((rows, lanes), lambda h, j: (0, h))] if resumed else []
    return pl.pallas_call(
        functools.partial(attend_back_kernel, scale, head_dim, row_step, resumed),
        grid=(pairs, count // step),
        in_specs=[
            pl.BlockSpec((rows, lanes), lambda h, j: (0, h)),
            pl.BlockSpec((rows, lanes), lambda h, j: (0, h)),
            pl.BlockSpec((None, rows, lanes), lambda h, j: (h, 0, 0)),
            pl.BlockSpec((None, rows, lanes), lambda h, j: (h, 0, 0)),
            pl.BlockSpec((step, lanes), lambda h, j: (j + skip, h)),
            pl.BlockSpec((step, lanes), lambda h, j: (j + skip, h + pairs)),
            pl.BlockSpec((step, lanes), lambda h, j: (j + skip, 0)),
        ]
        + more,
        out_specs=[
            pl.BlockSpec((rows, lanes), lambda h, j: (0, h)),
            pl.BlockSpec((2, lanes, step), lambda h, j: (0, h, j)),
        ],
        out_shape=[
            jax.ShapeDtypeStruct((rows, width), f32),
            jax.ShapeDtypeStruct((2, width, count), bf16),
        ],
        compiler_params=pltpu.CompilerParams(vmem_limit_bytes=vmem_grant),
        cost_estimate=pl.CostEstimate(
            flops=10 * rows * count * width * 4,
            bytes_accessed=count * width * 8 + rows * width * 12,
            transcendentals=rows * count * width // head_dim,
        ),
        name="attend_back",
    )(queries, grads, stats, deltas, both, both, extra, *([start] if resumed else []))


def key_lanes(live, head_dim):
    lane = jnp.arange(lanes, dtype=jnp.int32) % head_dim
    bias = jnp.where(live, 0.0, masked_bias)[:, None]
    ones = jnp.where((lane >= 1) & (lane <= 3), 1.0, 0.0)[None, :]
    return jnp.where(lane[None, :] == 0, bias, ones).astype(bf16)


def middle_kernel(
    head_dim,
    chunk,
    mixed_ref,
    x_ref,
    cot_ref,
    live_ref,
    out_ref,
    up_ref,
    down_ref,
    vec_ref,
    up_bias_ref,
    y_ref,
    active_ref,
    hidden_ref,
    dbranch_ref,
    dupper_ref,
    dz_ref,
    dattn_ref,
    dmixed_ref,
    delta_ref,
    sums_ref,
    up_sum_ref,
    slope,
):
    width = x_ref.shape[1]
    inner = up_ref.shape[1]
    out_bias, gain_first, shift_first = (vec_ref[0:1, :], vec_ref[1:2, :], vec_ref[2:3, :])
    down_bias, gain_second, shift_second = (vec_ref[3:4, :], vec_ref[4:5, :], vec_ref[5:6, :])
    live = live_ref[...]
    mixed = mixed_ref[...]
    attn = dot(mixed, out_ref[...], 1, 0) + out_bias
    hidden, unit_first, inverse_first = norm_parts(
        x_ref[...].astype(f32) + attn, gain_first, shift_first
    )
    hidden_low = hidden.astype(bf16)
    hidden_ref[...] = hidden_low
    branch = down_bias
    for first in range(0, inner, chunk):
        part = slice(first, first + chunk)
        upper = dot(hidden_low, up_ref[:, part], 1, 0) + up_bias_ref[:, part]
        below = 0.5 + 0.5 * lax.erf(upper * (0.5**0.5))
        active = (upper * below).astype(bf16)
        bell = jnp.exp2(upper * upper * (-0.5 * log2_e)) * 0.3989422804014327
        slope[:, part] = (below + upper * bell).astype(bf16)
        active_ref[:, part] = active
        branch = branch + dot(active, down_ref[part, :], 1, 0)
    normed, unit_second, inverse_second = norm_parts(hidden + branch, gain_second, shift_second)
    result = normed * live
    y_ref[...] = result.astype(bf16)
    grad_out = cot_ref[...].astype(f32) * live
    grad_second = norm_back(grad_out * gain_second, unit_second, inverse_second)
    grad_branch = grad_second.astype(bf16)
    dbranch_ref[...] = grad_branch
    grad_hidden = grad_second
    up_sums = []
    for first in range(0, inner, chunk):
        part = slice(first, first + chunk)
        grad_active = dot(grad_branch, down_ref[part, :], 1, 1)
        grad_upper = (grad_active * slope[:, part].astype(f32)).astype(bf16)
        dupper_ref[:, part] = grad_upper
        up_sums.append(jnp.sum(grad_upper.astype(f32), axis=0, keepdims=True))
        grad_hidden = grad_hidden + dot(grad_upper, up_ref[:, part], 1, 1)
    grad_first = norm_back(grad_hidden * gain_first, unit_first, inverse_first)
    dz_ref[...] = grad_first
    grad_attn = grad_first.astype(bf16)
    dattn_ref[...] = grad_attn
    grad_mixed = dot(grad_attn, out_ref[...], 1, 1).astype(bf16)
    dmixed_ref[...] = grad_mixed
    cross = grad_mixed.astype(f32) * mixed.astype(f32)
    lane = lax.broadcasted_iota(jnp.int32, (1, lanes), 1)
    lower = lane < head_dim
    for p in range(width // lanes):
        pair = cross[:, p * lanes : (p + 1) * lanes]
        first_head = jnp.sum(jnp.where(lower, pair, 0.0), axis=1, keepdims=True)
        second_head = jnp.sum(jnp.where(lower, 0.0, pair), axis=1, keepdims=True)
        delta_ref[p] = spread_lanes(first_head, second_head, 0.0, head_dim)
    sums = [
        grad_attn.astype(f32),
        grad_hidden * unit_first,
        grad_hidden,
        grad_branch.astype(f32),
        grad_out * unit_second,
        grad_out,
        result * result,
        attn * attn * live,
        branch * branch * live,
    ]
    first_step = pl.program_id(0) == 0

    @pl.when(first_step)
    def _():
        sums_ref[...] = jnp.zeros_like(sums_ref)
        up_sum_ref[...] = jnp.zeros_like(up_sum_ref)

    for i, value in enumerate(sums):
        sums_ref[i : i + 1, :] += jnp.sum(value, axis=0, keepdims=True)
    up_sum_ref[0:1, :] += jnp.concatenate(up_sums, axis=1)


def middle(mixed, rows, cot, live, out_all, up_all, down_all, vectors, up_bias, head_dim):
    count, width = rows.shape
    inner = up_all.shape[1]
    pairs = width // lanes
    row_step = min(256, count)
    chunk = min(768, inner)

    def fixed(shape):
        return pl.BlockSpec(shape, lambda i: (0, 0), pipeline_mode=pl.Buffered(1))

    def block(columns):
        return pl.BlockSpec((row_step, columns), lambda i: (i, 0))

    return pl.pallas_call(
        functools.partial(middle_kernel, head_dim, chunk),
        grid=(count // row_step,),
        in_specs=[
            block(width),
            block(width),
            block(width),
            block(1),
            fixed((width, width)),
            fixed((width, inner)),
            fixed((inner, width)),
            fixed(vectors.shape),
            fixed(up_bias.shape),
        ],
        out_specs=[
            block(width),
            block(inner),
            block(width),
            block(width),
            block(inner),
            block(width),
            block(width),
            block(width),
            pl.BlockSpec((pairs, row_step, lanes), lambda i: (0, i, 0)),
            pl.BlockSpec((16, width), lambda i: (0, 0)),
            pl.BlockSpec((8, inner), lambda i: (0, 0)),
        ],
        out_shape=[
            jax.ShapeDtypeStruct((count, width), bf16),
            jax.ShapeDtypeStruct((count, inner), bf16),
            jax.ShapeDtypeStruct((count, width), bf16),
            jax.ShapeDtypeStruct((count, width), bf16),
            jax.ShapeDtypeStruct((count, inner), bf16),
            jax.ShapeDtypeStruct((count, width), f32),
            jax.ShapeDtypeStruct((count, width), bf16),
            jax.ShapeDtypeStruct((count, width), bf16),
            jax.ShapeDtypeStruct((pairs, count, lanes), bf16),
            jax.ShapeDtypeStruct((16, width), f32),
            jax.ShapeDtypeStruct((8, inner), f32),
        ],
        scratch_shapes=[pltpu.VMEM((row_step, inner), bf16)],
        compiler_params=pltpu.CompilerParams(vmem_limit_bytes=vmem_grant),
        cost_estimate=pl.CostEstimate(
            flops=4 * count * width * (2 * inner + width),
            bytes_accessed=4 * width * inner + count * (18 * width + 4 * inner),
            transcendentals=4 * count * inner,
        ),
        name="middle",
    )(mixed, rows, cot, live, out_all, up_all, down_all, vectors, up_bias)


def up_out_kernel(blocks, hidden_ref, dupper_ref, mixed_ref, dattn_ref, o_ref):
    s = pl.program_id(0)

    @pl.when(s < blocks)
    def _():
        o_ref[...] = dot(hidden_ref[...], dupper_ref[...], 0, 0).astype(bf16).reshape(o_ref.shape)

    @pl.when(s == blocks)
    def _():
        o_ref[...] = dot(mixed_ref[...], dattn_ref[...], 0, 0).astype(bf16).reshape(o_ref.shape)


def down_kernel(active_ref, dbranch_ref, held_ref, o_ref):
    del held_ref
    o_ref[...] = dot(active_ref[...], dbranch_ref[...], 0, 0).astype(bf16).reshape(o_ref.shape)


def middle_grads(hidden, dupper, mixed, dattn, active, dbranch, owners, ring):
    count, width = hidden.shape
    inner = dupper.shape[1]
    devices = owners * ring
    share = width // devices
    blocks = inner // width
    tall = inner // devices
    piece = blocks * share + tall + share
    shape = jax.ShapeDtypeStruct((devices, piece, width), bf16)
    params = pltpu.CompilerParams(vmem_limit_bytes=vmem_grant)
    whole = pl.BlockSpec((count, width), lambda s: (0, 0))
    held = pl.pallas_call(
        functools.partial(up_out_kernel, blocks),
        grid=(blocks + 1,),
        in_specs=[
            whole,
            pl.BlockSpec((count, width), lambda s: (0, jnp.minimum(s, blocks - 1))),
            whole,
            whole,
        ],
        out_specs=pl.BlockSpec(
            (devices, share, width),
            lambda s: (0, jnp.where(s < blocks, s, piece // share - 1), 0),
        ),
        out_shape=shape,
        compiler_params=params,
        cost_estimate=pl.CostEstimate(
            flops=2 * count * width * (inner + width),
            bytes_accessed=2 * (count + width) * (inner + 3 * width),
            transcendentals=0,
        ),
        name="up_grads",
    )(hidden, dupper, mixed, dattn)
    return pl.pallas_call(
        down_kernel,
        grid=(owners,),
        in_specs=[
            pl.BlockSpec((count, inner // owners), lambda s: (0, s)),
            whole,
            pl.BlockSpec(memory_space=pl.ANY),
        ],
        out_specs=pl.BlockSpec((ring, tall, width), lambda s: (s, blocks * share // tall, 0)),
        out_shape=shape,
        input_output_aliases={2: 0},
        compiler_params=params,
        cost_estimate=pl.CostEstimate(
            flops=2 * count * width * inner,
            bytes_accessed=2 * (count + width) * (inner + width),
            transcendentals=0,
        ),
        name="down_grads",
    )(active, dbranch, held)


def closing_kernel(
    owners, ring, widths, dq_ref, x_ref, *refs
):
    shares = refs[: len(widths)]
    small_ref, home_ref, out_ref, small_out_ref, home_out_ref = refs[len(widths) : len(widths) + 5]
    (
        xs,
        dq,
        dkv,
        whole,
        parts,
        in_core,
        by_owner,
        in_owner,
        by_piece,
        in_piece,
        done,
        in_done,
        small,
        small_core,
        small_owner,
        small_piece,
        load_sem,
        send_sem,
        recv_sem,
    ) = refs[len(widths) + 5 :]
    row, here = (lax.axis_index("dp"), lax.axis_index("ctx"))
    core, depth = (lax.rem(here, 2), here // 2)
    deep = ring // 2
    count = dq.shape[0]
    loads = [
        pltpu.make_async_copy(dq_ref, dq, load_sem.at[0]),
        pltpu.make_async_copy(x_ref, xs, load_sem.at[1]),
    ]
    first = xs.shape[0]
    for i, width in enumerate(widths):
        first -= width
        loads.append(
            pltpu.make_async_copy(
                shares[i], dkv.at[:, :, pl.ds(first, width)], load_sem.at[2 + i]
            )
        )
    for load in loads:
        load.start()

    mate = (row, here ^ 1)
    owner_peers = [(row ^ k, here) for k in range(1, owners)]
    depth_peers = [(row, here ^ (2 * k)) for k in range(1, deep)]
    barrier = pltpu.get_barrier_semaphore()
    peers = [mate] + owner_peers + depth_peers
    for peer in peers:
        pl.semaphore_signal(barrier, inc=1, device_id=peer, device_id_type=pl.DeviceIdType.MESH)

    sent = []

    def send(source, target, peer, m, slot):
        copy = pltpu.make_async_remote_copy(
            src_ref=source,
            dst_ref=target,
            send_sem=send_sem.at[m, slot],
            recv_sem=recv_sem.at[m, slot],
            device_id=peer,
            device_id_type=pl.DeviceIdType.MESH,
        )
        copy.start()
        sent.append(copy)
        return copy

    at_owner = 1
    at_piece = owners
    at_done = at_piece + deep - 1
    at_back = at_done + deep - 1
    tile = 256

    def to_core(m):
        def one(t, carry):
            columns = pl.ds(pl.multiple_of(t * tile, tile), tile)
            if m == 0:
                whole[columns, :] = dot(xs[0:count, columns], dq[...].astype(bf16), 0, 0)
            else:
                whole[columns, :] = dot(xs[:, columns], dkv[m - 1], 0, 1)
            return carry

        lax.fori_loop(0, whole.shape[0] // tile, one, 0)
        parts[m] = whole[...].reshape(parts.shape[1:]).astype(bf16)
        return [send(parts.at[m, :, 1 - core], in_core.at[m], mate, m, 0)]

    def to_owner(m):
        mine = parts[m, :, core].astype(f32)
        by_owner[m] = (mine + in_core[m].astype(f32)).astype(bf16)
        return [
            send(by_owner.at[m, row ^ k], in_owner.at[m, k - 1], owner_peers[k - 1], m, at_owner + k - 1)
            for k in range(1, owners)
        ]

    def to_piece(m):
        total = by_owner[m, row].astype(f32)
        for k in range(1, owners):
            total = total + in_owner[m, k - 1].astype(f32)
        by_piece[m] = total.reshape(by_piece.shape[1:]).astype(bf16)
        return [
            send(
                by_piece.at[m, depth ^ k],
                in_piece.at[m, k - 1],
                depth_peers[k - 1],
                m,
                at_piece + k - 1,
            )
            for k in range(1, deep)
        ]

    def to_done(m):
        total = by_piece[m, depth].astype(f32)
        for k in range(1, deep):
            total = total + in_piece[m, k - 1].astype(f32)
        done[m, depth] = total.astype(bf16)
        return [
            send(done.at[m, depth], done.at[m, depth], depth_peers[k - 1], m, at_done + k - 1)
            for k in range(1, deep)
        ]

    def to_back(m):
        return [send(done.at[m], in_done.at[m], mate, m, at_back)]

    def finish(m):
        size = out_ref.shape[1]
        columns = slice(m * whole.shape[1], (m + 1) * whole.shape[1])
        out_ref[core, :, columns] = done[m].astype(f32).reshape(size, whole.shape[1])
        out_ref[1 - core, :, columns] = in_done[m].astype(f32).reshape(size, whole.shape[1])
        return []

    stages = [to_core, to_owner, to_piece, to_done, to_back, finish]
    waiting = [[], [], []]
    loads[0].wait()
    loads[1].wait()
    small[...] = small_ref[...]
    small[0:1, :] = jnp.sum(dq[...].astype(bf16).astype(f32), axis=0, keepdims=True)
    for load in loads[2:]:
        load.wait()
    ones = jnp.ones((8, dkv.shape[2]), bf16)
    small[1:2, :] = dot(ones, dkv[1], 1, 1)[0:1, :]
    pl.semaphore_wait(barrier, len(peers))
    home = send(home_ref, home_out_ref, (row, here ^ (ring // 2)), 3, at_back)
    small_waits = [send(small, small_core, mate, 3, 0)]
    for step in range(len(stages) + 2):
        for m in range(3):
            stage = step - m
            if 0 <= stage < len(stages):
                for copy in waiting[m]:
                    copy.wait_recv()
                waiting[m] = stages[stage](m)
        if step == 1:
            small_waits[0].wait_recv()
            small_owner[0] = small[...] + small_core[...]
            small_waits = [
                send(small_owner.at[0], small_owner.at[k], owner_peers[k - 1], 3, k)
                for k in range(1, owners)
            ]
        if step == 3:
            total = small_owner[0]
            for k in range(1, owners):
                small_waits[k - 1].wait_recv()
                total = total + small_owner[k]
            small_piece[0] = total
            small_waits = [
                send(small_piece.at[0], small_piece.at[k], depth_peers[k - 1], 3, at_piece + k - 1)
                for k in range(1, deep)
            ]
        if step == 5:
            total = small_piece[0]
            for k in range(1, deep):
                small_waits[k - 1].wait_recv()
                total = total + small_piece[k]
            small_out_ref[...] = total
    home.wait_recv()
    for copy in sent:
        copy.wait_send()


def closing(dq, stream, shares, small, home, owners, ring):
    count, width = dq.shape
    keys = stream.shape[0]
    widths = tuple(v.shape[2] for v in shares)
    deep = ring // 2
    half = width // owners // 2
    piece = half // deep
    slots = 1 + (owners - 1) + 2 * (deep - 1) + 1
    any_space = pl.BlockSpec(memory_space=pl.ANY)
    in_vmem = pl.BlockSpec(memory_space=pltpu.VMEM)
    return pl.pallas_call(
        functools.partial(closing_kernel, owners, ring, widths),
        in_specs=[any_space] * (2 + len(shares)) + [in_vmem, any_space],
        out_specs=[in_vmem, in_vmem, any_space],
        out_shape=[
            jax.ShapeDtypeStruct((2, half, 3 * width), f32),
            jax.ShapeDtypeStruct(small.shape, f32),
            jax.ShapeDtypeStruct(home.shape, home.dtype),
        ],
        scratch_shapes=[
            pltpu.VMEM((keys, width), bf16),
            pltpu.VMEM((count, width), f32),
            pltpu.VMEM((2, width, keys), bf16),
            pltpu.VMEM((width, width), f32),
            pltpu.VMEM((3, owners, 2, half, width), bf16),
            pltpu.VMEM((3, owners, half, width), bf16),
            pltpu.VMEM((3, owners, half, width), bf16),
            pltpu.VMEM((3, owners - 1, half, width), bf16),
            pltpu.VMEM((3, deep, piece, width), bf16),
            pltpu.VMEM((3, deep - 1, piece, width), bf16),
            pltpu.VMEM((3, deep, piece, width), bf16),
            pltpu.VMEM((3, deep, piece, width), bf16),
            pltpu.VMEM(small.shape, f32),
            pltpu.VMEM(small.shape, f32),
            pltpu.VMEM((owners,) + small.shape, f32),
            pltpu.VMEM((deep,) + small.shape, f32),
            pltpu.SemaphoreType.DMA((2 + len(shares),)),
            pltpu.SemaphoreType.DMA((4, slots)),
            pltpu.SemaphoreType.DMA((4, slots)),
        ],
        compiler_params=pltpu.CompilerParams(
            vmem_limit_bytes=vmem_grant, collective_id=0, has_side_effects=True
        ),
        cost_estimate=pl.CostEstimate(
            flops=20 * keys * width * width, bytes_accessed=100 << 20, transcendentals=0
        ),
        name="closing",
    )(dq, stream, *shares, small, home)


def shards(
    ring,
    tokens,
    cotangent,
    lengths,
    block_order,
    qkv_weight,
    query_bias,
    value_bias,
    out_weight,
    out_bias,
    attn_gain,
    attn_shift,
    up_weight,
    up_bias,
    down_weight,
    down_bias,
    ffn_gain,
    ffn_shift,
):
    seqs, block, width = tokens.shape
    head_dim = width // HEADS
    assert seqs == 2 and ring % 4 == 0
    half = ring // 2
    here = lax.axis_index("ctx")
    side = here // half

    def pick(array, index):
        return lax.dynamic_index_in_dim(array, index, 0, keepdims=False)

    def exchange(array, bit):
        return lax.ppermute(array, "ctx", [(i, i ^ bit) for i in range(ring)])

    def arrange(kept, other):
        first = jnp.where(side == 0, kept, other)
        second = jnp.where(side == 0, other, kept)
        return jnp.stack([first, second])

    def gather(array):
        return lax.all_gather(array, "dp", axis=0, tiled=True)

    qkv_all = gather(qkv_weight)
    own = pick(tokens, side)
    moved = exchange(pick(tokens, 1 - side), half)
    bits = []
    bit = half // 2
    while bit:
        bits.append(bit)
        bit //= 2
    ids = jnp.stack([here, here ^ half])
    pieces = [own, moved, exchange(own, bits[0]), exchange(moved, bits[0])]
    ids = jnp.concatenate([ids, ids ^ bits[0]])
    stream = jnp.concatenate(pieces, axis=0)
    for bit in bits[1:]:
        stream = jnp.concatenate([stream, exchange(stream, bit)], axis=0)
        ids = jnp.concatenate([ids, ids ^ bit])
    rows = stream[: 2 * block]
    count_rows = 2 * block

    order = pick(block_order, side)
    length = pick(lengths, side)
    table = jnp.arange(ring, dtype=jnp.int32)
    place_of = jnp.sum(jnp.where(ids[:, None] == table[None, :], order[None, :], 0), axis=1)
    places = place_of[:, None] * block + jnp.arange(block, dtype=jnp.int32)[None, :]
    live_keys = (places < length).reshape(-1)
    live_rows = live_keys[:count_rows, None].astype(f32)
    extra = key_lanes(live_keys, head_dim)

    row = lax.axis_index("dp")
    owners = lax.axis_size("dp")
    singles = [
        query_bias,
        value_bias,
        out_bias,
        attn_gain,
        attn_shift,
        down_bias,
        ffn_gain,
        ffn_shift,
    ]
    share = query_bias.shape[0]
    packed = jnp.concatenate(singles + [up_bias])[None, :]
    held = [packed]
    for k in range(1, owners):
        held.append(lax.ppermute(packed, "dp", [(i, i ^ k) for i in range(owners)]))
    vectors = []
    for d in range(owners):
        found = held[0]
        for k in range(1, owners):
            found = jnp.where((row ^ d) == k, held[k], found)
        vectors.append(found)
    vectors = jnp.concatenate(vectors, axis=0).astype(f32)
    bias = [vectors[:, i * share : (i + 1) * share].reshape(1, width) for i in range(8)]
    up_bias_all = vectors[:, 8 * share :].reshape(1, -1)
    queries = (
        jnp.dot(rows, qkv_all[:, :width], preferred_element_type=f32) + bias[0]
    ).astype(bf16)
    kv_bias = jnp.concatenate([jnp.zeros_like(bias[1]), bias[1]], axis=1)
    both = (jnp.dot(stream, qkv_all[:, width:], preferred_element_type=f32) + kv_bias).astype(bf16)
    out_all = gather(out_weight)
    up_all = gather(up_weight)
    down_all = gather(down_weight)
    held, _ = lax.optimization_barrier((cotangent, stream))
    cot = jnp.concatenate([pick(held, side), exchange(pick(held, 1 - side), half)], axis=0)

    mixed, stats = attend(queries, both, extra, head_dim)
    (
        result,
        active,
        hidden,
        grad_branch,
        grad_upper,
        grad_first,
        grad_attn,
        grad_mixed,
        deltas,
        sums,
        up_sum,
    ) = middle(
        mixed,
        rows,
        cot,
        live_rows,
        out_all,
        up_all,
        down_all,
        jnp.concatenate(bias[2:] + [jnp.zeros((2, width), f32)], axis=0),
        up_bias_all,
        head_dim,
    )
    output = arrange(result[:block], exchange(result[block:], half))

    def scatter(grad):
        return lax.psum_scatter(grad, ("dp", "ctx"), scatter_dimension=0, tiled=True)

    def spread(part):
        return lax.all_gather(part, "ctx", axis=0, tiled=True)

    devices = owners * ring
    inner = up_weight.shape[1]
    laid = width % (8 * devices) == 0 and inner % width == 0
    if laid:
        piece = middle_grads(hidden, grad_upper, mixed, grad_attn, active, grad_branch, owners, ring)
        pieces = spread(scatter(piece)).astype(f32)
        each, tall = (width // devices, inner // devices)
        blocks = inner // width
        cut = blocks * each
        grad_up_weight = jnp.concatenate(
            [pieces[:, i * each : (i + 1) * each, :].reshape(share, width) for i in range(blocks)],
            axis=1,
        )
        grad_down_weight = pieces[:, cut : cut + tall, :].reshape(-1, width)
        grad_out_weight = pieces[:, cut + tall :, :].reshape(share, width)
    else:
        grad_up_weight = spread(scatter(dot(hidden, grad_upper, 0, 0).astype(bf16))).astype(f32)
        grad_down_weight = spread(scatter(dot(active, grad_branch, 0, 0).astype(bf16))).astype(f32)
        grad_out_weight = spread(scatter(dot(mixed, grad_attn, 0, 0).astype(bf16))).astype(f32)

    kv_weight = qkv_all[:, width:]
    total_keys = stream.shape[0]
    grad_queries = None
    shares = []
    arrived = []
    last = total_keys
    for bit in list(reversed(bits)) + [0]:
        first = last // 2 if bit else 0
        grad_queries, grad_both = attend_back(
            queries, grad_mixed, stats, deltas, both, extra, head_dim, first, last - first, grad_queries
        )
        shares.append(grad_both)
        kv_grads = grad_both.reshape(2 * width, last - first)
        grad_stream = dot(kv_grads, kv_weight, 0, 1)
        for other in arrived:
            grad_stream = grad_stream + other[first:last].astype(f32)
        if bit:
            low = grad_stream.astype(bf16)
            low, grad_queries = lax.optimization_barrier((low, grad_queries))
            arrived.append(exchange(low, bit))
        last = first
    grad_query_low = grad_queries.astype(bf16)
    grad_rows = grad_first + dot(grad_query_low, qkv_all[:, :width], 1, 1) + grad_stream
    grad_rows_low = grad_rows.astype(bf16)
    grad_rows_low, grad_queries = lax.optimization_barrier((grad_rows_low, grad_queries))

    squares = jnp.sum(sums[6:9], axis=1)
    lane = jnp.arange(width)
    mine = (lane // 3) == (row * 2 + side)
    squares = jnp.where(
        lane % 3 == 0, squares[0], jnp.where(lane % 3 == 1, squares[1], squares[2])
    )
    squares = jnp.where(mine, squares, 0.0)[None, :]
    small = jnp.concatenate(
        [jnp.zeros((2, width), f32), sums[:6], squares, up_sum[0].reshape(-1, width)], axis=0
    )
    small = jnp.pad(small, ((0, -small.shape[0] % 8), (0, 0)))
    if laid:
        grad_qkv_weight, summed, other = closing(
            grad_queries, stream, shares, small, grad_rows_low[block:], owners, ring
        )
        grad_qkv_weight = grad_qkv_weight.reshape(share, 3 * width)
    else:
        other = exchange(grad_rows_low[block:], half)
        kv_parts = []
        for which in range(2):
            last = total_keys
            part = 0.0
            for v in shares:
                part = part + dot(stream[last - v.shape[2] : last], v[which], 0, 1)
                last = last - v.shape[2]
            kv_parts.append(part)
        grad_qkv_weight = jnp.concatenate([dot(rows, grad_query_low, 0, 0)] + kv_parts, axis=1)
        grad_qkv_weight = spread(scatter(grad_qkv_weight.astype(bf16))).astype(f32)
        grad_query_bias = jnp.sum(grad_query_low, axis=0, dtype=f32)
        grad_value_bias = sum(jnp.sum(v[1], axis=1, dtype=f32) for v in shares)
        small = jnp.concatenate([grad_query_bias[None], grad_value_bias[None], small[2:]], axis=0)
        summed = lax.psum(small, ("dp", "ctx"))

    grad_tokens = arrange(grad_rows_low[:block], other)
    totals = [lax.dynamic_slice_in_dim(summed[i], row * share, share) for i in range(8)]
    tall = inner // owners
    up_total = lax.dynamic_slice_in_dim(summed[9:].reshape(-1), row * tall, tall)
    seq_squares = lax.dynamic_slice_in_dim(summed[8], row * 6, 6).reshape(2, 3)
    branch_rms = jnp.sqrt(seq_squares / (lengths.astype(f32)[:, None] * width) + rms_eps)
    return (
        output,
        grad_tokens,
        grad_qkv_weight,
        totals[0],
        totals[1],
        grad_out_weight,
        totals[2],
        totals[3],
        totals[4],
        grad_up_weight,
        up_total,
        grad_down_weight,
        totals[5],
        totals[6],
        totals[7],
        branch_rms,
    )


def solution(mesh):
    in_specs = (
        P("dp", "ctx", None),
        P("dp", "ctx", None),
        P("dp"),
        P("dp", None),
        P("dp", None),
        P("dp"),
        P("dp"),
        P("dp", None),
        P("dp"),
        P("dp"),
        P("dp"),
        P("dp", None),
        P("dp"),
        P("dp", None),
        P("dp"),
        P("dp"),
        P("dp"),
    )
    out_specs = (
        P("dp", "ctx", None),
        P("dp", "ctx", None),
        P("dp", None),
        P("dp"),
        P("dp"),
        P("dp", None),
        P("dp"),
        P("dp"),
        P("dp"),
        P("dp", None),
        P("dp"),
        P("dp", None),
        P("dp"),
        P("dp"),
        P("dp"),
        P("dp", None),
    )
    return jax.shard_map(
        functools.partial(shards, mesh.shape["ctx"]),
        mesh=mesh,
        in_specs=in_specs,
        out_specs=out_specs,
        check_vma=False,
    )
```

```python
import functools

import jax
import jax.numpy as jnp
from jax import lax
from jax.experimental import pallas as pl
from jax.experimental.pallas import tpu as pltpu
from jax.sharding import PartitionSpec as P

HEADS = 12

norm_eps = 1e-12
rms_eps = 1e-06
masked_bias = -1e30
log2_e = 1.4426950408889634
lanes = 128
vmem_grant = 56 << 20
f32 = jnp.float32
bf16 = jnp.bfloat16


def norm_parts(total, gain, shift):
    mean = jnp.mean(total, axis=-1, keepdims=True)
    centred = total - mean
    inverse = lax.rsqrt(jnp.mean(centred * centred, axis=-1, keepdims=True) + norm_eps)
    unit = centred * inverse
    return (unit * gain + shift, unit, inverse)


def norm_back(grad_unit, unit, inverse):
    mean_grad = jnp.mean(grad_unit, axis=-1, keepdims=True)
    mean_cross = jnp.mean(grad_unit * unit, axis=-1, keepdims=True)
    return inverse * (grad_unit - mean_grad - unit * mean_cross)


def dot(left, right, left_dim, right_dim):
    return lax.dot_general(
        left, right, (((left_dim,), (right_dim,)), ((), ())), preferred_element_type=f32
    )


def head_lanes(head, head_dim):
    lane = lax.broadcasted_iota(jnp.int32, (1, lanes), 1)
    return (lane // head_dim) == head


def spread_lanes(first_head, second_head, unit, head_dim):
    rows = first_head.shape[0]
    lane = lax.broadcasted_iota(jnp.int32, (rows, lanes), 1)
    place = lane % head_dim
    value = -jnp.where(lane < head_dim, second_head, first_head)
    high = value.astype(bf16).astype(f32)
    rest = value - high
    mid = rest.astype(bf16).astype(f32)
    low = rest - mid
    out = jnp.where(place == 1, high, jnp.where(place == 2, mid, jnp.where(place == 3, low, 0.0)))
    return jnp.where(place == 0, unit, out).astype(bf16)


def attend_kernel(scale, head_dim, step, q_ref, k_ref, v_ref, extra_ref, o_ref, stat_ref, kb, vb):
    keys = k_ref.shape[0]

    @pl.when(pl.program_id(1) == 0)
    def _():
        for h in range(2):
            kb[h] = jnp.where(head_lanes(h, head_dim), k_ref[...], extra_ref[...])
            vb[h] = jnp.where(head_lanes(h, head_dim), v_ref[...], extra_ref[...])

    factor = scale * log2_e
    queries = q_ref[...]
    lane = lax.broadcasted_iota(jnp.int32, (1, lanes), 1)
    bias_lane = jnp.where(lane % head_dim == 0, 1.0, 0.0).astype(bf16)
    outs, logs = ([], [])
    for h in range(2):
        own = jnp.where(head_lanes(h, head_dim), queries, bias_lane)
        best, acc = (None, None)
        for first in range(0, keys, step):
            scores = dot(own, kb[h, first : first + step, :], 1, 1)
            high = jnp.max(scores, axis=1, keepdims=True)
            new_best = high if best is None else jnp.maximum(best, high)
            weights = jnp.exp2((scores - new_best) * factor).astype(bf16)
            part = dot(weights, vb[h, first : first + step, :], 1, 0)
            acc = part if best is None else acc * jnp.exp2((best - new_best) * factor) + part
            best = new_best
        free = (1 - h) * head_dim + 1
        total = acc[:, free : free + 1]
        outs.append(acc / total)
        logs.append(best + jnp.log2(total) * (1.0 / factor))
    o_ref[...] = jnp.where(head_lanes(0, head_dim), outs[0], outs[1]).astype(bf16)
    stat_ref[...] = spread_lanes(logs[0], logs[1], 1.0, head_dim)


def attend(queries, both, extra, head_dim):
    rows, width = queries.shape
    keys = both.shape[0]
    pairs = width // lanes
    row_step = min(512, rows)
    step = min(2048, keys)
    scale = head_dim ** (-0.5)
    return pl.pallas_call(
        functools.partial(attend_kernel, scale, head_dim, step),
        grid=(pairs, rows // row_step),
        in_specs=[
            pl.BlockSpec((row_step, lanes), lambda h, i: (i, h)),
            pl.BlockSpec((keys, lanes), lambda h, i: (0, h)),
            pl.BlockSpec((keys, lanes), lambda h, i: (0, h + pairs)),
            pl.BlockSpec((keys, lanes), lambda h, i: (0, 0)),
        ],
        out_specs=[
            pl.BlockSpec((row_step, lanes), lambda h, i: (i, h)),
            pl.BlockSpec((None, row_step, lanes), lambda h, i: (h, i, 0)),
        ],
        out_shape=[
            jax.ShapeDtypeStruct((rows, width), bf16),
            jax.ShapeDtypeStruct((pairs, rows, lanes), bf16),
        ],
        scratch_shapes=[pltpu.VMEM((2, keys, lanes), bf16), pltpu.VMEM((2, keys, lanes), bf16)],
        compiler_params=pltpu.CompilerParams(vmem_limit_bytes=vmem_grant),
        cost_estimate=pl.CostEstimate(
            flops=4 * rows * keys * width * 4,
            bytes_accessed=keys * width * 4 + rows * width * 6,
            transcendentals=rows * keys * width // head_dim,
        ),
        name="attend",
    )(queries, both, both, extra)


def attend_back_kernel(scale, head_dim, row_step, resumed, *refs):
    q_ref, da_ref, qx_ref, dax_ref, k_ref, v_ref, extra_ref = refs[:7]
    start_ref = refs[7] if resumed else None
    dq_ref, dkv_ref = refs[-2:]
    j = pl.program_id(1)
    rows = q_ref.shape[0]
    factor = scale * log2_e
    keys, values, extra = (k_ref[...], v_ref[...], extra_ref[...])
    dk, dv = (None, None)
    for first in range(0, rows, row_step):
        part = slice(first, first + row_step)
        queries, grads = (q_ref[part, :], da_ref[part, :])
        queries_extra, grads_extra = (qx_ref[part, :], dax_ref[part, :])
        dq = None
        for h in range(2):
            sel = head_lanes(h, head_dim)
            scores = dot(
                jnp.where(sel, queries, queries_extra), jnp.where(sel, keys, extra), 1, 1
            )
            weights = jnp.exp2(scores * factor)
            grad_weights = dot(
                jnp.where(sel, grads, grads_extra), jnp.where(sel, values, extra), 1, 1
            )
            grad_scores = (weights * grad_weights).astype(bf16)
            none = jnp.zeros_like(queries)
            part_dv = dot(jnp.where(sel, grads, none), weights.astype(bf16), 0, 0)
            part_dk = dot(jnp.where(sel, queries, none), grad_scores, 0, 0)
            part_dq = dot(grad_scores, jnp.where(sel, keys, jnp.zeros_like(keys)), 1, 0)
            dv = part_dv if dv is None else dv + part_dv
            dk = part_dk if dk is None else dk + part_dk
            dq = part_dq if dq is None else dq + part_dq
        dq = dq * scale

        @pl.when(j == 0)
        def _():
            dq_ref[part, :] = dq + start_ref[part, :] if resumed else dq

        @pl.when(j > 0)
        def _():
            dq_ref[part, :] += dq

    dkv_ref[0] = (dk * scale).astype(bf16)
    dkv_ref[1] = dv.astype(bf16)


def attend_back(queries, grads, stats, deltas, both, extra, head_dim, first, count, start):
    rows, width = queries.shape
    pairs = width // lanes
    row_step = min(1024, rows)
    step = min(512, count)
    skip = first // step
    scale = head_dim ** (-0.5)
    resumed = start is not None
    more = [pl.BlockSpec((rows, lanes), lambda h, j: (0, h))] if resumed else []
    return pl.pallas_call(
        functools.partial(attend_back_kernel, scale, head_dim, row_step, resumed),
        grid=(pairs, count // step),
        in_specs=[
            pl.BlockSpec((rows, lanes), lambda h, j: (0, h)),
            pl.BlockSpec((rows, lanes), lambda h, j: (0, h)),
            pl.BlockSpec((None, rows, lanes), lambda h, j: (h, 0, 0)),
            pl.BlockSpec((None, rows, lanes), lambda h, j: (h, 0, 0)),
            pl.BlockSpec((step, lanes), lambda h, j: (j + skip, h)),
            pl.BlockSpec((step, lanes), lambda h, j: (j + skip, h + pairs)),
            pl.BlockSpec((step, lanes), lambda h, j: (j + skip, 0)),
        ]
        + more,
        out_specs=[
            pl.BlockSpec((rows, lanes), lambda h, j: (0, h)),
            pl.BlockSpec((2, lanes, step), lambda h, j: (0, h, j)),
        ],
        out_shape=[
            jax.ShapeDtypeStruct((rows, width), f32),
            jax.ShapeDtypeStruct((2, width, count), bf16),
        ],
        compiler_params=pltpu.CompilerParams(vmem_limit_bytes=vmem_grant),
        cost_estimate=pl.CostEstimate(
            flops=10 * rows * count * width * 4,
            bytes_accessed=count * width * 8 + rows * width * 12,
            transcendentals=rows * count * width // head_dim,
        ),
        name="attend_back",
    )(queries, grads, stats, deltas, both, both, extra, *([start] if resumed else []))


def key_lanes(live, head_dim):
    lane = jnp.arange(lanes, dtype=jnp.int32) % head_dim
    bias = jnp.where(live, 0.0, masked_bias)[:, None]
    ones = jnp.where((lane >= 1) & (lane <= 3), 1.0, 0.0)[None, :]
    return jnp.where(lane[None, :] == 0, bias, ones).astype(bf16)


def opening_kernel(
    owners,
    ring,
    pieces,
    own_ref,
    other_ref,
    weight_ref,
    packed_ref,
    x_ref,
    w_ref,
    vec_ref,
    q_ref,
    kv_ref,
    xs,
    ws,
    vec,
    qs,
    kvs,
    load_sem,
    store_sem,
    send_sem,
    recv_sem,
):
    row, here = (lax.axis_index("dp"), lax.axis_index("ctx"))
    core = lax.rem(here, 2)
    block, width = own_ref.shape
    share = weight_ref.shape[0]
    half = share // 2
    mate, deep, far = ((row, here ^ 1), (row, here ^ 2), (row, here ^ (ring // 2)))
    owner_peers = [(row ^ k, here) for k in range(1, owners)]
    peers = [mate, deep, far] + owner_peers
    barrier = pltpu.get_barrier_semaphore()
    for peer in peers:
        pl.semaphore_signal(barrier, inc=1, device_id=peer, device_id_type=pl.DeviceIdType.MESH)
    own_load = pltpu.make_async_copy(own_ref, xs.at[0], load_sem.at[0])
    weight_load = pltpu.make_async_copy(weight_ref, ws.at[row], load_sem.at[1])
    vec_load = pltpu.make_async_copy(packed_ref, vec.at[row], load_sem.at[2])
    for load in (own_load, weight_load, vec_load):
        load.start()
    sent, stored = ([], [])
    count = [0]

    def send(source, target, peer):
        slot = count[0]
        count[0] += 1
        copy = pltpu.make_async_remote_copy(
            src_ref=source,
            dst_ref=target,
            send_sem=send_sem.at[slot],
            recv_sem=recv_sem.at[slot],
            device_id=peer,
            device_id_type=pl.DeviceIdType.MESH,
        )
        copy.start()
        sent.append(copy)
        return copy

    def store(source, target):
        copy = pltpu.make_async_copy(source, target, store_sem.at[len(stored)])
        copy.start()
        stored.append(copy)

    step = block // pieces
    parts = [pl.ds(j * step, step) for j in range(pieces)]
    pl.semaphore_wait(barrier, len(peers))
    weights = [
        send(weight_ref.at[pl.ds(core * half, half)], ws.at[row, pl.ds(core * half, half)], peer)
        for peer in owner_peers
    ]
    moved = [send(other_ref.at[part], xs.at[1, part], far) for part in parts]
    own_deep = send(own_ref, xs.at[2], deep)
    own_mate = send(own_ref, xs.at[4], mate)
    vectors = [send(packed_ref, vec.at[row], peer) for peer in owner_peers]

    moved_deep, moved_mate = ([], [])
    weights_mate = []
    for j, part in enumerate(parts):
        moved[j].wait_recv()
        moved_deep.append(send(xs.at[1, part], xs.at[3, part], deep))
        moved_mate.append(send(xs.at[1, part], xs.at[5, part], mate))
        if j == pieces // 2:
            for k in range(1, owners):
                weights[k - 1].wait_recv()
                held = ws.at[row ^ k, pl.ds(core * half, half)]
                weights_mate.append(send(held, held, mate))
    own_deep.wait_recv()
    deep_mate = send(xs.at[2], xs.at[6], mate)
    for load in (own_load, weight_load, vec_load):
        load.wait()
    for copy in vectors + weights_mate:
        copy.wait_recv()
    for d in range(owners):
        store(ws.at[d], w_ref.at[d])
    store(vec, vec_ref)

    def bias(which):
        return jnp.concatenate(
            [vec[d, :, which * share : (which + 1) * share] for d in range(owners)], axis=1
        ).astype(f32)

    value_bias = bias(1)
    none = jnp.zeros_like(value_bias)

    def product(place, first, last):
        total = None
        for d in range(owners):
            left = xs[place, :, d * share : (d + 1) * share]
            part = dot(left, ws[d, :, first:last], 1, 0)
            total = part if total is None else total + part
        return total

    def project(place):
        store(xs.at[place], x_ref.at[place])
        if place < 2:
            qs[place] = (product(place, 0, width) + bias(0)).astype(bf16)
            store(qs.at[place], q_ref.at[place])
        kvs[place, :, :width] = product(place, width, 2 * width).astype(bf16)
        kvs[place, :, width:] = (product(place, 2 * width, 3 * width) + value_bias).astype(bf16)
        store(kvs.at[place], kv_ref.at[place])

    project(0)
    own_mate.wait_recv()
    project(4)
    project(1)
    for copy in moved_mate:
        copy.wait_recv()
    project(5)
    project(2)
    deep_mate.wait_recv()
    project(6)
    far_mate = []
    for j, part in enumerate(parts):
        moved_deep[j].wait_recv()
        far_mate.append(send(xs.at[3, part], xs.at[7, part], mate))
    project(3)
    for copy in far_mate:
        copy.wait_recv()
    project(7)
    for copy in sent:
        copy.wait_send()
    for copy in stored:
        copy.wait()


def opening(own, other, weight, packed, owners, ring):
    block, width = own.shape
    share = weight.shape[0]
    blocks = ring
    pieces = 4
    any_space = pl.BlockSpec(memory_space=pl.ANY)
    copies = 2 * (owners - 1) + 3 * pieces + 3 + (owners - 1) + pieces
    shapes = [
        jax.ShapeDtypeStruct((blocks, block, width), bf16),
        jax.ShapeDtypeStruct((owners,) + weight.shape, bf16),
        jax.ShapeDtypeStruct((owners,) + packed.shape, bf16),
        jax.ShapeDtypeStruct((2, block, width), bf16),
        jax.ShapeDtypeStruct((blocks, block, 2 * width), bf16),
    ]
    return pl.pallas_call(
        functools.partial(opening_kernel, owners, ring, pieces),
        in_specs=[any_space] * 4,
        out_specs=[any_space] * 5,
        out_shape=shapes,
        scratch_shapes=[pltpu.VMEM(v.shape, v.dtype) for v in shapes]
        + [
            pltpu.SemaphoreType.DMA((3,)),
            pltpu.SemaphoreType.DMA((owners + 1 + 2 * blocks + 2,)),
            pltpu.SemaphoreType.DMA((copies,)),
            pltpu.SemaphoreType.DMA((copies,)),
        ],
        compiler_params=pltpu.CompilerParams(
            vmem_limit_bytes=vmem_grant, collective_id=1, has_side_effects=True
        ),
        cost_estimate=pl.CostEstimate(
            flops=8 * blocks * block * width * width, bytes_accessed=200 << 20, transcendentals=0
        ),
        name="opening",
    )(own, other, weight, packed)


def middle_kernel(
    head_dim,
    chunk,
    mixed_ref,
    x_ref,
    cot_ref,
    live_ref,
    out_ref,
    up_ref,
    down_ref,
    vec_ref,
    up_bias_ref,
    y_ref,
    active_ref,
    hidden_ref,
    dbranch_ref,
    dupper_ref,
    dz_ref,
    dattn_ref,
    dmixed_ref,
    delta_ref,
    sums_ref,
    up_sum_ref,
    slope,
):
    width = x_ref.shape[1]
    inner = up_ref.shape[1]
    out_bias, gain_first, shift_first = (vec_ref[0:1, :], vec_ref[1:2, :], vec_ref[2:3, :])
    down_bias, gain_second, shift_second = (vec_ref[3:4, :], vec_ref[4:5, :], vec_ref[5:6, :])
    live = live_ref[...]
    mixed = mixed_ref[...]
    attn = dot(mixed, out_ref[...], 1, 0) + out_bias
    hidden, unit_first, inverse_first = norm_parts(
        x_ref[...].astype(f32) + attn, gain_first, shift_first
    )
    hidden_low = hidden.astype(bf16)
    hidden_ref[...] = hidden_low
    branch = down_bias
    for first in range(0, inner, chunk):
        part = slice(first, first + chunk)
        upper = dot(hidden_low, up_ref[:, part], 1, 0) + up_bias_ref[:, part]
        below = 0.5 + 0.5 * lax.erf(upper * (0.5**0.5))
        active = (upper * below).astype(bf16)
        bell = jnp.exp2(upper * upper * (-0.5 * log2_e)) * 0.3989422804014327
        slope[:, part] = (below + upper * bell).astype(bf16)
        active_ref[:, part] = active
        branch = branch + dot(active, down_ref[part, :], 1, 0)
    normed, unit_second, inverse_second = norm_parts(hidden + branch, gain_second, shift_second)
    result = normed * live
    y_ref[...] = result.astype(bf16)
    grad_out = cot_ref[...].astype(f32) * live
    grad_second = norm_back(grad_out * gain_second, unit_second, inverse_second)
    grad_branch = grad_second.astype(bf16)
    dbranch_ref[...] = grad_branch
    grad_hidden = grad_second
    up_sums = []
    for first in range(0, inner, chunk):
        part = slice(first, first + chunk)
        grad_active = dot(grad_branch, down_ref[part, :], 1, 1)
        grad_upper = (grad_active * slope[:, part].astype(f32)).astype(bf16)
        dupper_ref[:, part] = grad_upper
        up_sums.append(jnp.sum(grad_upper.astype(f32), axis=0, keepdims=True))
        grad_hidden = grad_hidden + dot(grad_upper, up_ref[:, part], 1, 1)
    grad_first = norm_back(grad_hidden * gain_first, unit_first, inverse_first)
    dz_ref[...] = grad_first
    grad_attn = grad_first.astype(bf16)
    dattn_ref[...] = grad_attn
    grad_mixed = dot(grad_attn, out_ref[...], 1, 1).astype(bf16)
    dmixed_ref[...] = grad_mixed
    cross = grad_mixed.astype(f32) * mixed.astype(f32)
    lane = lax.broadcasted_iota(jnp.int32, (1, lanes), 1)
    lower = lane < head_dim
    for p in range(width // lanes):
        pair = cross[:, p * lanes : (p + 1) * lanes]
        first_head = jnp.sum(jnp.where(lower, pair, 0.0), axis=1, keepdims=True)
        second_head = jnp.sum(jnp.where(lower, 0.0, pair), axis=1, keepdims=True)
        delta_ref[p] = spread_lanes(first_head, second_head, 0.0, head_dim)
    sums = [
        grad_attn.astype(f32),
        grad_hidden * unit_first,
        grad_hidden,
        grad_branch.astype(f32),
        grad_out * unit_second,
        grad_out,
        result * result,
        attn * attn * live,
        branch * branch * live,
    ]
    first_step = pl.program_id(0) == 0

    @pl.when(first_step)
    def _():
        sums_ref[...] = jnp.zeros_like(sums_ref)
        up_sum_ref[...] = jnp.zeros_like(up_sum_ref)

    for i, value in enumerate(sums):
        sums_ref[i : i + 1, :] += jnp.sum(value, axis=0, keepdims=True)
    up_sum_ref[0:1, :] += jnp.concatenate(up_sums, axis=1)


def middle(mixed, rows, cot, live, out_all, up_all, down_all, vectors, up_bias, head_dim):
    count, width = rows.shape
    inner = up_all.shape[1]
    pairs = width // lanes
    row_step = min(256, count)
    chunk = min(768, inner)

    def fixed(shape):
        return pl.BlockSpec(shape, lambda i: (0, 0), pipeline_mode=pl.Buffered(1))

    def block(columns):
        return pl.BlockSpec((row_step, columns), lambda i: (i, 0))

    return pl.pallas_call(
        functools.partial(middle_kernel, head_dim, chunk),
        grid=(count // row_step,),
        in_specs=[
            block(width),
            block(width),
            block(width),
            block(1),
            fixed((width, width)),
            fixed((width, inner)),
            fixed((inner, width)),
            fixed(vectors.shape),
            fixed(up_bias.shape),
        ],
        out_specs=[
            block(width),
            block(inner),
            block(width),
            block(width),
            block(inner),
            block(width),
            block(width),
            block(width),
            pl.BlockSpec((pairs, row_step, lanes), lambda i: (0, i, 0)),
            pl.BlockSpec((16, width), lambda i: (0, 0)),
            pl.BlockSpec((8, inner), lambda i: (0, 0)),
        ],
        out_shape=[
            jax.ShapeDtypeStruct((count, width), bf16),
            jax.ShapeDtypeStruct((count, inner), bf16),
            jax.ShapeDtypeStruct((count, width), bf16),
            jax.ShapeDtypeStruct((count, width), bf16),
            jax.ShapeDtypeStruct((count, inner), bf16),
            jax.ShapeDtypeStruct((count, width), f32),
            jax.ShapeDtypeStruct((count, width), bf16),
            jax.ShapeDtypeStruct((count, width), bf16),
            jax.ShapeDtypeStruct((pairs, count, lanes), bf16),
            jax.ShapeDtypeStruct((16, width), f32),
            jax.ShapeDtypeStruct((8, inner), f32),
        ],
        scratch_shapes=[pltpu.VMEM((row_step, inner), bf16)],
        compiler_params=pltpu.CompilerParams(vmem_limit_bytes=vmem_grant),
        cost_estimate=pl.CostEstimate(
            flops=4 * count * width * (2 * inner + width),
            bytes_accessed=4 * width * inner + count * (18 * width + 4 * inner),
            transcendentals=4 * count * inner,
        ),
        name="middle",
    )(mixed, rows, cot, live, out_all, up_all, down_all, vectors, up_bias)


def up_out_kernel(blocks, hidden_ref, dupper_ref, mixed_ref, dattn_ref, o_ref):
    s = pl.program_id(0)

    @pl.when(s < blocks)
    def _():
        o_ref[...] = dot(hidden_ref[...], dupper_ref[...], 0, 0).astype(bf16).reshape(o_ref.shape)

    @pl.when(s == blocks)
    def _():
        o_ref[...] = dot(mixed_ref[...], dattn_ref[...], 0, 0).astype(bf16).reshape(o_ref.shape)


def down_kernel(active_ref, dbranch_ref, held_ref, o_ref):
    del held_ref
    o_ref[...] = dot(active_ref[...], dbranch_ref[...], 0, 0).astype(bf16).reshape(o_ref.shape)


def middle_grads(hidden, dupper, mixed, dattn, active, dbranch, owners, ring):
    count, width = hidden.shape
    inner = dupper.shape[1]
    devices = owners * ring
    share = width // devices
    blocks = inner // width
    tall = inner // devices
    piece = blocks * share + tall + share
    shape = jax.ShapeDtypeStruct((devices, piece, width), bf16)
    params = pltpu.CompilerParams(vmem_limit_bytes=vmem_grant)
    whole = pl.BlockSpec((count, width), lambda s: (0, 0))
    held = pl.pallas_call(
        functools.partial(up_out_kernel, blocks),
        grid=(blocks + 1,),
        in_specs=[
            whole,
            pl.BlockSpec((count, width), lambda s: (0, jnp.minimum(s, blocks - 1))),
            whole,
            whole,
        ],
        out_specs=pl.BlockSpec(
            (devices, share, width),
            lambda s: (0, jnp.where(s < blocks, s, piece // share - 1), 0),
        ),
        out_shape=shape,
        compiler_params=params,
        cost_estimate=pl.CostEstimate(
            flops=2 * count * width * (inner + width),
            bytes_accessed=2 * (count + width) * (inner + 3 * width),
            transcendentals=0,
        ),
        name="up_grads",
    )(hidden, dupper, mixed, dattn)
    return pl.pallas_call(
        down_kernel,
        grid=(owners,),
        in_specs=[
            pl.BlockSpec((count, inner // owners), lambda s: (0, s)),
            whole,
            pl.BlockSpec(memory_space=pl.ANY),
        ],
        out_specs=pl.BlockSpec((ring, tall, width), lambda s: (s, blocks * share // tall, 0)),
        out_shape=shape,
        input_output_aliases={2: 0},
        compiler_params=params,
        cost_estimate=pl.CostEstimate(
            flops=2 * count * width * inner,
            bytes_accessed=2 * (count + width) * (inner + width),
            transcendentals=0,
        ),
        name="down_grads",
    )(active, dbranch, held)


def closing_kernel(owners, ring, firsts, dq_ref, x_ref, *refs):
    shares = refs[: len(firsts)]
    small_ref, home_ref, out_ref, small_out_ref, home_out_ref = refs[len(firsts) : len(firsts) + 5]
    (
        xs,
        dq,
        dkv,
        whole,
        parts,
        in_core,
        by_owner,
        in_owner,
        by_piece,
        in_piece,
        done,
        in_done,
        small,
        small_core,
        small_owner,
        small_piece,
        load_sem,
        send_sem,
        recv_sem,
    ) = refs[len(firsts) + 5 :]
    row, here = (lax.axis_index("dp"), lax.axis_index("ctx"))
    core, depth = (lax.rem(here, 2), here // 2)
    deep = ring // 2
    count = dq.shape[0]
    loads = [
        pltpu.make_async_copy(dq_ref, dq, load_sem.at[0]),
        pltpu.make_async_copy(x_ref, xs, load_sem.at[1]),
    ]
    for i, first in enumerate(firsts):
        columns = pl.ds(first, shares[i].shape[2])
        loads.append(pltpu.make_async_copy(shares[i], dkv.at[:, :, columns], load_sem.at[2 + i]))
    for load in loads:
        load.start()

    mate = (row, here ^ 1)
    owner_peers = [(row ^ k, here) for k in range(1, owners)]
    depth_peers = [(row, here ^ (2 * k)) for k in range(1, deep)]
    barrier = pltpu.get_barrier_semaphore()
    peers = [mate] + owner_peers + depth_peers
    for peer in peers:
        pl.semaphore_signal(barrier, inc=1, device_id=peer, device_id_type=pl.DeviceIdType.MESH)

    sent = []

    def send(source, target, peer, m, slot):
        copy = pltpu.make_async_remote_copy(
            src_ref=source,
            dst_ref=target,
            send_sem=send_sem.at[m, slot],
            recv_sem=recv_sem.at[m, slot],
            device_id=peer,
            device_id_type=pl.DeviceIdType.MESH,
        )
        copy.start()
        sent.append(copy)
        return copy

    at_owner = 1
    at_piece = owners
    at_done = at_piece + deep - 1
    at_back = at_done + deep - 1
    tile = 256

    def to_core(m):
        def one(t, carry):
            columns = pl.ds(pl.multiple_of(t * tile, tile), tile)
            if m == 0:
                whole[columns, :] = dot(xs[0:count, columns], dq[...].astype(bf16), 0, 0)
            else:
                whole[columns, :] = dot(xs[:, columns], dkv[m - 1], 0, 1)
            return carry

        lax.fori_loop(0, whole.shape[0] // tile, one, 0)
        parts[m] = whole[...].reshape(parts.shape[1:]).astype(bf16)
        return [send(parts.at[m, :, 1 - core], in_core.at[m], mate, m, 0)]

    def to_owner(m):
        mine = parts[m, :, core].astype(f32)
        by_owner[m] = (mine + in_core[m].astype(f32)).astype(bf16)
        return [
            send(by_owner.at[m, row ^ k], in_owner.at[m, k - 1], owner_peers[k - 1], m, at_owner + k - 1)
            for k in range(1, owners)
        ]

    def to_piece(m):
        total = by_owner[m, row].astype(f32)
        for k in range(1, owners):
            total = total + in_owner[m, k - 1].astype(f32)
        by_piece[m] = total.reshape(by_piece.shape[1:]).astype(bf16)
        return [
            send(
                by_piece.at[m, depth ^ k],
                in_piece.at[m, k - 1],
                depth_peers[k - 1],
                m,
                at_piece + k - 1,
            )
            for k in range(1, deep)
        ]

    def to_done(m):
        total = by_piece[m, depth].astype(f32)
        for k in range(1, deep):
            total = total + in_piece[m, k - 1].astype(f32)
        done[m, depth] = total.astype(bf16)
        return [
            send(done.at[m, depth], done.at[m, depth], depth_peers[k - 1], m, at_done + k - 1)
            for k in range(1, deep)
        ]

    def to_back(m):
        return [send(done.at[m], in_done.at[m], mate, m, at_back)]

    def finish(m):
        size = out_ref.shape[1]
        columns = slice(m * whole.shape[1], (m + 1) * whole.shape[1])
        out_ref[core, :, columns] = done[m].astype(f32).reshape(size, whole.shape[1])
        out_ref[1 - core, :, columns] = in_done[m].astype(f32).reshape(size, whole.shape[1])
        return []

    stages = [to_core, to_owner, to_piece, to_done, to_back, finish]
    waiting = [[], [], []]
    loads[0].wait()
    loads[1].wait()
    small[...] = small_ref[...]
    small[0:1, :] = jnp.sum(dq[...].astype(bf16).astype(f32), axis=0, keepdims=True)
    for load in loads[2:]:
        load.wait()
    ones = jnp.ones((8, dkv.shape[2]), bf16)
    small[1:2, :] = dot(ones, dkv[1], 1, 1)[0:1, :]
    pl.semaphore_wait(barrier, len(peers))
    home = send(home_ref, home_out_ref, (row, here ^ (ring // 2)), 3, at_back)
    small_waits = [send(small, small_core, mate, 3, 0)]
    for step in range(len(stages) + 2):
        for m in range(3):
            stage = step - m
            if 0 <= stage < len(stages):
                for copy in waiting[m]:
                    copy.wait_recv()
                waiting[m] = stages[stage](m)
        if step == 1:
            small_waits[0].wait_recv()
            small_owner[0] = small[...] + small_core[...]
            small_waits = [
                send(small_owner.at[0], small_owner.at[k], owner_peers[k - 1], 3, k)
                for k in range(1, owners)
            ]
        if step == 3:
            total = small_owner[0]
            for k in range(1, owners):
                small_waits[k - 1].wait_recv()
                total = total + small_owner[k]
            small_piece[0] = total
            small_waits = [
                send(small_piece.at[0], small_piece.at[k], depth_peers[k - 1], 3, at_piece + k - 1)
                for k in range(1, deep)
            ]
        if step == 5:
            total = small_piece[0]
            for k in range(1, deep):
                small_waits[k - 1].wait_recv()
                total = total + small_piece[k]
            small_out_ref[...] = total
    home.wait_recv()
    for copy in sent:
        copy.wait_send()


def closing(dq, stream, shares, small, home, owners, ring):
    count, width = dq.shape
    keys = stream.shape[0]
    firsts = tuple(first for first, _ in shares)
    shares = [v for _, v in shares]
    deep = ring // 2
    half = width // owners // 2
    piece = half // deep
    slots = 1 + (owners - 1) + 2 * (deep - 1) + 1
    any_space = pl.BlockSpec(memory_space=pl.ANY)
    in_vmem = pl.BlockSpec(memory_space=pltpu.VMEM)
    return pl.pallas_call(
        functools.partial(closing_kernel, owners, ring, firsts),
        in_specs=[any_space] * (2 + len(shares)) + [in_vmem, any_space],
        out_specs=[in_vmem, in_vmem, any_space],
        out_shape=[
            jax.ShapeDtypeStruct((2, half, 3 * width), f32),
            jax.ShapeDtypeStruct(small.shape, f32),
            jax.ShapeDtypeStruct(home.shape, home.dtype),
        ],
        scratch_shapes=[
            pltpu.VMEM((keys, width), bf16),
            pltpu.VMEM((count, width), f32),
            pltpu.VMEM((2, width, keys), bf16),
            pltpu.VMEM((width, width), f32),
            pltpu.VMEM((3, owners, 2, half, width), bf16),
            pltpu.VMEM((3, owners, half, width), bf16),
            pltpu.VMEM((3, owners, half, width), bf16),
            pltpu.VMEM((3, owners - 1, half, width), bf16),
            pltpu.VMEM((3, deep, piece, width), bf16),
            pltpu.VMEM((3, deep - 1, piece, width), bf16),
            pltpu.VMEM((3, deep, piece, width), bf16),
            pltpu.VMEM((3, deep, piece, width), bf16),
            pltpu.VMEM(small.shape, f32),
            pltpu.VMEM(small.shape, f32),
            pltpu.VMEM((owners,) + small.shape, f32),
            pltpu.VMEM((deep,) + small.shape, f32),
            pltpu.SemaphoreType.DMA((2 + len(shares),)),
            pltpu.SemaphoreType.DMA((4, slots)),
            pltpu.SemaphoreType.DMA((4, slots)),
        ],
        compiler_params=pltpu.CompilerParams(
            vmem_limit_bytes=vmem_grant, collective_id=0, has_side_effects=True
        ),
        cost_estimate=pl.CostEstimate(
            flops=20 * keys * width * width, bytes_accessed=100 << 20, transcendentals=0
        ),
        name="closing",
    )(dq, stream, *shares, small, home)


def shards(
    ring,
    tokens,
    cotangent,
    lengths,
    block_order,
    qkv_weight,
    query_bias,
    value_bias,
    out_weight,
    out_bias,
    attn_gain,
    attn_shift,
    up_weight,
    up_bias,
    down_weight,
    down_bias,
    ffn_gain,
    ffn_shift,
):
    seqs, block, width = tokens.shape
    head_dim = width // HEADS
    assert seqs == 2 and ring % 4 == 0
    half = ring // 2
    here = lax.axis_index("ctx")
    side = here // half

    def pick(array, index):
        return lax.dynamic_index_in_dim(array, index, 0, keepdims=False)

    def exchange(array, bit):
        return lax.ppermute(array, "ctx", [(i, i ^ bit) for i in range(ring)])

    def arrange(kept, other):
        first = jnp.where(side == 0, kept, other)
        second = jnp.where(side == 0, other, kept)
        return jnp.stack([first, second])

    def gather(array):
        return lax.all_gather(array, "dp", axis=0, tiled=True)

    own, other = (pick(tokens, side), pick(tokens, 1 - side))
    bits = []
    bit = half // 2
    while bit:
        bits.append(bit)
        bit //= 2
    ids = jnp.stack([here, here ^ half])
    for bit in bits:
        ids = jnp.concatenate([ids, ids ^ bit])
    count_rows = 2 * block

    order = pick(block_order, side)
    length = pick(lengths, side)
    table = jnp.arange(ring, dtype=jnp.int32)
    place_of = jnp.sum(jnp.where(ids[:, None] == table[None, :], order[None, :], 0), axis=1)
    places = place_of[:, None] * block + jnp.arange(block, dtype=jnp.int32)[None, :]
    live_keys = (places < length).reshape(-1)
    live_rows = live_keys[:count_rows, None].astype(f32)
    extra = key_lanes(live_keys, head_dim)

    row = lax.axis_index("dp")
    owners = lax.axis_size("dp")
    devices = owners * ring
    inner = up_weight.shape[1]
    share = query_bias.shape[0]
    laid = ring == 8 and width % (8 * devices) == 0 and inner % width == 0 and block % 32 == 0
    singles = [
        query_bias,
        value_bias,
        out_bias,
        attn_gain,
        attn_shift,
        down_bias,
        ffn_gain,
        ffn_shift,
    ]
    packed = jnp.concatenate(singles + [up_bias])[None, :]
    if laid:
        stream, qkv_all, vectors, queries, both = opening(
            own, other, qkv_weight, packed, owners, ring
        )
        stream = stream.reshape(-1, width)
        qkv_all = qkv_all.reshape(width, -1)
        vectors = vectors.reshape(owners, -1).astype(f32)
        queries = queries.reshape(-1, width)
        both = both.reshape(-1, 2 * width)
    else:
        qkv_all = gather(qkv_weight)
        vectors = gather(packed).astype(f32)
        stream = jnp.concatenate([own, exchange(other, half)], axis=0)
        for bit in bits:
            stream = jnp.concatenate([stream, exchange(stream, bit)], axis=0)
    rows = stream[:count_rows]
    bias = [vectors[:, i * share : (i + 1) * share].reshape(1, width) for i in range(8)]
    up_bias_all = vectors[:, 8 * share :].reshape(1, -1)
    if not laid:
        queries = (
            jnp.dot(rows, qkv_all[:, :width], preferred_element_type=f32) + bias[0]
        ).astype(bf16)
        kv_bias = jnp.concatenate([jnp.zeros_like(bias[1]), bias[1]], axis=1)
        both = jnp.dot(stream, qkv_all[:, width:], preferred_element_type=f32) + kv_bias
        both = both.astype(bf16)
    out_all = gather(out_weight)
    up_all = gather(up_weight)
    down_all = gather(down_weight)
    held, _ = lax.optimization_barrier((cotangent, stream))
    cot = jnp.concatenate([pick(held, side), exchange(pick(held, 1 - side), half)], axis=0)

    mixed, stats = attend(queries, both, extra, head_dim)
    (
        result,
        active,
        hidden,
        grad_branch,
        grad_upper,
        grad_first,
        grad_attn,
        grad_mixed,
        deltas,
        sums,
        up_sum,
    ) = middle(
        mixed,
        rows,
        cot,
        live_rows,
        out_all,
        up_all,
        down_all,
        jnp.concatenate(bias[2:] + [jnp.zeros((2, width), f32)], axis=0),
        up_bias_all,
        head_dim,
    )
    output = arrange(result[:block], exchange(result[block:], half))

    def scatter(grad):
        return lax.psum_scatter(grad, ("dp", "ctx"), scatter_dimension=0, tiled=True)

    def spread(parts):
        return jax.tree.map(lambda v: lax.all_gather(v, "ctx", axis=0, tiled=True), parts)

    if laid:
        scattered = scatter(
            middle_grads(hidden, grad_upper, mixed, grad_attn, active, grad_branch, owners, ring)
        )
    else:
        grads = (dot(hidden, grad_upper, 0, 0), dot(active, grad_branch, 0, 0), dot(mixed, grad_attn, 0, 0))
        scattered = tuple(scatter(grad.astype(bf16)) for grad in grads)
    gathered = []

    kv_weight = qkv_all[:, width:]
    size = 2 * block
    grad_queries = None
    shares = []

    def reduced(place, level):
        nonlocal grad_queries
        if level == len(bits):
            first = place * size
            if place == 0:
                held, grad_queries = lax.optimization_barrier((scattered, grad_queries))
                gathered.append(spread(held))
            grad_queries, grad_both = attend_back(
                queries, grad_mixed, stats, deltas, both, extra, head_dim, first, size, grad_queries
            )
            shares.append((first, grad_both))
            return dot(grad_both.reshape(2 * width, size), kv_weight, 0, 1)
        low = reduced(place + (1 << level), level + 1).astype(bf16)
        low, grad_queries = lax.optimization_barrier((low, grad_queries))
        other = exchange(low, bits[level])
        return reduced(place, level + 1) + other.astype(f32)

    grad_stream = reduced(0, 0)
    grad_query_low = grad_queries.astype(bf16)
    grad_rows = grad_first + dot(grad_query_low, qkv_all[:, :width], 1, 1) + grad_stream
    grad_rows_low = grad_rows.astype(bf16)
    grad_rows_low, grad_queries, pieces = lax.optimization_barrier(
        (grad_rows_low, grad_queries, gathered[0])
    )
    if laid:
        pieces = pieces.astype(f32)
        each, tall = (width // devices, inner // devices)
        blocks = inner // width
        cut = blocks * each
        grad_up_weight = jnp.concatenate(
            [pieces[:, i * each : (i + 1) * each, :].reshape(share, width) for i in range(blocks)],
            axis=1,
        )
        grad_down_weight = pieces[:, cut : cut + tall, :].reshape(-1, width)
        grad_out_weight = pieces[:, cut + tall :, :].reshape(share, width)
    else:
        grad_up_weight, grad_down_weight, grad_out_weight = (v.astype(f32) for v in pieces)

    squares = jnp.sum(sums[6:9], axis=1)
    lane = jnp.arange(width)
    mine = (lane // 3) == (row * 2 + side)
    squares = jnp.where(
        lane % 3 == 0, squares[0], jnp.where(lane % 3 == 1, squares[1], squares[2])
    )
    squares = jnp.where(mine, squares, 0.0)[None, :]
    small = jnp.concatenate(
        [jnp.zeros((2, width), f32), sums[:6], squares, up_sum[0].reshape(-1, width)], axis=0
    )
    small = jnp.pad(small, ((0, -small.shape[0] % 8), (0, 0)))
    if laid:
        grad_qkv_weight, summed, other = closing(
            grad_queries, stream, shares, small, grad_rows_low[block:], owners, ring
        )
        grad_qkv_weight = grad_qkv_weight.reshape(share, 3 * width)
    else:
        other = exchange(grad_rows_low[block:], half)
        kv_parts = []
        for which in range(2):
            part = 0.0
            for first, v in shares:
                part = part + dot(stream[first : first + size], v[which], 0, 1)
            kv_parts.append(part)
        grad_qkv_weight = jnp.concatenate([dot(rows, grad_query_low, 0, 0)] + kv_parts, axis=1)
        grad_qkv_weight = spread(scatter(grad_qkv_weight.astype(bf16))).astype(f32)
        grad_query_bias = jnp.sum(grad_query_low, axis=0, dtype=f32)
        grad_value_bias = sum(jnp.sum(v[1], axis=1, dtype=f32) for _, v in shares)
        small = jnp.concatenate([grad_query_bias[None], grad_value_bias[None], small[2:]], axis=0)
        summed = lax.psum(small, ("dp", "ctx"))

    grad_tokens = arrange(grad_rows_low[:block], other)
    totals = [lax.dynamic_slice_in_dim(summed[i], row * share, share) for i in range(8)]
    tall = inner // owners
    up_total = lax.dynamic_slice_in_dim(summed[9:].reshape(-1), row * tall, tall)
    seq_squares = lax.dynamic_slice_in_dim(summed[8], row * 6, 6).reshape(2, 3)
    branch_rms = jnp.sqrt(seq_squares / (lengths.astype(f32)[:, None] * width) + rms_eps)
    return (
        output,
        grad_tokens,
        grad_qkv_weight,
        totals[0],
        totals[1],
        grad_out_weight,
        totals[2],
        totals[3],
        totals[4],
        grad_up_weight,
        up_total,
        grad_down_weight,
        totals[5],
        totals[6],
        totals[7],
        branch_rms,
    )


def solution(mesh):
    in_specs = (
        P("dp", "ctx", None),
        P("dp", "ctx", None),
        P("dp"),
        P("dp", None),
        P("dp", None),
        P("dp"),
        P("dp"),
        P("dp", None),
        P("dp"),
        P("dp"),
        P("dp"),
        P("dp", None),
        P("dp"),
        P("dp", None),
        P("dp"),
        P("dp"),
        P("dp"),
    )
    out_specs = (
        P("dp", "ctx", None),
        P("dp", "ctx", None),
        P("dp", None),
        P("dp"),
        P("dp"),
        P("dp", None),
        P("dp"),
        P("dp"),
        P("dp"),
        P("dp", None),
        P("dp"),
        P("dp", None),
        P("dp"),
        P("dp"),
        P("dp"),
        P("dp", None),
    )
    return jax.shard_map(
        functools.partial(shards, mesh.shape["ctx"]),
        mesh=mesh,
        in_specs=in_specs,
        out_specs=out_specs,
        check_vma=False,
    )
```

```python
import functools

import jax
import jax.numpy as jnp
from jax import lax
from jax.experimental import pallas as pl
from jax.experimental.pallas import tpu as pltpu
from jax.sharding import PartitionSpec as P

HEADS = 12

norm_eps = 1e-12
rms_eps = 1e-06
masked_bias = -1e30
log2_e = 1.4426950408889634
lanes = 128
vmem_grant = 56 << 20
f32 = jnp.float32
bf16 = jnp.bfloat16


def norm_parts(total, gain, shift):
    mean = jnp.mean(total, axis=-1, keepdims=True)
    centred = total - mean
    inverse = lax.rsqrt(jnp.mean(centred * centred, axis=-1, keepdims=True) + norm_eps)
    unit = centred * inverse
    return (unit * gain + shift, unit, inverse)


def norm_back(grad_unit, unit, inverse):
    mean_grad = jnp.mean(grad_unit, axis=-1, keepdims=True)
    mean_cross = jnp.mean(grad_unit * unit, axis=-1, keepdims=True)
    return inverse * (grad_unit - mean_grad - unit * mean_cross)


def dot(left, right, left_dim, right_dim):
    return lax.dot_general(
        left, right, (((left_dim,), (right_dim,)), ((), ())), preferred_element_type=f32
    )


def head_lanes(head, head_dim):
    lane = lax.broadcasted_iota(jnp.int32, (1, lanes), 1)
    return (lane // head_dim) == head


def spread_lanes(first_head, second_head, unit, head_dim):
    rows = first_head.shape[0]
    lane = lax.broadcasted_iota(jnp.int32, (rows, lanes), 1)
    place = lane % head_dim
    value = -jnp.where(lane < head_dim, second_head, first_head)
    high = value.astype(bf16).astype(f32)
    rest = value - high
    mid = rest.astype(bf16).astype(f32)
    low = rest - mid
    out = jnp.where(place == 1, high, jnp.where(place == 2, mid, jnp.where(place == 3, low, 0.0)))
    return jnp.where(place == 0, unit, out).astype(bf16)


def attend_kernel(
    scale, head_dim, step, q_ref, k_ref, v_ref, extra_ref, o_ref, p_ref, factor_ref, kb, vb
):
    keys = k_ref.shape[0]

    @pl.when(pl.program_id(1) == 0)
    def _():
        for h in range(2):
            kb[h] = jnp.where(head_lanes(h, head_dim), k_ref[...], extra_ref[...])
            vb[h] = jnp.where(head_lanes(h, head_dim), v_ref[...], extra_ref[...])

    factor = scale * log2_e
    queries = q_ref[...]
    lane = lax.broadcasted_iota(jnp.int32, (1, lanes), 1)
    bias_lane = jnp.where(lane % head_dim == 0, 1.0, 0.0).astype(bf16)
    outs, factors = ([], [])
    for h in range(2):
        own = jnp.where(head_lanes(h, head_dim), queries, bias_lane)
        best, acc = (None, None)
        bests = []
        for first in range(0, keys, step):
            scores = dot(own, kb[h, first : first + step, :], 1, 1)
            high = jnp.max(scores, axis=1, keepdims=True)
            new_best = high if best is None else jnp.maximum(best, high)
            weights = jnp.exp2((scores - new_best) * factor).astype(bf16)
            p_ref[h, :, first : first + step] = weights
            part = dot(weights, vb[h, first : first + step, :], 1, 0)
            acc = part if best is None else acc * jnp.exp2((best - new_best) * factor) + part
            best = new_best
            bests.append(best)
        free = (1 - h) * head_dim + 1
        total = acc[:, free : free + 1]
        outs.append(acc / total)
        factors.append([jnp.exp2((high - best) * factor) / total for high in bests])
    o_ref[...] = jnp.where(head_lanes(0, head_dim), outs[0], outs[1]).astype(bf16)
    for s in range(keys // step):
        factor_ref[s] = jnp.where(head_lanes(0, head_dim), factors[0][s], factors[1][s])


def attend(queries, both, extra, head_dim):
    rows, width = queries.shape
    keys = both.shape[0]
    pairs = width // lanes
    row_step = min(512, rows)
    step = min(2048, keys)
    scale = head_dim ** (-0.5)
    return pl.pallas_call(
        functools.partial(attend_kernel, scale, head_dim, step),
        grid=(pairs, rows // row_step),
        in_specs=[
            pl.BlockSpec((row_step, lanes), lambda h, i: (i, h)),
            pl.BlockSpec((keys, lanes), lambda h, i: (0, h)),
            pl.BlockSpec((keys, lanes), lambda h, i: (0, h + pairs)),
            pl.BlockSpec((keys, lanes), lambda h, i: (0, 0)),
        ],
        out_specs=[
            pl.BlockSpec((row_step, lanes), lambda h, i: (i, h)),
            pl.BlockSpec((None, 2, row_step, keys), lambda h, i: (h, 0, i, 0)),
            pl.BlockSpec((None, keys // step, row_step, lanes), lambda h, i: (h, 0, i, 0)),
        ],
        out_shape=[
            jax.ShapeDtypeStruct((rows, width), bf16),
            jax.ShapeDtypeStruct((pairs, 2, rows, keys), bf16),
            jax.ShapeDtypeStruct((pairs, keys // step, rows, lanes), f32),
        ],
        scratch_shapes=[pltpu.VMEM((2, keys, lanes), bf16), pltpu.VMEM((2, keys, lanes), bf16)],
        compiler_params=pltpu.CompilerParams(vmem_limit_bytes=vmem_grant),
        cost_estimate=pl.CostEstimate(
            flops=4 * rows * keys * width * 4,
            bytes_accessed=keys * width * 4 + rows * width * 6 + 4 * pairs * rows * keys,
            transcendentals=rows * keys * width // head_dim,
        ),
        name="attend",
    )(queries, both, both, extra)


def attend_back_kernel(scale, head_dim, row_step, resumed, *refs):
    q_ref, da_ref, dax_ref, factor_ref, p_ref, k_ref, v_ref, extra_ref = refs[:8]
    start_ref = refs[8] if resumed else None
    dq_ref, dkv_ref, scaled, scaled_extra = refs[-4:]
    j = pl.program_id(1)
    rows = q_ref.shape[0]

    @pl.when(j == 0)
    def _():
        factors = factor_ref[...]
        scaled[...] = (da_ref[...].astype(f32) * factors).astype(bf16)
        turned = pltpu.roll(factors, head_dim, 1)
        scaled_extra[...] = (dax_ref[...].astype(f32) * turned).astype(bf16)

    keys, values, extra = (k_ref[...], v_ref[...], extra_ref[...])
    dk, dv = (None, None)
    for first in range(0, rows, row_step):
        part = slice(first, first + row_step)
        queries, grads, grads_extra = (q_ref[part, :], scaled[part, :], scaled_extra[part, :])
        none = jnp.zeros_like(queries)
        dq = None
        for h in range(2):
            sel = head_lanes(h, head_dim)
            weights = p_ref[h, part, :]
            grad_weights = dot(
                jnp.where(sel, grads, grads_extra), jnp.where(sel, values, extra), 1, 1
            )
            grad_scores = (weights.astype(f32) * grad_weights).astype(bf16)
            part_dv = dot(jnp.where(sel, grads, none), weights, 0, 0)
            part_dk = dot(jnp.where(sel, queries, none), grad_scores, 0, 0)
            part_dq = dot(grad_scores, jnp.where(sel, keys, jnp.zeros_like(keys)), 1, 0)
            dv = part_dv if dv is None else dv + part_dv
            dk = part_dk if dk is None else dk + part_dk
            dq = part_dq if dq is None else dq + part_dq
        dq = dq * scale

        @pl.when(j == 0)
        def _():
            dq_ref[part, :] = dq + start_ref[part, :] if resumed else dq

        @pl.when(j > 0)
        def _():
            dq_ref[part, :] += dq

    dkv_ref[0] = (dk * scale).astype(bf16)
    dkv_ref[1] = dv.astype(bf16)


def attend_back(
    queries, grads, deltas, saved, factors, both, extra, head_dim, first, count, start
):
    rows, width = queries.shape
    pairs = width // lanes
    row_step = min(512, rows)
    step = min(1024, count)
    skip = first // step
    group = first * factors.shape[1] // both.shape[0]
    scale = head_dim ** (-0.5)
    resumed = start is not None
    more = [pl.BlockSpec((rows, lanes), lambda h, j: (0, h))] if resumed else []
    return pl.pallas_call(
        functools.partial(attend_back_kernel, scale, head_dim, row_step, resumed),
        grid=(pairs, count // step),
        in_specs=[
            pl.BlockSpec((rows, lanes), lambda h, j: (0, h)),
            pl.BlockSpec((rows, lanes), lambda h, j: (0, h)),
            pl.BlockSpec((None, rows, lanes), lambda h, j: (h, 0, 0)),
            pl.BlockSpec((None, None, rows, lanes), lambda h, j: (h, group, 0, 0)),
            pl.BlockSpec((None, 2, rows, step), lambda h, j: (h, 0, 0, j + skip)),
            pl.BlockSpec((step, lanes), lambda h, j: (j + skip, h)),
            pl.BlockSpec((step, lanes), lambda h, j: (j + skip, h + pairs)),
            pl.BlockSpec((step, lanes), lambda h, j: (j + skip, 0)),
        ]
        + more,
        out_specs=[
            pl.BlockSpec((rows, lanes), lambda h, j: (0, h)),
            pl.BlockSpec((2, lanes, step), lambda h, j: (0, h, j)),
        ],
        out_shape=[
            jax.ShapeDtypeStruct((rows, width), f32),
            jax.ShapeDtypeStruct((2, width, count), bf16),
        ],
        scratch_shapes=[pltpu.VMEM((rows, lanes), bf16), pltpu.VMEM((rows, lanes), bf16)],
        compiler_params=pltpu.CompilerParams(vmem_limit_bytes=vmem_grant),
        cost_estimate=pl.CostEstimate(
            flops=8 * rows * count * width * 4,
            bytes_accessed=count * width * 8 + rows * width * 16 + 4 * pairs * rows * count,
            transcendentals=0,
        ),
        name="attend_back",
    )(
        queries,
        grads,
        deltas,
        factors,
        saved,
        both,
        both,
        extra,
        *([start] if resumed else []),
    )


def key_lanes(live, head_dim):
    lane = jnp.arange(lanes, dtype=jnp.int32) % head_dim
    bias = jnp.where(live, 0.0, masked_bias)[:, None]
    ones = jnp.where((lane >= 1) & (lane <= 3), 1.0, 0.0)[None, :]
    return jnp.where(lane[None, :] == 0, bias, ones).astype(bf16)


def opening_kernel(
    owners,
    ring,
    pieces,
    tokens_ref,
    weight_ref,
    packed_ref,
    x_ref,
    w_ref,
    vec_ref,
    q_ref,
    kv_ref,
    xs,
    ws,
    vec,
    qs,
    kvs,
    load_sem,
    store_sem,
    send_sem,
    recv_sem,
):
    row, here = (lax.axis_index("dp"), lax.axis_index("ctx"))
    core = lax.rem(here, 2)
    side = here // (ring // 2)
    own_ref = tokens_ref.at[side]
    block, width = tokens_ref.shape[1:]
    share = weight_ref.shape[0]
    half = share // 2
    mate, deep, far = ((row, here ^ 1), (row, here ^ 2), (row, here ^ (ring // 2)))
    owner_peers = [(row ^ k, here) for k in range(1, owners)]
    peers = [mate, deep, far] + owner_peers
    barrier = pltpu.get_barrier_semaphore()
    for peer in peers:
        pl.semaphore_signal(barrier, inc=1, device_id=peer, device_id_type=pl.DeviceIdType.MESH)
    own_load = pltpu.make_async_copy(own_ref, xs.at[0], load_sem.at[0])
    weight_load = pltpu.make_async_copy(weight_ref, ws.at[row], load_sem.at[1])
    vec_load = pltpu.make_async_copy(packed_ref, vec.at[row], load_sem.at[2])
    for load in (own_load, weight_load, vec_load):
        load.start()
    sent, stored = ([], [])
    count = [0]

    def send(source, target, peer):
        slot = count[0]
        count[0] += 1
        copy = pltpu.make_async_remote_copy(
            src_ref=source,
            dst_ref=target,
            send_sem=send_sem.at[slot],
            recv_sem=recv_sem.at[slot],
            device_id=peer,
            device_id_type=pl.DeviceIdType.MESH,
        )
        copy.start()
        sent.append(copy)
        return copy

    def store(source, target):
        copy = pltpu.make_async_copy(source, target, store_sem.at[len(stored)])
        copy.start()
        stored.append(copy)

    step = block // pieces
    parts = [pl.ds(j * step, step) for j in range(pieces)]
    pl.semaphore_wait(barrier, len(peers))
    weights = [
        send(weight_ref.at[pl.ds(core * half, half)], ws.at[row, pl.ds(core * half, half)], peer)
        for peer in owner_peers
    ]
    moved = [send(tokens_ref.at[1 - side, part], xs.at[1, part], far) for part in parts]
    own_deep = send(own_ref, xs.at[2], deep)
    own_mate = send(own_ref, xs.at[4], mate)
    vectors = [send(packed_ref, vec.at[row], peer) for peer in owner_peers]

    moved_deep, moved_mate = ([], [])
    weights_mate = []
    for j, part in enumerate(parts):
        moved[j].wait_recv()
        moved_deep.append(send(xs.at[1, part], xs.at[3, part], deep))
        moved_mate.append(send(xs.at[1, part], xs.at[5, part], mate))
        if j == pieces // 2:
            for k in range(1, owners):
                weights[k - 1].wait_recv()
                held = ws.at[row ^ k, pl.ds(core * half, half)]
                weights_mate.append(send(held, held, mate))
    own_deep.wait_recv()
    deep_mate = send(xs.at[2], xs.at[6], mate)
    for load in (own_load, weight_load, vec_load):
        load.wait()
    for copy in vectors + weights_mate:
        copy.wait_recv()
    for d in range(owners):
        store(ws.at[d], w_ref.at[d])
    store(vec, vec_ref)

    def bias(which):
        return jnp.concatenate(
            [vec[d, which : which + 1, :] for d in range(owners)], axis=1
        ).astype(f32)

    value_bias = bias(1)
    none = jnp.zeros_like(value_bias)

    def product(place, first, last):
        total = None
        for d in range(owners):
            left = xs[place, :, d * share : (d + 1) * share]
            part = dot(left, ws[d, :, first:last], 1, 0)
            total = part if total is None else total + part
        return total

    def project(place):
        store(xs.at[place], x_ref.at[place])
        if place < 2:
            qs[place] = (product(place, 0, width) + bias(0)).astype(bf16)
            store(qs.at[place], q_ref.at[place])
        kvs[place, :, :width] = product(place, width, 2 * width).astype(bf16)
        kvs[place, :, width:] = (product(place, 2 * width, 3 * width) + value_bias).astype(bf16)
        store(kvs.at[place], kv_ref.at[place])

    project(0)
    own_mate.wait_recv()
    project(4)
    project(1)
    for copy in moved_mate:
        copy.wait_recv()
    project(5)
    project(2)
    deep_mate.wait_recv()
    project(6)
    far_mate = []
    for j, part in enumerate(parts):
        moved_deep[j].wait_recv()
        far_mate.append(send(xs.at[3, part], xs.at[7, part], mate))
    project(3)
    for copy in far_mate:
        copy.wait_recv()
    project(7)
    for copy in sent:
        copy.wait_send()
    for copy in stored:
        copy.wait()


def opening(tokens, weight, packed, owners, ring):
    block, width = tokens.shape[1:]
    blocks = ring
    pieces = 4
    any_space = pl.BlockSpec(memory_space=pl.ANY)
    copies = 2 * (owners - 1) + 3 * pieces + 3 + (owners - 1) + pieces
    shapes = [
        jax.ShapeDtypeStruct((blocks, block, width), bf16),
        jax.ShapeDtypeStruct((owners,) + weight.shape, bf16),
        jax.ShapeDtypeStruct((owners,) + packed.shape, bf16),
        jax.ShapeDtypeStruct((2, block, width), bf16),
        jax.ShapeDtypeStruct((blocks, block, 2 * width), bf16),
    ]
    return pl.pallas_call(
        functools.partial(opening_kernel, owners, ring, pieces),
        in_specs=[any_space] * 3,
        out_specs=[any_space] * 5,
        out_shape=shapes,
        scratch_shapes=[pltpu.VMEM(v.shape, v.dtype) for v in shapes]
        + [
            pltpu.SemaphoreType.DMA((3,)),
            pltpu.SemaphoreType.DMA((owners + 1 + 2 * blocks + 2,)),
            pltpu.SemaphoreType.DMA((copies,)),
            pltpu.SemaphoreType.DMA((copies,)),
        ],
        compiler_params=pltpu.CompilerParams(
            vmem_limit_bytes=vmem_grant, collective_id=1, has_side_effects=True
        ),
        cost_estimate=pl.CostEstimate(
            flops=8 * blocks * block * width * width, bytes_accessed=200 << 20, transcendentals=0
        ),
        name="opening",
    )(tokens, weight, packed)


def middle_kernel(
    head_dim,
    chunk,
    mixed_ref,
    x_ref,
    cot_ref,
    live_ref,
    out_ref,
    up_ref,
    down_ref,
    vec_ref,
    up_bias_ref,
    y_ref,
    active_ref,
    hidden_ref,
    dbranch_ref,
    dupper_ref,
    dz_ref,
    dattn_ref,
    dmixed_ref,
    delta_ref,
    sums_ref,
    up_sum_ref,
    slope,
):
    width = x_ref.shape[1]
    inner = up_ref.shape[1]
    out_bias, gain_first, shift_first = (vec_ref[0:1, :], vec_ref[1:2, :], vec_ref[2:3, :])
    down_bias, gain_second, shift_second = (vec_ref[3:4, :], vec_ref[4:5, :], vec_ref[5:6, :])
    live = live_ref[...]
    mixed = mixed_ref[...]
    attn = dot(mixed, out_ref[...], 1, 0) + out_bias
    hidden, unit_first, inverse_first = norm_parts(
        x_ref[...].astype(f32) + attn, gain_first, shift_first
    )
    hidden_low = hidden.astype(bf16)
    hidden_ref[...] = hidden_low
    branch = down_bias
    for first in range(0, inner, chunk):
        part = slice(first, first + chunk)
        upper = dot(hidden_low, up_ref[:, part], 1, 0) + up_bias_ref[:, part]
        below = 0.5 + 0.5 * lax.erf(upper * (0.5**0.5))
        active = (upper * below).astype(bf16)
        bell = jnp.exp2(upper * upper * (-0.5 * log2_e)) * 0.3989422804014327
        slope[:, part] = (below + upper * bell).astype(bf16)
        active_ref[:, part] = active
        branch = branch + dot(active, down_ref[part, :], 1, 0)
    normed, unit_second, inverse_second = norm_parts(hidden + branch, gain_second, shift_second)
    result = normed * live
    y_ref[...] = result.astype(bf16)
    grad_out = cot_ref[...].astype(f32) * live
    grad_second = norm_back(grad_out * gain_second, unit_second, inverse_second)
    grad_branch = grad_second.astype(bf16)
    dbranch_ref[...] = grad_branch
    grad_hidden = grad_second
    up_sums = []
    for first in range(0, inner, chunk):
        part = slice(first, first + chunk)
        grad_active = dot(grad_branch, down_ref[part, :], 1, 1)
        grad_upper = (grad_active * slope[:, part].astype(f32)).astype(bf16)
        dupper_ref[:, part] = grad_upper
        up_sums.append(jnp.sum(grad_upper.astype(f32), axis=0, keepdims=True))
        grad_hidden = grad_hidden + dot(grad_upper, up_ref[:, part], 1, 1)
    grad_first = norm_back(grad_hidden * gain_first, unit_first, inverse_first)
    dz_ref[...] = grad_first
    grad_attn = grad_first.astype(bf16)
    dattn_ref[...] = grad_attn
    grad_mixed = dot(grad_attn, out_ref[...], 1, 1).astype(bf16)
    dmixed_ref[...] = grad_mixed
    cross = grad_mixed.astype(f32) * mixed.astype(f32)
    lane = lax.broadcasted_iota(jnp.int32, (1, lanes), 1)
    lower = lane < head_dim
    for p in range(width // lanes):
        pair = cross[:, p * lanes : (p + 1) * lanes]
        first_head = jnp.sum(jnp.where(lower, pair, 0.0), axis=1, keepdims=True)
        second_head = jnp.sum(jnp.where(lower, 0.0, pair), axis=1, keepdims=True)
        delta_ref[p] = spread_lanes(first_head, second_head, 0.0, head_dim)
    sums = [
        grad_attn.astype(f32),
        grad_hidden * unit_first,
        grad_hidden,
        grad_branch.astype(f32),
        grad_out * unit_second,
        grad_out,
        result * result,
        attn * attn * live,
        branch * branch * live,
    ]
    first_step = pl.program_id(0) == 0

    @pl.when(first_step)
    def _():
        sums_ref[...] = jnp.zeros_like(sums_ref)
        up_sum_ref[...] = jnp.zeros_like(up_sum_ref)

    for i, value in enumerate(sums):
        sums_ref[i : i + 1, :] += jnp.sum(value, axis=0, keepdims=True)
    up_sum_ref[0:1, :] += jnp.concatenate(up_sums, axis=1)


def middle(mixed, stream, cot, live, out_all, up_all, down_all, vectors, up_bias, head_dim):
    count, width = mixed.shape
    inner = up_all.shape[1]
    pairs = width // lanes
    row_step = min(256, count)
    chunk = min(768, inner)

    def fixed(shape):
        return pl.BlockSpec(shape, lambda i: (0, 0), pipeline_mode=pl.Buffered(1))

    def block(columns):
        return pl.BlockSpec((row_step, columns), lambda i: (i, 0))

    return pl.pallas_call(
        functools.partial(middle_kernel, head_dim, chunk),
        grid=(count // row_step,),
        in_specs=[
            block(width),
            block(width),
            block(width),
            block(1),
            fixed((width, width)),
            fixed((width, inner)),
            fixed((inner, width)),
            fixed(vectors.shape),
            fixed(up_bias.shape),
        ],
        out_specs=[
            block(width),
            block(inner),
            block(width),
            block(width),
            block(inner),
            block(width),
            block(width),
            block(width),
            pl.BlockSpec((pairs, row_step, lanes), lambda i: (0, i, 0)),
            pl.BlockSpec((16, width), lambda i: (0, 0)),
            pl.BlockSpec((8, inner), lambda i: (0, 0)),
        ],
        out_shape=[
            jax.ShapeDtypeStruct((count, width), bf16),
            jax.ShapeDtypeStruct((count, inner), bf16),
            jax.ShapeDtypeStruct((count, width), bf16),
            jax.ShapeDtypeStruct((count, width), bf16),
            jax.ShapeDtypeStruct((count, inner), bf16),
            jax.ShapeDtypeStruct((count, width), f32),
            jax.ShapeDtypeStruct((count, width), bf16),
            jax.ShapeDtypeStruct((count, width), bf16),
            jax.ShapeDtypeStruct((pairs, count, lanes), bf16),
            jax.ShapeDtypeStruct((16, width), f32),
            jax.ShapeDtypeStruct((8, inner), f32),
        ],
        scratch_shapes=[pltpu.VMEM((row_step, inner), bf16)],
        compiler_params=pltpu.CompilerParams(vmem_limit_bytes=vmem_grant),
        cost_estimate=pl.CostEstimate(
            flops=4 * count * width * (2 * inner + width),
            bytes_accessed=4 * width * inner + count * (18 * width + 4 * inner),
            transcendentals=4 * count * inner,
        ),
        name="middle",
    )(mixed, stream, cot, live, out_all, up_all, down_all, vectors, up_bias)


def up_out_kernel(blocks, hidden_ref, dupper_ref, mixed_ref, dattn_ref, o_ref):
    s = pl.program_id(0)

    @pl.when(s < blocks)
    def _():
        o_ref[...] = dot(hidden_ref[...], dupper_ref[...], 0, 0).astype(bf16).reshape(o_ref.shape)

    @pl.when(s == blocks)
    def _():
        o_ref[...] = dot(mixed_ref[...], dattn_ref[...], 0, 0).astype(bf16).reshape(o_ref.shape)


def down_kernel(active_ref, dbranch_ref, held_ref, o_ref):
    del held_ref
    o_ref[...] = dot(active_ref[...], dbranch_ref[...], 0, 0).astype(bf16).reshape(o_ref.shape)


def middle_grads(hidden, dupper, mixed, dattn, active, dbranch, owners, ring):
    count, width = hidden.shape
    inner = dupper.shape[1]
    devices = owners * ring
    share = width // devices
    blocks = inner // width
    tall = inner // devices
    piece = blocks * share + tall + share
    shape = jax.ShapeDtypeStruct((devices, piece, width), bf16)
    params = pltpu.CompilerParams(vmem_limit_bytes=vmem_grant)
    whole = pl.BlockSpec((count, width), lambda s: (0, 0))
    held = pl.pallas_call(
        functools.partial(up_out_kernel, blocks),
        grid=(blocks + 1,),
        in_specs=[
            whole,
            pl.BlockSpec((count, width), lambda s: (0, jnp.minimum(s, blocks - 1))),
            whole,
            whole,
        ],
        out_specs=pl.BlockSpec(
            (devices, share, width),
            lambda s: (0, jnp.where(s < blocks, s, piece // share - 1), 0),
        ),
        out_shape=shape,
        compiler_params=params,
        cost_estimate=pl.CostEstimate(
            flops=2 * count * width * (inner + width),
            bytes_accessed=2 * (count + width) * (inner + 3 * width),
            transcendentals=0,
        ),
        name="up_grads",
    )(hidden, dupper, mixed, dattn)
    return pl.pallas_call(
        down_kernel,
        grid=(owners,),
        in_specs=[
            pl.BlockSpec((count, inner // owners), lambda s: (0, s)),
            whole,
            pl.BlockSpec(memory_space=pl.ANY),
        ],
        out_specs=pl.BlockSpec((ring, tall, width), lambda s: (s, blocks * share // tall, 0)),
        out_shape=shape,
        input_output_aliases={2: 0},
        compiler_params=params,
        cost_estimate=pl.CostEstimate(
            flops=2 * count * width * inner,
            bytes_accessed=2 * (count + width) * (inner + width),
            transcendentals=0,
        ),
        name="down_grads",
    )(active, dbranch, held)


def closing_kernel(owners, ring, firsts, dq_ref, x_ref, *refs):
    shares = refs[: len(firsts)]
    small_ref, home_ref, out_ref, small_out_ref, home_out_ref = refs[len(firsts) : len(firsts) + 5]
    (
        xs,
        dq,
        dkv,
        whole,
        parts,
        in_core,
        by_owner,
        in_owner,
        by_piece,
        in_piece,
        done,
        in_done,
        small,
        small_core,
        small_owner,
        small_piece,
        load_sem,
        send_sem,
        recv_sem,
    ) = refs[len(firsts) + 5 :]
    row, here = (lax.axis_index("dp"), lax.axis_index("ctx"))
    core, depth = (lax.rem(here, 2), here // 2)
    deep = ring // 2
    count = dq.shape[0]
    loads = [
        pltpu.make_async_copy(dq_ref, dq, load_sem.at[0]),
        pltpu.make_async_copy(x_ref, xs, load_sem.at[1]),
    ]
    for i, first in enumerate(firsts):
        columns = pl.ds(first, shares[i].shape[2])
        loads.append(pltpu.make_async_copy(shares[i], dkv.at[:, :, columns], load_sem.at[2 + i]))
    for load in loads:
        load.start()

    mate = (row, here ^ 1)
    owner_peers = [(row ^ k, here) for k in range(1, owners)]
    depth_peers = [(row, here ^ (2 * k)) for k in range(1, deep)]
    barrier = pltpu.get_barrier_semaphore()
    peers = [mate] + owner_peers + depth_peers
    for peer in peers:
        pl.semaphore_signal(barrier, inc=1, device_id=peer, device_id_type=pl.DeviceIdType.MESH)

    sent = []

    def send(source, target, peer, m, slot):
        copy = pltpu.make_async_remote_copy(
            src_ref=source,
            dst_ref=target,
            send_sem=send_sem.at[m, slot],
            recv_sem=recv_sem.at[m, slot],
            device_id=peer,
            device_id_type=pl.DeviceIdType.MESH,
        )
        copy.start()
        sent.append(copy)
        return copy

    at_owner = 1
    at_piece = owners
    at_done = at_piece + deep - 1
    at_back = at_done + deep - 1
    tile = 256

    def to_core(m):
        def one(t, carry):
            columns = pl.ds(pl.multiple_of(t * tile, tile), tile)
            if m == 0:
                whole[columns, :] = dot(xs[0:count, columns], dq[...].astype(bf16), 0, 0)
            else:
                whole[columns, :] = dot(xs[:, columns], dkv[m - 1], 0, 1)
            return carry

        lax.fori_loop(0, whole.shape[0] // tile, one, 0)
        parts[m] = whole[...].reshape(parts.shape[1:]).astype(bf16)
        return [send(parts.at[m, :, 1 - core], in_core.at[m], mate, m, 0)]

    def to_owner(m):
        mine = parts[m, :, core].astype(f32)
        by_owner[m] = (mine + in_core[m].astype(f32)).astype(bf16)
        return [
            send(by_owner.at[m, row ^ k], in_owner.at[m, k - 1], owner_peers[k - 1], m, at_owner + k - 1)
            for k in range(1, owners)
        ]

    def to_piece(m):
        total = by_owner[m, row].astype(f32)
        for k in range(1, owners):
            total = total + in_owner[m, k - 1].astype(f32)
        by_piece[m] = total.reshape(by_piece.shape[1:]).astype(bf16)
        return [
            send(
                by_piece.at[m, depth ^ k],
                in_piece.at[m, k - 1],
                depth_peers[k - 1],
                m,
                at_piece + k - 1,
            )
            for k in range(1, deep)
        ]

    def to_done(m):
        total = by_piece[m, depth].astype(f32)
        for k in range(1, deep):
            total = total + in_piece[m, k - 1].astype(f32)
        done[m, depth] = total.astype(bf16)
        return [
            send(done.at[m, depth], done.at[m, depth], depth_peers[k - 1], m, at_done + k - 1)
            for k in range(1, deep)
        ]

    def to_back(m):
        return [send(done.at[m], in_done.at[m], mate, m, at_back)]

    def finish(m):
        size = out_ref.shape[1]
        columns = slice(m * whole.shape[1], (m + 1) * whole.shape[1])
        out_ref[core, :, columns] = done[m].astype(f32).reshape(size, whole.shape[1])
        out_ref[1 - core, :, columns] = in_done[m].astype(f32).reshape(size, whole.shape[1])
        return []

    stages = [to_core, to_owner, to_piece, to_done, to_back, finish]
    waiting = [[], [], []]
    loads[0].wait()
    loads[1].wait()
    pl.semaphore_wait(barrier, len(peers))
    home = send(home_ref, home_out_ref, (row, here ^ (ring // 2)), 3, at_back)
    small_waits = []
    for step in range(len(stages) + 2):
        for m in range(3):
            stage = step - m
            if 0 <= stage < len(stages):
                for copy in waiting[m]:
                    copy.wait_recv()
                waiting[m] = stages[stage](m)
        if step == 0:
            small[...] = small_ref[...]
            small[0:1, :] = jnp.sum(dq[...].astype(bf16).astype(f32), axis=0, keepdims=True)
            for load in loads[2:]:
                load.wait()
            ones = jnp.ones((8, dkv.shape[2]), bf16)
            small[1:2, :] = dot(ones, dkv[1], 1, 1)[0:1, :]
            small_waits = [send(small, small_core, mate, 3, 0)]
        if step == 1:
            small_waits[0].wait_recv()
            small_owner[0] = small[...] + small_core[...]
            small_waits = [
                send(small_owner.at[0], small_owner.at[k], owner_peers[k - 1], 3, k)
                for k in range(1, owners)
            ]
        if step == 3:
            total = small_owner[0]
            for k in range(1, owners):
                small_waits[k - 1].wait_recv()
                total = total + small_owner[k]
            small_piece[0] = total
            small_waits = [
                send(small_piece.at[0], small_piece.at[k], depth_peers[k - 1], 3, at_piece + k - 1)
                for k in range(1, deep)
            ]
        if step == 5:
            total = small_piece[0]
            for k in range(1, deep):
                small_waits[k - 1].wait_recv()
                total = total + small_piece[k]
            small_out_ref[...] = total
    home.wait_recv()
    for copy in sent:
        copy.wait_send()


def closing(dq, stream, shares, small, home, owners, ring):
    count, width = dq.shape
    keys = stream.shape[0]
    firsts = tuple(first for first, _ in shares)
    shares = [v for _, v in shares]
    deep = ring // 2
    half = width // owners // 2
    piece = half // deep
    slots = 1 + (owners - 1) + 2 * (deep - 1) + 1
    any_space = pl.BlockSpec(memory_space=pl.ANY)
    in_vmem = pl.BlockSpec(memory_space=pltpu.VMEM)
    return pl.pallas_call(
        functools.partial(closing_kernel, owners, ring, firsts),
        in_specs=[any_space] * (2 + len(shares)) + [in_vmem, any_space],
        out_specs=[in_vmem, in_vmem, any_space],
        out_shape=[
            jax.ShapeDtypeStruct((2, half, 3 * width), f32),
            jax.ShapeDtypeStruct(small.shape, f32),
            jax.ShapeDtypeStruct(home.shape, home.dtype),
        ],
        scratch_shapes=[
            pltpu.VMEM((keys, width), bf16),
            pltpu.VMEM((count, width), f32),
            pltpu.VMEM((2, width, keys), bf16),
            pltpu.VMEM((width, width), f32),
            pltpu.VMEM((3, owners, 2, half, width), bf16),
            pltpu.VMEM((3, owners, half, width), bf16),
            pltpu.VMEM((3, owners, half, width), bf16),
            pltpu.VMEM((3, owners - 1, half, width), bf16),
            pltpu.VMEM((3, deep, piece, width), bf16),
            pltpu.VMEM((3, deep - 1, piece, width), bf16),
            pltpu.VMEM((3, deep, piece, width), bf16),
            pltpu.VMEM((3, deep, piece, width), bf16),
            pltpu.VMEM(small.shape, f32),
            pltpu.VMEM(small.shape, f32),
            pltpu.VMEM((owners,) + small.shape, f32),
            pltpu.VMEM((deep,) + small.shape, f32),
            pltpu.SemaphoreType.DMA((2 + len(shares),)),
            pltpu.SemaphoreType.DMA((4, slots)),
            pltpu.SemaphoreType.DMA((4, slots)),
        ],
        compiler_params=pltpu.CompilerParams(
            vmem_limit_bytes=vmem_grant, collective_id=0, has_side_effects=True
        ),
        cost_estimate=pl.CostEstimate(
            flops=20 * keys * width * width, bytes_accessed=100 << 20, transcendentals=0
        ),
        name="closing",
    )(dq, stream, *shares, small, home)


def shards(
    ring,
    tokens,
    cotangent,
    lengths,
    block_order,
    qkv_weight,
    query_bias,
    value_bias,
    out_weight,
    out_bias,
    attn_gain,
    attn_shift,
    up_weight,
    up_bias,
    down_weight,
    down_bias,
    ffn_gain,
    ffn_shift,
):
    seqs, block, width = tokens.shape
    head_dim = width // HEADS
    assert seqs == 2 and ring % 4 == 0
    half = ring // 2
    here = lax.axis_index("ctx")
    side = here // half

    def pick(array, index):
        return lax.dynamic_index_in_dim(array, index, 0, keepdims=False)

    def exchange(array, bit):
        return lax.ppermute(array, "ctx", [(i, i ^ bit) for i in range(ring)])

    def arrange(kept, other):
        first = jnp.where(side == 0, kept, other)
        second = jnp.where(side == 0, other, kept)
        return jnp.stack([first, second])

    def gather(array):
        return lax.all_gather(array, "dp", axis=0, tiled=True)

    bits = []
    bit = half // 2
    while bit:
        bits.append(bit)
        bit //= 2
    ids = jnp.stack([here, here ^ half])
    for bit in bits:
        ids = jnp.concatenate([ids, ids ^ bit])
    count_rows = 2 * block

    order = pick(block_order, side)
    length = pick(lengths, side)
    table = jnp.arange(ring, dtype=jnp.int32)
    place_of = jnp.sum(jnp.where(ids[:, None] == table[None, :], order[None, :], 0), axis=1)
    places = place_of[:, None] * block + jnp.arange(block, dtype=jnp.int32)[None, :]
    live_keys = (places < length).reshape(-1)
    live_rows = live_keys[:count_rows, None].astype(f32)
    extra = key_lanes(live_keys, head_dim)

    row = lax.axis_index("dp")
    owners = lax.axis_size("dp")
    devices = owners * ring
    inner = up_weight.shape[1]
    share = query_bias.shape[0]
    laid = ring == 8 and width % (8 * devices) == 0 and inner % width == 0 and block % 32 == 0
    singles = [
        query_bias,
        value_bias,
        out_bias,
        attn_gain,
        attn_shift,
        down_bias,
        ffn_gain,
        ffn_shift,
    ]
    packed = jnp.concatenate([jnp.stack(singles), up_bias.reshape(-1, share)], axis=0)
    if laid:
        stream, qkv_all, vectors, queries, both = opening(
            tokens, qkv_weight, packed, owners, ring
        )
        stream = stream.reshape(-1, width)
        qkv_all = qkv_all.reshape(width, -1)
        vectors = vectors.astype(f32)
        queries = queries.reshape(-1, width)
        both = both.reshape(-1, 2 * width)
    else:
        qkv_all = gather(qkv_weight)
        vectors = gather(packed[None]).astype(f32)
        other = exchange(pick(tokens, 1 - side), half)
        stream = jnp.concatenate([pick(tokens, side), other], axis=0)
        for bit in bits:
            stream = jnp.concatenate([stream, exchange(stream, bit)], axis=0)
    rows = stream[:count_rows]
    bias = [vectors[:, i].reshape(1, width) for i in range(8)]
    up_bias_all = vectors[:, 8:].reshape(1, -1)
    if not laid:
        queries = (
            jnp.dot(rows, qkv_all[:, :width], preferred_element_type=f32) + bias[0]
        ).astype(bf16)
        kv_bias = jnp.concatenate([jnp.zeros_like(bias[1]), bias[1]], axis=1)
        both = jnp.dot(stream, qkv_all[:, width:], preferred_element_type=f32) + kv_bias
        both = both.astype(bf16)
    out_all = gather(out_weight)
    up_all = gather(up_weight)
    down_all = gather(down_weight)
    held, _ = lax.optimization_barrier((cotangent, stream))
    cot = jnp.concatenate([pick(held, side), exchange(pick(held, 1 - side), half)], axis=0)

    mixed, saved, factors = attend(queries, both, extra, head_dim)
    (
        result,
        active,
        hidden,
        grad_branch,
        grad_upper,
        grad_first,
        grad_attn,
        grad_mixed,
        deltas,
        sums,
        up_sum,
    ) = middle(
        mixed,
        stream,
        cot,
        live_rows,
        out_all,
        up_all,
        down_all,
        jnp.concatenate(bias[2:] + [jnp.zeros((2, width), f32)], axis=0),
        up_bias_all,
        head_dim,
    )
    output = arrange(result[:block], exchange(result[block:], half))

    def scatter(grad):
        return lax.psum_scatter(grad, ("dp", "ctx"), scatter_dimension=0, tiled=True)

    def spread(parts):
        return jax.tree.map(lambda v: lax.all_gather(v, "ctx", axis=0, tiled=True), parts)

    if laid:
        scattered = scatter(
            middle_grads(hidden, grad_upper, mixed, grad_attn, active, grad_branch, owners, ring)
        )
    else:
        grads = (dot(hidden, grad_upper, 0, 0), dot(active, grad_branch, 0, 0), dot(mixed, grad_attn, 0, 0))
        scattered = tuple(scatter(grad.astype(bf16)) for grad in grads)
    gathered = []

    kv_weight = qkv_all[:, width:]
    size = 2 * block
    grad_queries = None
    shares = []

    def reduced(place, level):
        nonlocal grad_queries
        if level == len(bits):
            first = place * size
            if place == 0:
                held, grad_queries = lax.optimization_barrier((scattered, grad_queries))
                gathered.append(spread(held))
            grad_queries, grad_both = attend_back(
                queries,
                grad_mixed,
                deltas,
                saved,
                factors,
                both,
                extra,
                head_dim,
                first,
                size,
                grad_queries,
            )
            shares.append((first, grad_both))
            return dot(grad_both.reshape(2 * width, size), kv_weight, 0, 1)
        low = reduced(place + (1 << level), level + 1).astype(bf16)
        low, grad_queries = lax.optimization_barrier((low, grad_queries))
        other = exchange(low, bits[level])
        return reduced(place, level + 1) + other.astype(f32)

    grad_stream = reduced(0, 0)
    grad_query_low = grad_queries.astype(bf16)
    grad_rows = grad_first + dot(grad_query_low, qkv_all[:, :width], 1, 1) + grad_stream
    grad_rows_low = grad_rows.astype(bf16)
    grad_rows_low, grad_queries, pieces = lax.optimization_barrier(
        (grad_rows_low, grad_queries, gathered[0])
    )
    if laid:
        pieces = pieces.astype(f32)
        each, tall = (width // devices, inner // devices)
        blocks = inner // width
        cut = blocks * each
        grad_up_weight = jnp.concatenate(
            [pieces[:, i * each : (i + 1) * each, :].reshape(share, width) for i in range(blocks)],
            axis=1,
        )
        grad_down_weight = pieces[:, cut : cut + tall, :].reshape(-1, width)
        grad_out_weight = pieces[:, cut + tall :, :].reshape(share, width)
    else:
        grad_up_weight, grad_down_weight, grad_out_weight = (v.astype(f32) for v in pieces)

    squares = jnp.sum(sums[6:9], axis=1)
    lane = jnp.arange(width)
    mine = (lane // 3) == (row * 2 + side)
    squares = jnp.where(
        lane % 3 == 0, squares[0], jnp.where(lane % 3 == 1, squares[1], squares[2])
    )
    squares = jnp.where(mine, squares, 0.0)[None, :]
    small = jnp.concatenate(
        [jnp.zeros((2, width), f32), sums[:6], squares, up_sum[0].reshape(-1, width)], axis=0
    )
    small = jnp.pad(small, ((0, -small.shape[0] % 8), (0, 0)))
    if laid:
        grad_qkv_weight, summed, other = closing(
            grad_queries, stream, shares, small, grad_rows_low[block:], owners, ring
        )
        grad_qkv_weight = grad_qkv_weight.reshape(share, 3 * width)
    else:
        other = exchange(grad_rows_low[block:], half)
        kv_parts = []
        for which in range(2):
            part = 0.0
            for first, v in shares:
                part = part + dot(stream[first : first + size], v[which], 0, 1)
            kv_parts.append(part)
        grad_qkv_weight = jnp.concatenate([dot(rows, grad_query_low, 0, 0)] + kv_parts, axis=1)
        grad_qkv_weight = spread(scatter(grad_qkv_weight.astype(bf16))).astype(f32)
        grad_query_bias = jnp.sum(grad_query_low, axis=0, dtype=f32)
        grad_value_bias = sum(jnp.sum(v[1], axis=1, dtype=f32) for _, v in shares)
        small = jnp.concatenate([grad_query_bias[None], grad_value_bias[None], small[2:]], axis=0)
        summed = lax.psum(small, ("dp", "ctx"))

    grad_tokens = arrange(grad_rows_low[:block], other)
    totals = [lax.dynamic_slice_in_dim(summed[i], row * share, share) for i in range(8)]
    tall = inner // owners
    up_total = lax.dynamic_slice_in_dim(summed[9:].reshape(-1), row * tall, tall)
    seq_squares = lax.dynamic_slice_in_dim(summed[8], row * 6, 6).reshape(2, 3)
    branch_rms = jnp.sqrt(seq_squares / (lengths.astype(f32)[:, None] * width) + rms_eps)
    return (
        output,
        grad_tokens,
        grad_qkv_weight,
        totals[0],
        totals[1],
        grad_out_weight,
        totals[2],
        totals[3],
        totals[4],
        grad_up_weight,
        up_total,
        grad_down_weight,
        totals[5],
        totals[6],
        totals[7],
        branch_rms,
    )


def solution(mesh):
    in_specs = (
        P("dp", "ctx", None),
        P("dp", "ctx", None),
        P("dp"),
        P("dp", None),
        P("dp", None),
        P("dp"),
        P("dp"),
        P("dp", None),
        P("dp"),
        P("dp"),
        P("dp"),
        P("dp", None),
        P("dp"),
        P("dp", None),
        P("dp"),
        P("dp"),
        P("dp"),
    )
    out_specs = (
        P("dp", "ctx", None),
        P("dp", "ctx", None),
        P("dp", None),
        P("dp"),
        P("dp"),
        P("dp", None),
        P("dp"),
        P("dp"),
        P("dp"),
        P("dp", None),
        P("dp"),
        P("dp", None),
        P("dp"),
        P("dp"),
        P("dp"),
        P("dp", None),
    )
    return jax.shard_map(
        functools.partial(shards, mesh.shape["ctx"]),
        mesh=mesh,
        in_specs=in_specs,
        out_specs=out_specs,
        check_vma=False,
    )
```

```python
import functools

import jax
import jax.numpy as jnp
from jax import lax
from jax.experimental import pallas as pl
from jax.experimental.pallas import tpu as pltpu
from jax.sharding import PartitionSpec as P

HEADS = 12

norm_eps = 1e-12
rms_eps = 1e-06
masked_bias = -1e30
log2_e = 1.4426950408889634
lanes = 128
vmem_grant = 56 << 20
f32 = jnp.float32
bf16 = jnp.bfloat16


def norm_parts(total, gain, shift):
    mean = jnp.mean(total, axis=-1, keepdims=True)
    centred = total - mean
    inverse = lax.rsqrt(jnp.mean(centred * centred, axis=-1, keepdims=True) + norm_eps)
    unit = centred * inverse
    return (unit * gain + shift, unit, inverse)


def norm_back(grad_unit, unit, inverse):
    mean_grad = jnp.mean(grad_unit, axis=-1, keepdims=True)
    mean_cross = jnp.mean(grad_unit * unit, axis=-1, keepdims=True)
    return inverse * (grad_unit - mean_grad - unit * mean_cross)


def dot(left, right, left_dim, right_dim):
    return lax.dot_general(
        left, right, (((left_dim,), (right_dim,)), ((), ())), preferred_element_type=f32
    )


def head_lanes(head, head_dim):
    lane = lax.broadcasted_iota(jnp.int32, (1, lanes), 1)
    return (lane // head_dim) == head


def spread_lanes(first_head, second_head, unit, head_dim):
    rows = first_head.shape[0]
    lane = lax.broadcasted_iota(jnp.int32, (rows, lanes), 1)
    place = lane % head_dim
    value = -jnp.where(lane < head_dim, second_head, first_head)
    high = value.astype(bf16).astype(f32)
    rest = value - high
    mid = rest.astype(bf16).astype(f32)
    low = rest - mid
    out = jnp.where(place == 1, high, jnp.where(place == 2, mid, jnp.where(place == 3, low, 0.0)))
    return jnp.where(place == 0, unit, out).astype(bf16)


def attend_kernel(
    scale, head_dim, step, q_ref, k_ref, v_ref, extra_ref, o_ref, p_ref, factor_ref, kb, vb
):
    keys = k_ref.shape[0]

    @pl.when(pl.program_id(1) == 0)
    def _():
        for h in range(2):
            kb[h] = jnp.where(head_lanes(h, head_dim), k_ref[...], extra_ref[...])
            vb[h] = jnp.where(head_lanes(h, head_dim), v_ref[...], extra_ref[...])

    factor = scale * log2_e
    queries = q_ref[...]
    lane = lax.broadcasted_iota(jnp.int32, (1, lanes), 1)
    bias_lane = jnp.where(lane % head_dim == 0, 1.0, 0.0).astype(bf16)
    outs, factors = ([], [])
    for h in range(2):
        own = jnp.where(head_lanes(h, head_dim), queries, bias_lane)
        best, acc = (None, None)
        bests = []
        for first in range(0, keys, step):
            scores = dot(own, kb[h, first : first + step, :], 1, 1)
            high = jnp.max(scores, axis=1, keepdims=True)
            new_best = high if best is None else jnp.maximum(best, high)
            weights = jnp.exp2((scores - new_best) * factor).astype(bf16)
            p_ref[h, :, first : first + step] = weights
            part = dot(weights, vb[h, first : first + step, :], 1, 0)
            acc = part if best is None else acc * jnp.exp2((best - new_best) * factor) + part
            best = new_best
            bests.append(best)
        free = (1 - h) * head_dim + 1
        total = acc[:, free : free + 1]
        outs.append(acc / total)
        factors.append([jnp.exp2((high - best) * factor) / total for high in bests])
    o_ref[...] = jnp.where(head_lanes(0, head_dim), outs[0], outs[1]).astype(bf16)
    for s in range(keys // step):
        factor_ref[s] = jnp.where(head_lanes(0, head_dim), factors[0][s], factors[1][s])


def attend(queries, both, extra, head_dim):
    rows, width = queries.shape
    keys = both.shape[0]
    pairs = width // lanes
    row_step = min(512, rows)
    step = min(2048, keys)
    scale = head_dim ** (-0.5)
    return pl.pallas_call(
        functools.partial(attend_kernel, scale, head_dim, step),
        grid=(pairs, rows // row_step),
        in_specs=[
            pl.BlockSpec((row_step, lanes), lambda h, i: (i, h)),
            pl.BlockSpec((keys, lanes), lambda h, i: (0, h)),
            pl.BlockSpec((keys, lanes), lambda h, i: (0, h + pairs)),
            pl.BlockSpec((keys, lanes), lambda h, i: (0, 0)),
        ],
        out_specs=[
            pl.BlockSpec((row_step, lanes), lambda h, i: (i, h)),
            pl.BlockSpec((None, 2, row_step, keys), lambda h, i: (h, 0, i, 0)),
            pl.BlockSpec((None, keys // step, row_step, lanes), lambda h, i: (h, 0, i, 0)),
        ],
        out_shape=[
            jax.ShapeDtypeStruct((rows, width), bf16),
            jax.ShapeDtypeStruct((pairs, 2, rows, keys), bf16),
            jax.ShapeDtypeStruct((pairs, keys // step, rows, lanes), f32),
        ],
        scratch_shapes=[pltpu.VMEM((2, keys, lanes), bf16), pltpu.VMEM((2, keys, lanes), bf16)],
        compiler_params=pltpu.CompilerParams(vmem_limit_bytes=vmem_grant),
        cost_estimate=pl.CostEstimate(
            flops=4 * rows * keys * width * 4,
            bytes_accessed=keys * width * 4 + rows * width * 6 + 4 * pairs * rows * keys,
            transcendentals=rows * keys * width // head_dim,
        ),
        name="attend",
    )(queries, both, both, extra)


def attend_back_kernel(scale, head_dim, row_step, resumed, *refs):
    q_ref, da_ref, dax_ref, factor_ref, p_ref, k_ref, v_ref, extra_ref = refs[:8]
    start_ref = refs[8] if resumed else None
    dq_ref, dkv_ref, scaled, scaled_extra = refs[-4:]
    j = pl.program_id(1)
    rows = q_ref.shape[0]

    @pl.when(j == 0)
    def _():
        factors = factor_ref[...]
        scaled[...] = (da_ref[...].astype(f32) * factors).astype(bf16)
        turned = pltpu.roll(factors, head_dim, 1)
        scaled_extra[...] = (dax_ref[...].astype(f32) * turned).astype(bf16)

    keys, values, extra = (k_ref[...], v_ref[...], extra_ref[...])
    dk, dv = (None, None)
    for first in range(0, rows, row_step):
        part = slice(first, first + row_step)
        queries, grads, grads_extra = (q_ref[part, :], scaled[part, :], scaled_extra[part, :])
        none = jnp.zeros_like(queries)
        dq = None
        for h in range(2):
            sel = head_lanes(h, head_dim)
            weights = p_ref[h, part, :]
            grad_weights = dot(
                jnp.where(sel, grads, grads_extra), jnp.where(sel, values, extra), 1, 1
            )
            grad_scores = (weights.astype(f32) * grad_weights).astype(bf16)
            part_dv = dot(jnp.where(sel, grads, none), weights, 0, 0)
            part_dk = dot(jnp.where(sel, queries, none), grad_scores, 0, 0)
            part_dq = dot(grad_scores, jnp.where(sel, keys, jnp.zeros_like(keys)), 1, 0)
            dv = part_dv if dv is None else dv + part_dv
            dk = part_dk if dk is None else dk + part_dk
            dq = part_dq if dq is None else dq + part_dq
        dq = dq * scale

        @pl.when(j == 0)
        def _():
            dq_ref[part, :] = dq + start_ref[part, :] if resumed else dq

        @pl.when(j > 0)
        def _():
            dq_ref[part, :] += dq

    dkv_ref[0] = (dk * scale).astype(bf16)
    dkv_ref[1] = dv.astype(bf16)


def attend_back(
    queries, grads, deltas, saved, factors, both, extra, head_dim, first, count, start
):
    rows, width = queries.shape
    pairs = width // lanes
    row_step = min(512, rows)
    step = min(1024, count)
    skip = first // step
    group = first * factors.shape[1] // both.shape[0]
    scale = head_dim ** (-0.5)
    resumed = start is not None
    more = [pl.BlockSpec((rows, lanes), lambda h, j: (0, h))] if resumed else []
    return pl.pallas_call(
        functools.partial(attend_back_kernel, scale, head_dim, row_step, resumed),
        grid=(pairs, count // step),
        in_specs=[
            pl.BlockSpec((rows, lanes), lambda h, j: (0, h)),
            pl.BlockSpec((rows, lanes), lambda h, j: (0, h)),
            pl.BlockSpec((None, rows, lanes), lambda h, j: (h, 0, 0)),
            pl.BlockSpec((None, None, rows, lanes), lambda h, j: (h, group, 0, 0)),
            pl.BlockSpec((None, 2, rows, step), lambda h, j: (h, 0, 0, j + skip)),
            pl.BlockSpec((step, lanes), lambda h, j: (j + skip, h)),
            pl.BlockSpec((step, lanes), lambda h, j: (j + skip, h + pairs)),
            pl.BlockSpec((step, lanes), lambda h, j: (j + skip, 0)),
        ]
        + more,
        out_specs=[
            pl.BlockSpec((rows, lanes), lambda h, j: (0, h)),
            pl.BlockSpec((2, lanes, step), lambda h, j: (0, h, j)),
        ],
        out_shape=[
            jax.ShapeDtypeStruct((rows, width), f32),
            jax.ShapeDtypeStruct((2, width, count), bf16),
        ],
        scratch_shapes=[pltpu.VMEM((rows, lanes), bf16), pltpu.VMEM((rows, lanes), bf16)],
        compiler_params=pltpu.CompilerParams(vmem_limit_bytes=vmem_grant),
        cost_estimate=pl.CostEstimate(
            flops=8 * rows * count * width * 4,
            bytes_accessed=count * width * 8 + rows * width * 16 + 4 * pairs * rows * count,
            transcendentals=0,
        ),
        name="attend_back",
    )(
        queries,
        grads,
        deltas,
        factors,
        saved,
        both,
        both,
        extra,
        *([start] if resumed else []),
    )


def key_lanes(live, head_dim):
    lane = jnp.arange(lanes, dtype=jnp.int32) % head_dim
    bias = jnp.where(live, 0.0, masked_bias)[:, None]
    ones = jnp.where((lane >= 1) & (lane <= 3), 1.0, 0.0)[None, :]
    return jnp.where(lane[None, :] == 0, bias, ones).astype(bf16)


def opening_kernel(
    owners,
    ring,
    pieces,
    tokens_ref,
    weight_ref,
    packed_ref,
    x_ref,
    w_ref,
    vec_ref,
    q_ref,
    kv_ref,
    xs,
    ws,
    vec,
    qs,
    kvs,
    load_sem,
    store_sem,
    send_sem,
    recv_sem,
):
    row, here = (lax.axis_index("dp"), lax.axis_index("ctx"))
    core = lax.rem(here, 2)
    side = here // (ring // 2)
    own_ref = tokens_ref.at[side]
    block, width = tokens_ref.shape[1:]
    share = weight_ref.shape[0]
    half = share // 2
    mate, deep, far = ((row, here ^ 1), (row, here ^ 2), (row, here ^ (ring // 2)))
    owner_peers = [(row ^ k, here) for k in range(1, owners)]
    peers = [mate, deep, far] + owner_peers
    barrier = pltpu.get_barrier_semaphore()
    for peer in peers:
        pl.semaphore_signal(barrier, inc=1, device_id=peer, device_id_type=pl.DeviceIdType.MESH)
    own_load = pltpu.make_async_copy(own_ref, xs.at[0], load_sem.at[0])
    weight_load = pltpu.make_async_copy(weight_ref, ws.at[row], load_sem.at[1])
    vec_load = pltpu.make_async_copy(packed_ref, vec.at[row], load_sem.at[2])
    for load in (own_load, weight_load, vec_load):
        load.start()
    sent, stored = ([], [])
    count = [0]

    def send(source, target, peer):
        slot = count[0]
        count[0] += 1
        copy = pltpu.make_async_remote_copy(
            src_ref=source,
            dst_ref=target,
            send_sem=send_sem.at[slot],
            recv_sem=recv_sem.at[slot],
            device_id=peer,
            device_id_type=pl.DeviceIdType.MESH,
        )
        copy.start()
        sent.append(copy)
        return copy

    def store(source, target):
        copy = pltpu.make_async_copy(source, target, store_sem.at[len(stored)])
        copy.start()
        stored.append(copy)

    step = block // pieces
    parts = [pl.ds(j * step, step) for j in range(pieces)]
    pl.semaphore_wait(barrier, len(peers))
    weights = [
        send(weight_ref.at[pl.ds(core * half, half)], ws.at[row, pl.ds(core * half, half)], peer)
        for peer in owner_peers
    ]
    moved = [send(tokens_ref.at[1 - side, part], xs.at[1, part], far) for part in parts]
    own_deep = send(own_ref, xs.at[2], deep)
    own_mate = send(own_ref, xs.at[4], mate)
    vectors = [send(packed_ref, vec.at[row], peer) for peer in owner_peers]

    moved_deep, moved_mate = ([], [])
    weights_mate = []
    for j, part in enumerate(parts):
        moved[j].wait_recv()
        moved_deep.append(send(xs.at[1, part], xs.at[3, part], deep))
        moved_mate.append(send(xs.at[1, part], xs.at[5, part], mate))
        if j == pieces // 2:
            for k in range(1, owners):
                weights[k - 1].wait_recv()
                held = ws.at[row ^ k, pl.ds(core * half, half)]
                weights_mate.append(send(held, held, mate))
    own_deep.wait_recv()
    deep_mate = send(xs.at[2], xs.at[6], mate)
    for load in (own_load, weight_load, vec_load):
        load.wait()
    for copy in vectors + weights_mate:
        copy.wait_recv()
    for d in range(owners):
        store(ws.at[d], w_ref.at[d])
    store(vec, vec_ref)

    def bias(which):
        return jnp.concatenate(
            [vec[d, which : which + 1, :] for d in range(owners)], axis=1
        ).astype(f32)

    value_bias = bias(1)
    none = jnp.zeros_like(value_bias)

    def product(place, first, last):
        total = None
        for d in range(owners):
            left = xs[place, :, d * share : (d + 1) * share]
            part = dot(left, ws[d, :, first:last], 1, 0)
            total = part if total is None else total + part
        return total

    def project(place):
        store(xs.at[place], x_ref.at[place])
        if place < 2:
            qs[place] = (product(place, 0, width) + bias(0)).astype(bf16)
            store(qs.at[place], q_ref.at[place])
        kvs[place, :, :width] = product(place, width, 2 * width).astype(bf16)
        kvs[place, :, width:] = (product(place, 2 * width, 3 * width) + value_bias).astype(bf16)
        store(kvs.at[place], kv_ref.at[place])

    project(0)
    own_mate.wait_recv()
    project(4)
    project(1)
    for copy in moved_mate:
        copy.wait_recv()
    project(5)
    project(2)
    deep_mate.wait_recv()
    project(6)
    far_mate = []
    for j, part in enumerate(parts):
        moved_deep[j].wait_recv()
        far_mate.append(send(xs.at[3, part], xs.at[7, part], mate))
    project(3)
    for copy in far_mate:
        copy.wait_recv()
    project(7)
    for copy in sent:
        copy.wait_send()
    for copy in stored:
        copy.wait()


def opening(tokens, weight, packed, owners, ring):
    block, width = tokens.shape[1:]
    blocks = ring
    pieces = 4
    any_space = pl.BlockSpec(memory_space=pl.ANY)
    copies = 2 * (owners - 1) + 3 * pieces + 3 + (owners - 1) + pieces
    shapes = [
        jax.ShapeDtypeStruct((blocks, block, width), bf16),
        jax.ShapeDtypeStruct((owners,) + weight.shape, bf16),
        jax.ShapeDtypeStruct((owners,) + packed.shape, bf16),
        jax.ShapeDtypeStruct((2, block, width), bf16),
        jax.ShapeDtypeStruct((blocks, block, 2 * width), bf16),
    ]
    return pl.pallas_call(
        functools.partial(opening_kernel, owners, ring, pieces),
        in_specs=[any_space] * 3,
        out_specs=[any_space] * 5,
        out_shape=shapes,
        scratch_shapes=[pltpu.VMEM(v.shape, v.dtype) for v in shapes]
        + [
            pltpu.SemaphoreType.DMA((3,)),
            pltpu.SemaphoreType.DMA((owners + 1 + 2 * blocks + 2,)),
            pltpu.SemaphoreType.DMA((copies,)),
            pltpu.SemaphoreType.DMA((copies,)),
        ],
        compiler_params=pltpu.CompilerParams(
            vmem_limit_bytes=vmem_grant, collective_id=1, has_side_effects=True
        ),
        cost_estimate=pl.CostEstimate(
            flops=8 * blocks * block * width * width, bytes_accessed=200 << 20, transcendentals=0
        ),
        name="opening",
    )(tokens, weight, packed)


def middle_kernel(
    head_dim,
    chunk,
    mixed_ref,
    x_ref,
    cot_ref,
    live_ref,
    out_ref,
    up_ref,
    down_ref,
    vec_ref,
    up_bias_ref,
    y_ref,
    active_ref,
    hidden_ref,
    dbranch_ref,
    dupper_ref,
    dz_ref,
    dattn_ref,
    dmixed_ref,
    delta_ref,
    sums_ref,
    up_sum_ref,
    slope,
):
    width = x_ref.shape[1]
    inner = up_ref.shape[1]
    out_bias, gain_first, shift_first = (vec_ref[0:1, :], vec_ref[1:2, :], vec_ref[2:3, :])
    down_bias, gain_second, shift_second = (vec_ref[3:4, :], vec_ref[4:5, :], vec_ref[5:6, :])
    live = live_ref[...]
    mixed = mixed_ref[...]
    attn = dot(mixed, out_ref[...], 1, 0) + out_bias
    hidden, unit_first, inverse_first = norm_parts(
        x_ref[...].astype(f32) + attn, gain_first, shift_first
    )
    hidden_low = hidden.astype(bf16)
    hidden_ref[...] = hidden_low
    branch = down_bias
    for first in range(0, inner, chunk):
        part = slice(first, first + chunk)
        upper = dot(hidden_low, up_ref[:, part], 1, 0) + up_bias_ref[:, part]
        below = 0.5 + 0.5 * lax.erf(upper * (0.5**0.5))
        active = (upper * below).astype(bf16)
        bell = jnp.exp2(upper * upper * (-0.5 * log2_e)) * 0.3989422804014327
        slope[:, part] = (below + upper * bell).astype(bf16)
        active_ref[:, part] = active
        branch = branch + dot(active, down_ref[part, :], 1, 0)
    normed, unit_second, inverse_second = norm_parts(hidden + branch, gain_second, shift_second)
    result = normed * live
    y_ref[...] = result.astype(bf16)
    grad_out = cot_ref[...].astype(f32) * live
    grad_second = norm_back(grad_out * gain_second, unit_second, inverse_second)
    grad_branch = grad_second.astype(bf16)
    dbranch_ref[...] = grad_branch
    grad_hidden = grad_second
    up_sums = []
    for first in range(0, inner, chunk):
        part = slice(first, first + chunk)
        grad_active = dot(grad_branch, down_ref[part, :], 1, 1)
        grad_upper = (grad_active * slope[:, part].astype(f32)).astype(bf16)
        dupper_ref[:, part] = grad_upper
        up_sums.append(jnp.sum(grad_upper.astype(f32), axis=0, keepdims=True))
        grad_hidden = grad_hidden + dot(grad_upper, up_ref[:, part], 1, 1)
    grad_first = norm_back(grad_hidden * gain_first, unit_first, inverse_first)
    dz_ref[...] = grad_first
    grad_attn = grad_first.astype(bf16)
    dattn_ref[...] = grad_attn
    grad_mixed = dot(grad_attn, out_ref[...], 1, 1).astype(bf16)
    dmixed_ref[...] = grad_mixed
    cross = grad_mixed.astype(f32) * mixed.astype(f32)
    lane = lax.broadcasted_iota(jnp.int32, (1, lanes), 1)
    lower = lane < head_dim
    for p in range(width // lanes):
        pair = cross[:, p * lanes : (p + 1) * lanes]
        first_head = jnp.sum(jnp.where(lower, pair, 0.0), axis=1, keepdims=True)
        second_head = jnp.sum(jnp.where(lower, 0.0, pair), axis=1, keepdims=True)
        delta_ref[p] = spread_lanes(first_head, second_head, 0.0, head_dim)
    sums = [
        grad_attn.astype(f32),
        grad_hidden * unit_first,
        grad_hidden,
        grad_branch.astype(f32),
        grad_out * unit_second,
        grad_out,
        result * result,
        attn * attn * live,
        branch * branch * live,
    ]
    first_step = pl.program_id(0) == 0

    @pl.when(first_step)
    def _():
        sums_ref[...] = jnp.zeros_like(sums_ref)
        up_sum_ref[...] = jnp.zeros_like(up_sum_ref)

    for i, value in enumerate(sums):
        sums_ref[i : i + 1, :] += jnp.sum(value, axis=0, keepdims=True)
    up_sum_ref[0:1, :] += jnp.concatenate(up_sums, axis=1)


def middle(mixed, stream, cot, live, out_all, up_all, down_all, vectors, up_bias, head_dim):
    count, width = mixed.shape
    inner = up_all.shape[1]
    pairs = width // lanes
    row_step = min(256, count)
    chunk = min(768, inner)

    def fixed(shape):
        return pl.BlockSpec(shape, lambda i: (0, 0), pipeline_mode=pl.Buffered(1))

    def block(columns):
        return pl.BlockSpec((row_step, columns), lambda i: (i, 0))

    return pl.pallas_call(
        functools.partial(middle_kernel, head_dim, chunk),
        grid=(count // row_step,),
        in_specs=[
            block(width),
            block(width),
            block(width),
            block(1),
            fixed((width, width)),
            fixed((width, inner)),
            fixed((inner, width)),
            fixed(vectors.shape),
            fixed(up_bias.shape),
        ],
        out_specs=[
            block(width),
            block(inner),
            block(width),
            block(width),
            block(inner),
            block(width),
            block(width),
            block(width),
            pl.BlockSpec((pairs, row_step, lanes), lambda i: (0, i, 0)),
            pl.BlockSpec((16, width), lambda i: (0, 0)),
            pl.BlockSpec((8, inner), lambda i: (0, 0)),
        ],
        out_shape=[
            jax.ShapeDtypeStruct((count, width), bf16),
            jax.ShapeDtypeStruct((count, inner), bf16),
            jax.ShapeDtypeStruct((count, width), bf16),
            jax.ShapeDtypeStruct((count, width), bf16),
            jax.ShapeDtypeStruct((count, inner), bf16),
            jax.ShapeDtypeStruct((count, width), f32),
            jax.ShapeDtypeStruct((count, width), bf16),
            jax.ShapeDtypeStruct((count, width), bf16),
            jax.ShapeDtypeStruct((pairs, count, lanes), bf16),
            jax.ShapeDtypeStruct((16, width), f32),
            jax.ShapeDtypeStruct((8, inner), f32),
        ],
        scratch_shapes=[pltpu.VMEM((row_step, inner), bf16)],
        compiler_params=pltpu.CompilerParams(vmem_limit_bytes=vmem_grant),
        cost_estimate=pl.CostEstimate(
            flops=4 * count * width * (2 * inner + width),
            bytes_accessed=4 * width * inner + count * (18 * width + 4 * inner),
            transcendentals=4 * count * inner,
        ),
        name="middle",
    )(mixed, stream, cot, live, out_all, up_all, down_all, vectors, up_bias)


def put_pieces(value, keep_ref, give_ref):
    share, width = keep_ref.shape[1:]
    core = lax.rem(lax.axis_index("ctx"), 2)
    value = value.reshape(-1, 2, share, width)
    even, odd = (value[:, 0], value[:, 1])
    keep_ref[...] = jnp.where(core == 0, even, odd).astype(bf16)
    give_ref[...] = jnp.where(core == 0, odd, even).astype(bf16)


def up_out_kernel(blocks, hidden_ref, dupper_ref, mixed_ref, dattn_ref, keep_ref, give_ref):
    s = pl.program_id(0)

    @pl.when(s < blocks)
    def _():
        put_pieces(dot(hidden_ref[...], dupper_ref[...], 0, 0), keep_ref, give_ref)

    @pl.when(s == blocks)
    def _():
        put_pieces(dot(mixed_ref[...], dattn_ref[...], 0, 0), keep_ref, give_ref)


def down_kernel(active_ref, dbranch_ref, held_keep, held_give, keep_ref, give_ref):
    del held_keep, held_give
    put_pieces(dot(active_ref[...], dbranch_ref[...], 0, 0), keep_ref, give_ref)


def middle_grads(hidden, dupper, mixed, dattn, active, dbranch, owners, ring):
    count, width = hidden.shape
    inner = dupper.shape[1]
    devices = owners * ring
    share = width // devices
    blocks = inner // width
    tall = inner // devices
    piece = blocks * share + tall + share
    shape = [jax.ShapeDtypeStruct((devices // 2, piece, width), bf16)] * 2
    params = pltpu.CompilerParams(vmem_limit_bytes=vmem_grant)
    whole = pl.BlockSpec((count, width), lambda s: (0, 0))
    any_space = pl.BlockSpec(memory_space=pl.ANY)
    keep, give = pl.pallas_call(
        functools.partial(up_out_kernel, blocks),
        grid=(blocks + 1,),
        in_specs=[
            whole,
            pl.BlockSpec((count, width), lambda s: (0, jnp.minimum(s, blocks - 1))),
            whole,
            whole,
        ],
        out_specs=[
            pl.BlockSpec(
                (devices // 2, share, width),
                lambda s: (0, jnp.where(s < blocks, s, piece // share - 1), 0),
            )
        ]
        * 2,
        out_shape=shape,
        compiler_params=params,
        cost_estimate=pl.CostEstimate(
            flops=2 * count * width * (inner + width),
            bytes_accessed=2 * (count + width) * (inner + 3 * width),
            transcendentals=0,
        ),
        name="up_grads",
    )(hidden, dupper, mixed, dattn)
    return pl.pallas_call(
        down_kernel,
        grid=(owners,),
        in_specs=[
            pl.BlockSpec((count, inner // owners), lambda s: (0, s)),
            whole,
            any_space,
            any_space,
        ],
        out_specs=[
            pl.BlockSpec((ring // 2, tall, width), lambda s: (s, blocks * share // tall, 0))
        ]
        * 2,
        out_shape=shape,
        input_output_aliases={2: 0, 3: 1},
        compiler_params=params,
        cost_estimate=pl.CostEstimate(
            flops=2 * count * width * inner,
            bytes_accessed=2 * (count + width) * (inner + width),
            transcendentals=0,
        ),
        name="down_grads",
    )(active, dbranch, keep, give)


def closing_kernel(owners, ring, firsts, dq_ref, x_ref, *refs):
    shares = refs[: len(firsts)]
    small_ref, home_ref, out_ref, small_out_ref, home_out_ref = refs[len(firsts) : len(firsts) + 5]
    (
        xs,
        dq,
        dkv,
        whole,
        parts,
        in_core,
        by_owner,
        in_owner,
        by_piece,
        in_piece,
        done,
        in_done,
        small,
        small_core,
        small_owner,
        small_piece,
        load_sem,
        send_sem,
        recv_sem,
    ) = refs[len(firsts) + 5 :]
    row, here = (lax.axis_index("dp"), lax.axis_index("ctx"))
    core, depth = (lax.rem(here, 2), here // 2)
    deep = ring // 2
    count = dq.shape[0]
    loads = [
        pltpu.make_async_copy(dq_ref, dq, load_sem.at[0]),
        pltpu.make_async_copy(x_ref, xs, load_sem.at[1]),
    ]
    for i, first in enumerate(firsts):
        columns = pl.ds(first, shares[i].shape[2])
        loads.append(pltpu.make_async_copy(shares[i], dkv.at[:, :, columns], load_sem.at[2 + i]))
    for load in loads:
        load.start()

    mate = (row, here ^ 1)
    owner_peers = [(row ^ k, here) for k in range(1, owners)]
    depth_peers = [(row, here ^ (2 * k)) for k in range(1, deep)]
    barrier = pltpu.get_barrier_semaphore()
    peers = [mate] + owner_peers + depth_peers
    for peer in peers:
        pl.semaphore_signal(barrier, inc=1, device_id=peer, device_id_type=pl.DeviceIdType.MESH)

    sent = []

    def send(source, target, peer, m, slot):
        copy = pltpu.make_async_remote_copy(
            src_ref=source,
            dst_ref=target,
            send_sem=send_sem.at[m, slot],
            recv_sem=recv_sem.at[m, slot],
            device_id=peer,
            device_id_type=pl.DeviceIdType.MESH,
        )
        copy.start()
        sent.append(copy)
        return copy

    at_owner = 1
    at_piece = owners
    at_done = at_piece + deep - 1
    at_back = at_done + deep - 1
    tile = 256

    def to_core(m):
        def one(t, carry):
            columns = pl.ds(pl.multiple_of(t * tile, tile), tile)
            if m == 0:
                whole[columns, :] = dot(xs[0:count, columns], dq[...].astype(bf16), 0, 0)
            else:
                whole[columns, :] = dot(xs[:, columns], dkv[m - 1], 0, 1)
            return carry

        lax.fori_loop(0, whole.shape[0] // tile, one, 0)
        parts[m] = whole[...].reshape(parts.shape[1:]).astype(bf16)
        return [send(parts.at[m, :, 1 - core], in_core.at[m], mate, m, 0)]

    def to_owner(m):
        mine = parts[m, :, core].astype(f32)
        by_owner[m] = (mine + in_core[m].astype(f32)).astype(bf16)
        return [
            send(by_owner.at[m, row ^ k], in_owner.at[m, k - 1], owner_peers[k - 1], m, at_owner + k - 1)
            for k in range(1, owners)
        ]

    def to_piece(m):
        total = by_owner[m, row].astype(f32)
        for k in range(1, owners):
            total = total + in_owner[m, k - 1].astype(f32)
        by_piece[m] = total.reshape(by_piece.shape[1:]).astype(bf16)
        return [
            send(
                by_piece.at[m, depth ^ k],
                in_piece.at[m, k - 1],
                depth_peers[k - 1],
                m,
                at_piece + k - 1,
            )
            for k in range(1, deep)
        ]

    def to_done(m):
        total = by_piece[m, depth].astype(f32)
        for k in range(1, deep):
            total = total + in_piece[m, k - 1].astype(f32)
        done[m, depth] = total.astype(bf16)
        return [
            send(done.at[m, depth], done.at[m, depth], depth_peers[k - 1], m, at_done + k - 1)
            for k in range(1, deep)
        ]

    def to_back(m):
        return [send(done.at[m], in_done.at[m], mate, m, at_back)]

    def finish(m):
        size = out_ref.shape[1]
        columns = slice(m * whole.shape[1], (m + 1) * whole.shape[1])
        out_ref[core, :, columns] = done[m].astype(f32).reshape(size, whole.shape[1])
        out_ref[1 - core, :, columns] = in_done[m].astype(f32).reshape(size, whole.shape[1])
        return []

    stages = [to_core, to_owner, to_piece, to_done, to_back, finish]
    waiting = [[], [], []]
    loads[0].wait()
    loads[1].wait()
    pl.semaphore_wait(barrier, len(peers))
    home = send(home_ref, home_out_ref, (row, here ^ (ring // 2)), 3, at_back)
    small_waits = []
    for step in range(len(stages) + 2):
        for m in range(3):
            stage = step - m
            if 0 <= stage < len(stages):
                for copy in waiting[m]:
                    copy.wait_recv()
                waiting[m] = stages[stage](m)
        if step == 0:
            small[...] = small_ref[...]
            small[0:1, :] = jnp.sum(dq[...].astype(bf16).astype(f32), axis=0, keepdims=True)
            for load in loads[2:]:
                load.wait()
            ones = jnp.ones((8, dkv.shape[2]), bf16)
            small[1:2, :] = dot(ones, dkv[1], 1, 1)[0:1, :]
            small_waits = [send(small, small_core, mate, 3, 0)]
        if step == 1:
            small_waits[0].wait_recv()
            small_owner[0] = small[...] + small_core[...]
            small_waits = [
                send(small_owner.at[0], small_owner.at[k], owner_peers[k - 1], 3, k)
                for k in range(1, owners)
            ]
        if step == 3:
            total = small_owner[0]
            for k in range(1, owners):
                small_waits[k - 1].wait_recv()
                total = total + small_owner[k]
            small_piece[0] = total
            small_waits = [
                send(small_piece.at[0], small_piece.at[k], depth_peers[k - 1], 3, at_piece + k - 1)
                for k in range(1, deep)
            ]
        if step == 5:
            total = small_piece[0]
            for k in range(1, deep):
                small_waits[k - 1].wait_recv()
                total = total + small_piece[k]
            small_out_ref[...] = total
    home.wait_recv()
    for copy in sent:
        copy.wait_send()


def closing(dq, stream, shares, small, home, owners, ring):
    count, width = dq.shape
    keys = stream.shape[0]
    firsts = tuple(first for first, _ in shares)
    shares = [v for _, v in shares]
    deep = ring // 2
    half = width // owners // 2
    piece = half // deep
    slots = 1 + (owners - 1) + 2 * (deep - 1) + 1
    any_space = pl.BlockSpec(memory_space=pl.ANY)
    in_vmem = pl.BlockSpec(memory_space=pltpu.VMEM)
    return pl.pallas_call(
        functools.partial(closing_kernel, owners, ring, firsts),
        in_specs=[any_space] * (2 + len(shares)) + [in_vmem, any_space],
        out_specs=[in_vmem, in_vmem, any_space],
        out_shape=[
            jax.ShapeDtypeStruct((2, half, 3 * width), f32),
            jax.ShapeDtypeStruct(small.shape, f32),
            jax.ShapeDtypeStruct(home.shape, home.dtype),
        ],
        scratch_shapes=[
            pltpu.VMEM((keys, width), bf16),
            pltpu.VMEM((count, width), f32),
            pltpu.VMEM((2, width, keys), bf16),
            pltpu.VMEM((width, width), f32),
            pltpu.VMEM((3, owners, 2, half, width), bf16),
            pltpu.VMEM((3, owners, half, width), bf16),
            pltpu.VMEM((3, owners, half, width), bf16),
            pltpu.VMEM((3, owners - 1, half, width), bf16),
            pltpu.VMEM((3, deep, piece, width), bf16),
            pltpu.VMEM((3, deep - 1, piece, width), bf16),
            pltpu.VMEM((3, deep, piece, width), bf16),
            pltpu.VMEM((3, deep, piece, width), bf16),
            pltpu.VMEM(small.shape, f32),
            pltpu.VMEM(small.shape, f32),
            pltpu.VMEM((owners,) + small.shape, f32),
            pltpu.VMEM((deep,) + small.shape, f32),
            pltpu.SemaphoreType.DMA((2 + len(shares),)),
            pltpu.SemaphoreType.DMA((4, slots)),
            pltpu.SemaphoreType.DMA((4, slots)),
        ],
        compiler_params=pltpu.CompilerParams(
            vmem_limit_bytes=vmem_grant, collective_id=0, has_side_effects=True
        ),
        cost_estimate=pl.CostEstimate(
            flops=20 * keys * width * width, bytes_accessed=100 << 20, transcendentals=0
        ),
        name="closing",
    )(dq, stream, *shares, small, home)


def shards(
    ring,
    tokens,
    cotangent,
    lengths,
    block_order,
    qkv_weight,
    query_bias,
    value_bias,
    out_weight,
    out_bias,
    attn_gain,
    attn_shift,
    up_weight,
    up_bias,
    down_weight,
    down_bias,
    ffn_gain,
    ffn_shift,
):
    seqs, block, width = tokens.shape
    head_dim = width // HEADS
    assert seqs == 2 and ring % 4 == 0
    half = ring // 2
    here = lax.axis_index("ctx")
    side = here // half

    def pick(array, index):
        return lax.dynamic_index_in_dim(array, index, 0, keepdims=False)

    def exchange(array, bit):
        return lax.ppermute(array, "ctx", [(i, i ^ bit) for i in range(ring)])

    def arrange(kept, other):
        first = jnp.where(side == 0, kept, other)
        second = jnp.where(side == 0, other, kept)
        return jnp.stack([first, second])

    def gather(array):
        return lax.all_gather(array, "dp", axis=0, tiled=True)

    bits = []
    bit = half // 2
    while bit:
        bits.append(bit)
        bit //= 2
    ids = jnp.stack([here, here ^ half])
    for bit in bits:
        ids = jnp.concatenate([ids, ids ^ bit])
    count_rows = 2 * block

    order = pick(block_order, side)
    length = pick(lengths, side)
    table = jnp.arange(ring, dtype=jnp.int32)
    place_of = jnp.sum(jnp.where(ids[:, None] == table[None, :], order[None, :], 0), axis=1)
    places = place_of[:, None] * block + jnp.arange(block, dtype=jnp.int32)[None, :]
    live_keys = (places < length).reshape(-1)
    live_rows = live_keys[:count_rows, None].astype(f32)
    extra = key_lanes(live_keys, head_dim)

    row = lax.axis_index("dp")
    owners = lax.axis_size("dp")
    devices = owners * ring
    inner = up_weight.shape[1]
    share = query_bias.shape[0]
    laid = ring == 8 and width % (8 * devices) == 0 and inner % width == 0 and block % 32 == 0
    singles = [
        query_bias,
        value_bias,
        out_bias,
        attn_gain,
        attn_shift,
        down_bias,
        ffn_gain,
        ffn_shift,
    ]
    ups = up_bias.reshape(-1, share)
    count_vectors = len(singles) + ups.shape[0]
    which = lax.broadcasted_iota(jnp.int32, (count_vectors, share), 0)
    packed = jnp.pad(ups, ((len(singles), 0), (0, 0)))
    for i, v in enumerate(singles):
        packed = jnp.where(which == i, v[None, :], packed)
    if laid:
        stream, qkv_all, vectors, queries, both = opening(
            tokens, qkv_weight, packed, owners, ring
        )
        stream = stream.reshape(-1, width)
        qkv_all = qkv_all.reshape(width, -1)
        vectors = vectors.astype(f32)
        queries = queries.reshape(-1, width)
        both = both.reshape(-1, 2 * width)
    else:
        qkv_all = gather(qkv_weight)
        vectors = gather(packed[None]).astype(f32)
        other = exchange(pick(tokens, 1 - side), half)
        stream = jnp.concatenate([pick(tokens, side), other], axis=0)
        for bit in bits:
            stream = jnp.concatenate([stream, exchange(stream, bit)], axis=0)
    rows = stream[:count_rows]
    bias = [vectors[:, i].reshape(1, width) for i in range(8)]
    up_bias_all = vectors[:, 8:].reshape(1, -1)
    if not laid:
        queries = (
            jnp.dot(rows, qkv_all[:, :width], preferred_element_type=f32) + bias[0]
        ).astype(bf16)
        kv_bias = jnp.concatenate([jnp.zeros_like(bias[1]), bias[1]], axis=1)
        both = jnp.dot(stream, qkv_all[:, width:], preferred_element_type=f32) + kv_bias
        both = both.astype(bf16)
    out_all = gather(out_weight)
    up_all = gather(up_weight)
    down_all = gather(down_weight)
    held, _ = lax.optimization_barrier((cotangent, stream))
    cot = jnp.concatenate([pick(held, side), exchange(pick(held, 1 - side), half)], axis=0)

    mixed, saved, factors = attend(queries, both, extra, head_dim)
    (
        result,
        active,
        hidden,
        grad_branch,
        grad_upper,
        grad_first,
        grad_attn,
        grad_mixed,
        deltas,
        sums,
        up_sum,
    ) = middle(
        mixed,
        stream,
        cot,
        live_rows,
        out_all,
        up_all,
        down_all,
        jnp.concatenate(bias[2:] + [jnp.zeros((2, width), f32)], axis=0),
        up_bias_all,
        head_dim,
    )
    output = arrange(result[:block], exchange(result[block:], half))

    def scatter(grad):
        return lax.psum_scatter(grad, ("dp", "ctx"), scatter_dimension=0, tiled=True)

    def spread(parts):
        return jax.tree.map(lambda v: lax.all_gather(v, "ctx", axis=0, tiled=True), parts)

    if laid:
        keep, give = middle_grads(
            hidden, grad_upper, mixed, grad_attn, active, grad_branch, owners, ring
        )
        given = exchange(give, 1)
        scattered = None
    else:
        grads = (dot(hidden, grad_upper, 0, 0), dot(active, grad_branch, 0, 0), dot(mixed, grad_attn, 0, 0))
        scattered = tuple(scatter(grad.astype(bf16)) for grad in grads)
    gathered = []
    calls = []

    kv_weight = qkv_all[:, width:]
    size = 2 * block
    grad_queries = None
    shares = []

    def reduced(place, level):
        nonlocal grad_queries, scattered
        if level == len(bits):
            first = place * size
            if laid and len(calls) == 1:
                both_cores = keep + given
                both_cores, grad_queries = lax.optimization_barrier((both_cores, grad_queries))
                scattered = lax.psum_scatter(
                    both_cores,
                    ("dp", "ctx"),
                    scatter_dimension=0,
                    axis_index_groups=[
                        [n for n in range(devices) if n % 2 == core] for core in range(2)
                    ],
                    tiled=True,
                )
            if place == 0:
                held, grad_queries = lax.optimization_barrier((scattered, grad_queries))
                gathered.append(spread(held))
            calls.append(place)
            grad_queries, grad_both = attend_back(
                queries,
                grad_mixed,
                deltas,
                saved,
                factors,
                both,
                extra,
                head_dim,
                first,
                size,
                grad_queries,
            )
            shares.append((first, grad_both))
            return dot(grad_both.reshape(2 * width, size), kv_weight, 0, 1)
        low = reduced(place + (1 << level), level + 1).astype(bf16)
        low, grad_queries = lax.optimization_barrier((low, grad_queries))
        other = exchange(low, bits[level])
        if level + 1 == len(bits):
            return reduced(place, level + 1) + other.astype(f32)
        if level + 2 < len(bits):
            return reduced(place, level + 1) + other.astype(f32)
        low = reduced(place + (1 << (level + 1)), level + 2).astype(bf16)
        low, other, grad_queries = lax.optimization_barrier((low, other, grad_queries))
        mate = exchange(low, bits[level + 1])
        return reduced(place, level + 2) + mate.astype(f32) + other.astype(f32)

    grad_stream = reduced(0, 0)
    grad_query_low = grad_queries.astype(bf16)
    grad_rows = grad_first + dot(grad_query_low, qkv_all[:, :width], 1, 1) + grad_stream
    grad_rows_low = grad_rows.astype(bf16)
    grad_rows_low, grad_queries, pieces = lax.optimization_barrier(
        (grad_rows_low, grad_queries, gathered[0])
    )
    if laid:
        pieces = pieces.astype(f32)
        each, tall = (width // devices, inner // devices)
        blocks = inner // width
        cut = blocks * each
        grad_up_weight = jnp.concatenate(
            [pieces[:, i * each : (i + 1) * each, :].reshape(share, width) for i in range(blocks)],
            axis=1,
        )
        grad_down_weight = pieces[:, cut : cut + tall, :].reshape(-1, width)
        grad_out_weight = pieces[:, cut + tall :, :].reshape(share, width)
    else:
        grad_up_weight, grad_down_weight, grad_out_weight = (v.astype(f32) for v in pieces)

    squares = jnp.sum(sums[6:9], axis=1)
    lane = jnp.arange(width)
    mine = (lane // 3) == (row * 2 + side)
    squares = jnp.where(
        lane % 3 == 0, squares[0], jnp.where(lane % 3 == 1, squares[1], squares[2])
    )
    squares = jnp.where(mine, squares, 0.0)[None, :]
    small = jnp.concatenate(
        [jnp.zeros((2, width), f32), sums[:6], squares, up_sum[0].reshape(-1, width)], axis=0
    )
    small = jnp.pad(small, ((0, -small.shape[0] % 8), (0, 0)))
    if laid:
        grad_qkv_weight, summed, other = closing(
            grad_queries, stream, shares, small, grad_rows_low[block:], owners, ring
        )
        grad_qkv_weight = grad_qkv_weight.reshape(share, 3 * width)
    else:
        other = exchange(grad_rows_low[block:], half)
        kv_parts = []
        for which in range(2):
            part = 0.0
            for first, v in shares:
                part = part + dot(stream[first : first + size], v[which], 0, 1)
            kv_parts.append(part)
        grad_qkv_weight = jnp.concatenate([dot(rows, grad_query_low, 0, 0)] + kv_parts, axis=1)
        grad_qkv_weight = spread(scatter(grad_qkv_weight.astype(bf16))).astype(f32)
        grad_query_bias = jnp.sum(grad_query_low, axis=0, dtype=f32)
        grad_value_bias = sum(jnp.sum(v[1], axis=1, dtype=f32) for _, v in shares)
        small = jnp.concatenate([grad_query_bias[None], grad_value_bias[None], small[2:]], axis=0)
        summed = lax.psum(small, ("dp", "ctx"))

    grad_tokens = arrange(grad_rows_low[:block], other)
    totals = [lax.dynamic_slice_in_dim(summed[i], row * share, share) for i in range(8)]
    tall = inner // owners
    up_total = lax.dynamic_slice_in_dim(summed[9:].reshape(-1), row * tall, tall)
    seq_squares = lax.dynamic_slice_in_dim(summed[8], row * 6, 6).reshape(2, 3)
    branch_rms = jnp.sqrt(seq_squares / (lengths.astype(f32)[:, None] * width) + rms_eps)
    return (
        output,
        grad_tokens,
        grad_qkv_weight,
        totals[0],
        totals[1],
        grad_out_weight,
        totals[2],
        totals[3],
        totals[4],
        grad_up_weight,
        up_total,
        grad_down_weight,
        totals[5],
        totals[6],
        totals[7],
        branch_rms,
    )


def solution(mesh):
    in_specs = (
        P("dp", "ctx", None),
        P("dp", "ctx", None),
        P("dp"),
        P("dp", None),
        P("dp", None),
        P("dp"),
        P("dp"),
        P("dp", None),
        P("dp"),
        P("dp"),
        P("dp"),
        P("dp", None),
        P("dp"),
        P("dp", None),
        P("dp"),
        P("dp"),
        P("dp"),
    )
    out_specs = (
        P("dp", "ctx", None),
        P("dp", "ctx", None),
        P("dp", None),
        P("dp"),
        P("dp"),
        P("dp", None),
        P("dp"),
        P("dp"),
        P("dp"),
        P("dp", None),
        P("dp"),
        P("dp", None),
        P("dp"),
        P("dp"),
        P("dp"),
        P("dp", None),
    )
    return jax.shard_map(
        functools.partial(shards, mesh.shape["ctx"]),
        mesh=mesh,
        in_specs=in_specs,
        out_specs=out_specs,
        check_vma=False,
    )
```

```python
import functools

import jax
import jax.numpy as jnp
from jax import lax
from jax.experimental import pallas as pl
from jax.experimental.pallas import tpu as pltpu
from jax.sharding import PartitionSpec as P

HEADS = 12

norm_eps = 1e-12
rms_eps = 1e-06
masked_bias = -1e30
log2_e = 1.4426950408889634
lanes = 128
vmem_grant = 56 << 20
f32 = jnp.float32
bf16 = jnp.bfloat16


def norm_parts(total, gain, shift):
    mean = jnp.mean(total, axis=-1, keepdims=True)
    centred = total - mean
    inverse = lax.rsqrt(jnp.mean(centred * centred, axis=-1, keepdims=True) + norm_eps)
    unit = centred * inverse
    return (unit * gain + shift, unit, inverse)


def norm_back(grad_unit, unit, inverse):
    mean_grad = jnp.mean(grad_unit, axis=-1, keepdims=True)
    mean_cross = jnp.mean(grad_unit * unit, axis=-1, keepdims=True)
    return inverse * (grad_unit - mean_grad - unit * mean_cross)


def dot(left, right, left_dim, right_dim):
    return lax.dot_general(
        left, right, (((left_dim,), (right_dim,)), ((), ())), preferred_element_type=f32
    )


def head_lanes(head, head_dim):
    lane = lax.broadcasted_iota(jnp.int32, (1, lanes), 1)
    return (lane // head_dim) == head


def spread_lanes(first_head, second_head, unit, head_dim):
    rows = first_head.shape[0]
    lane = lax.broadcasted_iota(jnp.int32, (rows, lanes), 1)
    place = lane % head_dim
    value = -jnp.where(lane < head_dim, second_head, first_head)
    high = value.astype(bf16).astype(f32)
    rest = value - high
    mid = rest.astype(bf16).astype(f32)
    low = rest - mid
    out = jnp.where(place == 1, high, jnp.where(place == 2, mid, jnp.where(place == 3, low, 0.0)))
    return jnp.where(place == 0, unit, out).astype(bf16)


def attend_kernel(
    scale, head_dim, step, q_ref, k_ref, v_ref, extra_ref, o_ref, p_ref, factor_ref, kb, vb
):
    keys = k_ref.shape[0]

    @pl.when(pl.program_id(1) == 0)
    def _():
        for h in range(2):
            kb[h] = jnp.where(head_lanes(h, head_dim), k_ref[...], extra_ref[...])
            vb[h] = jnp.where(head_lanes(h, head_dim), v_ref[...], extra_ref[...])

    factor = scale * log2_e
    queries = q_ref[...]
    lane = lax.broadcasted_iota(jnp.int32, (1, lanes), 1)
    bias_lane = jnp.where(lane % head_dim == 0, 1.0, 0.0).astype(bf16)
    outs, factors = ([], [])
    for h in range(2):
        own = jnp.where(head_lanes(h, head_dim), queries, bias_lane)
        best, acc = (None, None)
        bests = []
        for first in range(0, keys, step):
            scores = dot(own, kb[h, first : first + step, :], 1, 1)
            high = jnp.max(scores, axis=1, keepdims=True)
            new_best = high if best is None else jnp.maximum(best, high)
            weights = jnp.exp2((scores - new_best) * factor).astype(bf16)
            p_ref[h, :, first : first + step] = weights
            part = dot(weights, vb[h, first : first + step, :], 1, 0)
            acc = part if best is None else acc * jnp.exp2((best - new_best) * factor) + part
            best = new_best
            bests.append(best)
        free = (1 - h) * head_dim + 1
        total = acc[:, free : free + 1]
        outs.append(acc / total)
        factors.append([jnp.exp2((high - best) * factor) / total for high in bests])
    o_ref[...] = jnp.where(head_lanes(0, head_dim), outs[0], outs[1]).astype(bf16)
    for s in range(keys // step):
        factor_ref[s] = jnp.where(head_lanes(0, head_dim), factors[0][s], factors[1][s])


def attend(queries, both, extra, head_dim):
    rows, width = queries.shape
    keys = both.shape[0]
    pairs = width // lanes
    row_step = min(512, rows)
    step = min(2048, keys)
    scale = head_dim ** (-0.5)
    return pl.pallas_call(
        functools.partial(attend_kernel, scale, head_dim, step),
        grid=(pairs, rows // row_step),
        in_specs=[
            pl.BlockSpec((row_step, lanes), lambda h, i: (i, h)),
            pl.BlockSpec((keys, lanes), lambda h, i: (0, h)),
            pl.BlockSpec((keys, lanes), lambda h, i: (0, h + pairs)),
            pl.BlockSpec((keys, lanes), lambda h, i: (0, 0)),
        ],
        out_specs=[
            pl.BlockSpec((row_step, lanes), lambda h, i: (i, h)),
            pl.BlockSpec((None, 2, row_step, keys), lambda h, i: (h, 0, i, 0)),
            pl.BlockSpec((None, keys // step, row_step, lanes), lambda h, i: (h, 0, i, 0)),
        ],
        out_shape=[
            jax.ShapeDtypeStruct((rows, width), bf16),
            jax.ShapeDtypeStruct((pairs, 2, rows, keys), bf16),
            jax.ShapeDtypeStruct((pairs, keys // step, rows, lanes), f32),
        ],
        scratch_shapes=[pltpu.VMEM((2, keys, lanes), bf16), pltpu.VMEM((2, keys, lanes), bf16)],
        compiler_params=pltpu.CompilerParams(vmem_limit_bytes=vmem_grant),
        cost_estimate=pl.CostEstimate(
            flops=4 * rows * keys * width * 4,
            bytes_accessed=keys * width * 4 + rows * width * 6 + 4 * pairs * rows * keys,
            transcendentals=rows * keys * width // head_dim,
        ),
        name="attend",
    )(queries, both, both, extra)


def attend_back_kernel(scale, head_dim, row_step, resumed, *refs):
    q_ref, da_ref, dax_ref, factor_ref, p_ref, k_ref, v_ref, extra_ref = refs[:8]
    start_ref = refs[8] if resumed else None
    dq_ref, dkv_ref, scaled, scaled_extra = refs[-4:]
    j = pl.program_id(1)
    rows = q_ref.shape[0]

    @pl.when(j == 0)
    def _():
        factors = factor_ref[...]
        scaled[...] = (da_ref[...].astype(f32) * factors).astype(bf16)
        turned = pltpu.roll(factors, head_dim, 1)
        scaled_extra[...] = (dax_ref[...].astype(f32) * turned).astype(bf16)

    keys, values, extra = (k_ref[...], v_ref[...], extra_ref[...])
    dk, dv = (None, None)
    for first in range(0, rows, row_step):
        part = slice(first, first + row_step)
        queries, grads, grads_extra = (q_ref[part, :], scaled[part, :], scaled_extra[part, :])
        none = jnp.zeros_like(queries)
        dq = None
        for h in range(2):
            sel = head_lanes(h, head_dim)
            weights = p_ref[h, part, :]
            grad_weights = dot(
                jnp.where(sel, grads, grads_extra), jnp.where(sel, values, extra), 1, 1
            )
            grad_scores = (weights.astype(f32) * grad_weights).astype(bf16)
            part_dv = dot(jnp.where(sel, grads, none), weights, 0, 0)
            part_dk = dot(jnp.where(sel, queries, none), grad_scores, 0, 0)
            part_dq = dot(grad_scores, jnp.where(sel, keys, jnp.zeros_like(keys)), 1, 0)
            dv = part_dv if dv is None else dv + part_dv
            dk = part_dk if dk is None else dk + part_dk
            dq = part_dq if dq is None else dq + part_dq
        dq = dq * scale

        @pl.when(j == 0)
        def _():
            dq_ref[part, :] = dq + start_ref[part, :] if resumed else dq

        @pl.when(j > 0)
        def _():
            dq_ref[part, :] += dq

    dkv_ref[0] = (dk * scale).astype(bf16)
    dkv_ref[1] = dv.astype(bf16)


def attend_back(
    queries, grads, deltas, saved, factors, both, extra, head_dim, first, count, start
):
    rows, width = queries.shape
    pairs = width // lanes
    row_step = min(512, rows)
    step = min(1024, count)
    skip = first // step
    group = first * factors.shape[1] // both.shape[0]
    scale = head_dim ** (-0.5)
    resumed = start is not None
    more = [pl.BlockSpec((rows, lanes), lambda h, j: (0, h))] if resumed else []
    return pl.pallas_call(
        functools.partial(attend_back_kernel, scale, head_dim, row_step, resumed),
        grid=(pairs, count // step),
        in_specs=[
            pl.BlockSpec((rows, lanes), lambda h, j: (0, h)),
            pl.BlockSpec((rows, lanes), lambda h, j: (0, h)),
            pl.BlockSpec((None, rows, lanes), lambda h, j: (h, 0, 0)),
            pl.BlockSpec((None, None, rows, lanes), lambda h, j: (h, group, 0, 0)),
            pl.BlockSpec((None, 2, rows, step), lambda h, j: (h, 0, 0, j + skip)),
            pl.BlockSpec((step, lanes), lambda h, j: (j + skip, h)),
            pl.BlockSpec((step, lanes), lambda h, j: (j + skip, h + pairs)),
            pl.BlockSpec((step, lanes), lambda h, j: (j + skip, 0)),
        ]
        + more,
        out_specs=[
            pl.BlockSpec((rows, lanes), lambda h, j: (0, h)),
            pl.BlockSpec((2, lanes, step), lambda h, j: (0, h, j)),
        ],
        out_shape=[
            jax.ShapeDtypeStruct((rows, width), f32),
            jax.ShapeDtypeStruct((2, width, count), bf16),
        ],
        scratch_shapes=[pltpu.VMEM((rows, lanes), bf16), pltpu.VMEM((rows, lanes), bf16)],
        compiler_params=pltpu.CompilerParams(vmem_limit_bytes=vmem_grant),
        cost_estimate=pl.CostEstimate(
            flops=8 * rows * count * width * 4,
            bytes_accessed=count * width * 8 + rows * width * 16 + 4 * pairs * rows * count,
            transcendentals=0,
        ),
        name="attend_back",
    )(
        queries,
        grads,
        deltas,
        factors,
        saved,
        both,
        both,
        extra,
        *([start] if resumed else []),
    )


def key_lanes(live, head_dim):
    lane = jnp.arange(lanes, dtype=jnp.int32) % head_dim
    bias = jnp.where(live, 0.0, masked_bias)[:, None]
    ones = jnp.where((lane >= 1) & (lane <= 3), 1.0, 0.0)[None, :]
    return jnp.where(lane[None, :] == 0, bias, ones).astype(bf16)


def opening_kernel(
    owners,
    ring,
    pieces,
    tokens_ref,
    weight_ref,
    packed_ref,
    x_ref,
    w_ref,
    vec_ref,
    q_ref,
    kv_ref,
    xs,
    ws,
    vec,
    qs,
    kvs,
    load_sem,
    store_sem,
    send_sem,
    recv_sem,
):
    row, here = (lax.axis_index("dp"), lax.axis_index("ctx"))
    core = lax.rem(here, 2)
    side = here // (ring // 2)
    own_ref = tokens_ref.at[side]
    block, width = tokens_ref.shape[1:]
    share = weight_ref.shape[0]
    half = share // 2
    mate, deep, far = ((row, here ^ 1), (row, here ^ 2), (row, here ^ (ring // 2)))
    owner_peers = [(row ^ k, here) for k in range(1, owners)]
    peers = [mate, deep, far] + owner_peers
    barrier = pltpu.get_barrier_semaphore()
    for peer in peers:
        pl.semaphore_signal(barrier, inc=1, device_id=peer, device_id_type=pl.DeviceIdType.MESH)
    own_load = pltpu.make_async_copy(own_ref, xs.at[0], load_sem.at[0])
    weight_load = pltpu.make_async_copy(weight_ref, ws.at[row], load_sem.at[1])
    vec_load = pltpu.make_async_copy(packed_ref, vec.at[row], load_sem.at[2])
    for load in (own_load, weight_load, vec_load):
        load.start()
    sent, stored = ([], [])
    count = [0]

    def send(source, target, peer):
        slot = count[0]
        count[0] += 1
        copy = pltpu.make_async_remote_copy(
            src_ref=source,
            dst_ref=target,
            send_sem=send_sem.at[slot],
            recv_sem=recv_sem.at[slot],
            device_id=peer,
            device_id_type=pl.DeviceIdType.MESH,
        )
        copy.start()
        sent.append(copy)
        return copy

    def store(source, target):
        copy = pltpu.make_async_copy(source, target, store_sem.at[len(stored)])
        copy.start()
        stored.append(copy)

    step = block // pieces
    parts = [pl.ds(j * step, step) for j in range(pieces)]
    pl.semaphore_wait(barrier, len(peers))
    weights = [
        send(weight_ref.at[pl.ds(core * half, half)], ws.at[row, pl.ds(core * half, half)], peer)
        for peer in owner_peers
    ]
    moved = [send(tokens_ref.at[1 - side, part], xs.at[1, part], far) for part in parts]
    own_deep = send(own_ref, xs.at[2], deep)
    own_mate = send(own_ref, xs.at[4], mate)
    vectors = [send(packed_ref, vec.at[row], peer) for peer in owner_peers]

    moved_deep, moved_mate = ([], [])
    weights_mate = []
    for j, part in enumerate(parts):
        moved[j].wait_recv()
        moved_deep.append(send(xs.at[1, part], xs.at[3, part], deep))
        moved_mate.append(send(xs.at[1, part], xs.at[5, part], mate))
        if j == pieces // 2:
            for k in range(1, owners):
                weights[k - 1].wait_recv()
                held = ws.at[row ^ k, pl.ds(core * half, half)]
                weights_mate.append(send(held, held, mate))
    own_deep.wait_recv()
    deep_mate = send(xs.at[2], xs.at[6], mate)
    for load in (own_load, weight_load, vec_load):
        load.wait()
    for copy in vectors + weights_mate:
        copy.wait_recv()
    for d in range(owners):
        store(ws.at[d], w_ref.at[d])
    store(vec, vec_ref)

    def bias(which):
        return jnp.concatenate(
            [vec[d, which : which + 1, :] for d in range(owners)], axis=1
        ).astype(f32)

    value_bias = bias(1)
    none = jnp.zeros_like(value_bias)

    def product(place, first, last):
        total = None
        for d in range(owners):
            left = xs[place, :, d * share : (d + 1) * share]
            part = dot(left, ws[d, :, first:last], 1, 0)
            total = part if total is None else total + part
        return total

    def project(place):
        store(xs.at[place], x_ref.at[place])
        if place < 2:
            qs[place] = (product(place, 0, width) + bias(0)).astype(bf16)
            store(qs.at[place], q_ref.at[place])
        kvs[place, :, :width] = product(place, width, 2 * width).astype(bf16)
        kvs[place, :, width:] = (product(place, 2 * width, 3 * width) + value_bias).astype(bf16)
        store(kvs.at[place], kv_ref.at[place])

    project(0)
    own_mate.wait_recv()
    project(4)
    project(1)
    for copy in moved_mate:
        copy.wait_recv()
    project(5)
    project(2)
    deep_mate.wait_recv()
    project(6)
    far_mate = []
    for j, part in enumerate(parts):
        moved_deep[j].wait_recv()
        far_mate.append(send(xs.at[3, part], xs.at[7, part], mate))
    project(3)
    for copy in far_mate:
        copy.wait_recv()
    project(7)
    for copy in sent:
        copy.wait_send()
    for copy in stored:
        copy.wait()


def opening(tokens, weight, packed, owners, ring):
    block, width = tokens.shape[1:]
    blocks = ring
    pieces = 4
    any_space = pl.BlockSpec(memory_space=pl.ANY)
    copies = 2 * (owners - 1) + 3 * pieces + 3 + (owners - 1) + pieces
    shapes = [
        jax.ShapeDtypeStruct((blocks, block, width), bf16),
        jax.ShapeDtypeStruct((owners,) + weight.shape, bf16),
        jax.ShapeDtypeStruct((owners,) + packed.shape, bf16),
        jax.ShapeDtypeStruct((2, block, width), bf16),
        jax.ShapeDtypeStruct((blocks, block, 2 * width), bf16),
    ]
    return pl.pallas_call(
        functools.partial(opening_kernel, owners, ring, pieces),
        in_specs=[any_space] * 3,
        out_specs=[any_space] * 5,
        out_shape=shapes,
        scratch_shapes=[pltpu.VMEM(v.shape, v.dtype) for v in shapes]
        + [
            pltpu.SemaphoreType.DMA((3,)),
            pltpu.SemaphoreType.DMA((owners + 1 + 2 * blocks + 2,)),
            pltpu.SemaphoreType.DMA((copies,)),
            pltpu.SemaphoreType.DMA((copies,)),
        ],
        compiler_params=pltpu.CompilerParams(
            vmem_limit_bytes=vmem_grant, collective_id=1, has_side_effects=True
        ),
        cost_estimate=pl.CostEstimate(
            flops=8 * blocks * block * width * width, bytes_accessed=200 << 20, transcendentals=0
        ),
        name="opening",
    )(tokens, weight, packed)


def middle_kernel(
    head_dim,
    chunk,
    mixed_ref,
    x_ref,
    cot_ref,
    live_ref,
    out_ref,
    up_ref,
    down_ref,
    vec_ref,
    up_bias_ref,
    y_ref,
    active_ref,
    hidden_ref,
    dbranch_ref,
    dupper_ref,
    dz_ref,
    dattn_ref,
    dmixed_ref,
    delta_ref,
    sums_ref,
    up_sum_ref,
    slope,
):
    width = x_ref.shape[1]
    inner = up_ref.shape[1]
    out_bias, gain_first, shift_first = (vec_ref[0:1, :], vec_ref[1:2, :], vec_ref[2:3, :])
    down_bias, gain_second, shift_second = (vec_ref[3:4, :], vec_ref[4:5, :], vec_ref[5:6, :])
    live = live_ref[...]
    mixed = mixed_ref[...]
    attn = dot(mixed, out_ref[...], 1, 0) + out_bias
    hidden, unit_first, inverse_first = norm_parts(
        x_ref[...].astype(f32) + attn, gain_first, shift_first
    )
    hidden_low = hidden.astype(bf16)
    hidden_ref[...] = hidden_low
    branch = down_bias
    for first in range(0, inner, chunk):
        part = slice(first, first + chunk)
        upper = dot(hidden_low, up_ref[:, part], 1, 0) + up_bias_ref[:, part]
        below = 0.5 + 0.5 * lax.erf(upper * (0.5**0.5))
        active = (upper * below).astype(bf16)
        bell = jnp.exp2(upper * upper * (-0.5 * log2_e)) * 0.3989422804014327
        slope[:, part] = (below + upper * bell).astype(bf16)
        active_ref[:, part] = active
        branch = branch + dot(active, down_ref[part, :], 1, 0)
    normed, unit_second, inverse_second = norm_parts(hidden + branch, gain_second, shift_second)
    result = normed * live
    y_ref[...] = result.astype(bf16)
    grad_out = cot_ref[...].astype(f32) * live
    grad_second = norm_back(grad_out * gain_second, unit_second, inverse_second)
    grad_branch = grad_second.astype(bf16)
    dbranch_ref[...] = grad_branch
    grad_hidden = grad_second
    up_sums = []
    for first in range(0, inner, chunk):
        part = slice(first, first + chunk)
        grad_active = dot(grad_branch, down_ref[part, :], 1, 1)
        grad_upper = (grad_active * slope[:, part].astype(f32)).astype(bf16)
        dupper_ref[:, part] = grad_upper
        up_sums.append(jnp.sum(grad_upper.astype(f32), axis=0, keepdims=True))
        grad_hidden = grad_hidden + dot(grad_upper, up_ref[:, part], 1, 1)
    grad_first = norm_back(grad_hidden * gain_first, unit_first, inverse_first)
    dz_ref[...] = grad_first
    grad_attn = grad_first.astype(bf16)
    dattn_ref[...] = grad_attn
    grad_mixed = dot(grad_attn, out_ref[...], 1, 1).astype(bf16)
    dmixed_ref[...] = grad_mixed
    cross = grad_mixed.astype(f32) * mixed.astype(f32)
    lane = lax.broadcasted_iota(jnp.int32, (1, lanes), 1)
    lower = lane < head_dim
    for p in range(width // lanes):
        pair = cross[:, p * lanes : (p + 1) * lanes]
        first_head = jnp.sum(jnp.where(lower, pair, 0.0), axis=1, keepdims=True)
        second_head = jnp.sum(jnp.where(lower, 0.0, pair), axis=1, keepdims=True)
        delta_ref[p] = spread_lanes(first_head, second_head, 0.0, head_dim)
    sums = [
        grad_attn.astype(f32),
        grad_hidden * unit_first,
        grad_hidden,
        grad_branch.astype(f32),
        grad_out * unit_second,
        grad_out,
        result * result,
        attn * attn * live,
        branch * branch * live,
    ]
    first_step = pl.program_id(0) == 0

    @pl.when(first_step)
    def _():
        sums_ref[...] = jnp.zeros_like(sums_ref)
        up_sum_ref[...] = jnp.zeros_like(up_sum_ref)

    for i, value in enumerate(sums):
        sums_ref[i : i + 1, :] += jnp.sum(value, axis=0, keepdims=True)
    up_sum_ref[0:1, :] += jnp.concatenate(up_sums, axis=1)


def middle(mixed, stream, cot, live, out_all, up_all, down_all, vectors, up_bias, head_dim):
    count, width = mixed.shape
    inner = up_all.shape[1]
    pairs = width // lanes
    row_step = min(256, count)
    chunk = min(768, inner)

    def fixed(shape):
        return pl.BlockSpec(shape, lambda i: (0, 0), pipeline_mode=pl.Buffered(1))

    def block(columns):
        return pl.BlockSpec((row_step, columns), lambda i: (i, 0))

    return pl.pallas_call(
        functools.partial(middle_kernel, head_dim, chunk),
        grid=(count // row_step,),
        in_specs=[
            block(width),
            block(width),
            block(width),
            block(1),
            fixed((width, width)),
            fixed((width, inner)),
            fixed((inner, width)),
            fixed(vectors.shape),
            fixed(up_bias.shape),
        ],
        out_specs=[
            block(width),
            block(inner),
            block(width),
            block(width),
            block(inner),
            block(width),
            block(width),
            block(width),
            pl.BlockSpec((pairs, row_step, lanes), lambda i: (0, i, 0)),
            pl.BlockSpec((16, width), lambda i: (0, 0)),
            pl.BlockSpec((8, inner), lambda i: (0, 0)),
        ],
        out_shape=[
            jax.ShapeDtypeStruct((count, width), bf16),
            jax.ShapeDtypeStruct((count, inner), bf16),
            jax.ShapeDtypeStruct((count, width), bf16),
            jax.ShapeDtypeStruct((count, width), bf16),
            jax.ShapeDtypeStruct((count, inner), bf16),
            jax.ShapeDtypeStruct((count, width), f32),
            jax.ShapeDtypeStruct((count, width), bf16),
            jax.ShapeDtypeStruct((count, width), bf16),
            jax.ShapeDtypeStruct((pairs, count, lanes), bf16),
            jax.ShapeDtypeStruct((16, width), f32),
            jax.ShapeDtypeStruct((8, inner), f32),
        ],
        scratch_shapes=[pltpu.VMEM((row_step, inner), bf16)],
        compiler_params=pltpu.CompilerParams(vmem_limit_bytes=vmem_grant),
        cost_estimate=pl.CostEstimate(
            flops=4 * count * width * (2 * inner + width),
            bytes_accessed=4 * width * inner + count * (18 * width + 4 * inner),
            transcendentals=4 * count * inner,
        ),
        name="middle",
    )(mixed, stream, cot, live, out_all, up_all, down_all, vectors, up_bias)


def up_out_kernel(blocks, hidden_ref, dupper_ref, mixed_ref, dattn_ref, o_ref):
    s = pl.program_id(0)

    @pl.when(s < blocks)
    def _():
        o_ref[...] = dot(hidden_ref[...], dupper_ref[...], 0, 0).astype(bf16).reshape(o_ref.shape)

    @pl.when(s == blocks)
    def _():
        o_ref[...] = dot(mixed_ref[...], dattn_ref[...], 0, 0).astype(bf16).reshape(o_ref.shape)


def down_kernel(active_ref, dbranch_ref, held_ref, o_ref):
    del held_ref
    o_ref[...] = dot(active_ref[...], dbranch_ref[...], 0, 0).astype(bf16).reshape(o_ref.shape)


def middle_grads(hidden, dupper, mixed, dattn, active, dbranch, owners, ring):
    count, width = hidden.shape
    inner = dupper.shape[1]
    devices = owners * ring
    share = width // devices
    blocks = inner // width
    tall = inner // devices
    piece = blocks * share + tall + share
    shape = jax.ShapeDtypeStruct((devices, piece, width), bf16)
    params = pltpu.CompilerParams(vmem_limit_bytes=vmem_grant)
    whole = pl.BlockSpec((count, width), lambda s: (0, 0))
    held = pl.pallas_call(
        functools.partial(up_out_kernel, blocks),
        grid=(blocks + 1,),
        in_specs=[
            whole,
            pl.BlockSpec((count, width), lambda s: (0, jnp.minimum(s, blocks - 1))),
            whole,
            whole,
        ],
        out_specs=pl.BlockSpec(
            (devices, share, width),
            lambda s: (0, jnp.where(s < blocks, s, piece // share - 1), 0),
        ),
        out_shape=shape,
        compiler_params=params,
        cost_estimate=pl.CostEstimate(
            flops=2 * count * width * (inner + width),
            bytes_accessed=2 * (count + width) * (inner + 3 * width),
            transcendentals=0,
        ),
        name="up_grads",
    )(hidden, dupper, mixed, dattn)
    return pl.pallas_call(
        down_kernel,
        grid=(owners,),
        in_specs=[
            pl.BlockSpec((count, inner // owners), lambda s: (0, s)),
            whole,
            pl.BlockSpec(memory_space=pl.ANY),
        ],
        out_specs=pl.BlockSpec((ring, tall, width), lambda s: (s, blocks * share // tall, 0)),
        out_shape=shape,
        input_output_aliases={2: 0},
        compiler_params=params,
        cost_estimate=pl.CostEstimate(
            flops=2 * count * width * inner,
            bytes_accessed=2 * (count + width) * (inner + width),
            transcendentals=0,
        ),
        name="down_grads",
    )(active, dbranch, held)


def closing_kernel(
    owners,
    ring,
    dq_ref,
    x_ref,
    share_ref,
    sum_ref,
    small_ref,
    home_ref,
    out_ref,
    small_out_ref,
    home_out_ref,
    *refs,
):
    (
        xs,
        dq,
        dkv,
        before,
        whole,
        parts,
        in_core,
        by_owner,
        in_owner,
        by_piece,
        in_piece,
        done,
        in_done,
        small,
        small_core,
        small_owner,
        small_piece,
        load_sem,
        send_sem,
        recv_sem,
    ) = refs
    row, here = (lax.axis_index("dp"), lax.axis_index("ctx"))
    core, depth = (lax.rem(here, 2), here // 2)
    deep = ring // 2
    count = dq.shape[0]
    loads = [
        pltpu.make_async_copy(dq_ref, dq, load_sem.at[0]),
        pltpu.make_async_copy(x_ref.at[pl.ds(0, count)], xs, load_sem.at[1]),
        pltpu.make_async_copy(share_ref, dkv, load_sem.at[2]),
        pltpu.make_async_copy(sum_ref, before, load_sem.at[3]),
    ]
    for load in loads:
        load.start()

    mate = (row, here ^ 1)
    owner_peers = [(row ^ k, here) for k in range(1, owners)]
    depth_peers = [(row, here ^ (2 * k)) for k in range(1, deep)]
    barrier = pltpu.get_barrier_semaphore()
    peers = [mate] + owner_peers + depth_peers
    for peer in peers:
        pl.semaphore_signal(barrier, inc=1, device_id=peer, device_id_type=pl.DeviceIdType.MESH)

    sent = []

    def send(source, target, peer, m, slot):
        copy = pltpu.make_async_remote_copy(
            src_ref=source,
            dst_ref=target,
            send_sem=send_sem.at[m, slot],
            recv_sem=recv_sem.at[m, slot],
            device_id=peer,
            device_id_type=pl.DeviceIdType.MESH,
        )
        copy.start()
        sent.append(copy)
        return copy

    at_owner = 1
    at_piece = owners
    at_done = at_piece + deep - 1
    at_back = at_done + deep - 1
    tile = 256
    out_width = whole.shape[1]

    def to_core(m):
        def one(t, carry):
            columns = pl.ds(pl.multiple_of(t * tile, tile), tile)
            if m == 0:
                whole[columns, :] = dot(xs[:, columns], dq[...].astype(bf16), 0, 0)
            else:
                held = before[columns, (m - 1) * out_width : m * out_width]
                whole[columns, :] = held + dot(xs[:, columns], dkv[m - 1], 0, 1)
            return carry

        lax.fori_loop(0, whole.shape[0] // tile, one, 0)
        parts[m] = whole[...].reshape(parts.shape[1:]).astype(bf16)
        return [send(parts.at[m, :, 1 - core], in_core.at[m], mate, m, 0)]

    def to_owner(m):
        mine = parts[m, :, core].astype(f32)
        by_owner[m] = (mine + in_core[m].astype(f32)).astype(bf16)
        return [
            send(by_owner.at[m, row ^ k], in_owner.at[m, k - 1], owner_peers[k - 1], m, at_owner + k - 1)
            for k in range(1, owners)
        ]

    def to_piece(m):
        total = by_owner[m, row].astype(f32)
        for k in range(1, owners):
            total = total + in_owner[m, k - 1].astype(f32)
        by_piece[m] = total.reshape(by_piece.shape[1:]).astype(bf16)
        return [
            send(
                by_piece.at[m, depth ^ k],
                in_piece.at[m, k - 1],
                depth_peers[k - 1],
                m,
                at_piece + k - 1,
            )
            for k in range(1, deep)
        ]

    def to_done(m):
        total = by_piece[m, depth].astype(f32)
        for k in range(1, deep):
            total = total + in_piece[m, k - 1].astype(f32)
        done[m, depth] = total.astype(bf16)
        return [
            send(done.at[m, depth], done.at[m, depth], depth_peers[k - 1], m, at_done + k - 1)
            for k in range(1, deep)
        ]

    def to_back(m):
        return [send(done.at[m], in_done.at[m], mate, m, at_back)]

    def finish(m):
        size = out_ref.shape[1]
        columns = slice(m * whole.shape[1], (m + 1) * whole.shape[1])
        out_ref[core, :, columns] = done[m].astype(f32).reshape(size, whole.shape[1])
        out_ref[1 - core, :, columns] = in_done[m].astype(f32).reshape(size, whole.shape[1])
        return []

    stages = [to_core, to_owner, to_piece, to_done, to_back, finish]
    waiting = [[], [], []]
    loads[0].wait()
    loads[1].wait()
    pl.semaphore_wait(barrier, len(peers))
    home = send(home_ref, home_out_ref, (row, here ^ (ring // 2)), 3, at_back)
    small_waits = []
    for step in range(len(stages) + 2):
        for m in range(3):
            stage = step - m
            if 0 <= stage < len(stages):
                for copy in waiting[m]:
                    copy.wait_recv()
                waiting[m] = stages[stage](m)
        if step == 0:
            small[...] = small_ref[...]
            small[0:1, :] = jnp.sum(dq[...].astype(bf16).astype(f32), axis=0, keepdims=True)
            for load in loads[2:]:
                load.wait()
            ones = jnp.ones((8, dkv.shape[2]), bf16)
            small[1:2, :] += dot(ones, dkv[1], 1, 1)[0:1, :]
            small_waits = [send(small, small_core, mate, 3, 0)]
        if step == 1:
            small_waits[0].wait_recv()
            small_owner[0] = small[...] + small_core[...]
            small_waits = [
                send(small_owner.at[0], small_owner.at[k], owner_peers[k - 1], 3, k)
                for k in range(1, owners)
            ]
        if step == 3:
            total = small_owner[0]
            for k in range(1, owners):
                small_waits[k - 1].wait_recv()
                total = total + small_owner[k]
            small_piece[0] = total
            small_waits = [
                send(small_piece.at[0], small_piece.at[k], depth_peers[k - 1], 3, at_piece + k - 1)
                for k in range(1, deep)
            ]
        if step == 5:
            total = small_piece[0]
            for k in range(1, deep):
                small_waits[k - 1].wait_recv()
                total = total + small_piece[k]
            small_out_ref[...] = total
    home.wait_recv()
    for copy in sent:
        copy.wait_send()


def closing(dq, stream, share, kv_sum, small, home, owners, ring):
    count, width = dq.shape
    deep = ring // 2
    half = width // owners // 2
    piece = half // deep
    slots = 1 + (owners - 1) + 2 * (deep - 1) + 1
    any_space = pl.BlockSpec(memory_space=pl.ANY)
    in_vmem = pl.BlockSpec(memory_space=pltpu.VMEM)
    return pl.pallas_call(
        functools.partial(closing_kernel, owners, ring),
        in_specs=[any_space] * 4 + [in_vmem, any_space],
        out_specs=[in_vmem, in_vmem, any_space],
        out_shape=[
            jax.ShapeDtypeStruct((2, half, 3 * width), f32),
            jax.ShapeDtypeStruct(small.shape, f32),
            jax.ShapeDtypeStruct(home.shape, home.dtype),
        ],
        scratch_shapes=[
            pltpu.VMEM((count, width), bf16),
            pltpu.VMEM((count, width), f32),
            pltpu.VMEM(share.shape, bf16),
            pltpu.VMEM(kv_sum.shape, f32),
            pltpu.VMEM((width, width), f32),
            pltpu.VMEM((3, owners, 2, half, width), bf16),
            pltpu.VMEM((3, owners, half, width), bf16),
            pltpu.VMEM((3, owners, half, width), bf16),
            pltpu.VMEM((3, owners - 1, half, width), bf16),
            pltpu.VMEM((3, deep, piece, width), bf16),
            pltpu.VMEM((3, deep - 1, piece, width), bf16),
            pltpu.VMEM((3, deep, piece, width), bf16),
            pltpu.VMEM((3, deep, piece, width), bf16),
            pltpu.VMEM(small.shape, f32),
            pltpu.VMEM(small.shape, f32),
            pltpu.VMEM((owners,) + small.shape, f32),
            pltpu.VMEM((deep,) + small.shape, f32),
            pltpu.SemaphoreType.DMA((4,)),
            pltpu.SemaphoreType.DMA((4, slots)),
            pltpu.SemaphoreType.DMA((4, slots)),
        ],
        compiler_params=pltpu.CompilerParams(
            vmem_limit_bytes=vmem_grant, collective_id=0, has_side_effects=True
        ),
        cost_estimate=pl.CostEstimate(
            flops=6 * count * width * width, bytes_accessed=100 << 20, transcendentals=0
        ),
        name="closing",
    )(dq, stream, share, kv_sum, small, home)


def shards(
    ring,
    tokens,
    cotangent,
    lengths,
    block_order,
    qkv_weight,
    query_bias,
    value_bias,
    out_weight,
    out_bias,
    attn_gain,
    attn_shift,
    up_weight,
    up_bias,
    down_weight,
    down_bias,
    ffn_gain,
    ffn_shift,
):
    seqs, block, width = tokens.shape
    head_dim = width // HEADS
    assert seqs == 2 and ring % 4 == 0
    half = ring // 2
    here = lax.axis_index("ctx")
    side = here // half

    def pick(array, index):
        return lax.dynamic_index_in_dim(array, index, 0, keepdims=False)

    def exchange(array, bit):
        return lax.ppermute(array, "ctx", [(i, i ^ bit) for i in range(ring)])

    def arrange(kept, other):
        first = jnp.where(side == 0, kept, other)
        second = jnp.where(side == 0, other, kept)
        return jnp.stack([first, second])

    def gather(array):
        return lax.all_gather(array, "dp", axis=0, tiled=True)

    bits = []
    bit = half // 2
    while bit:
        bits.append(bit)
        bit //= 2
    ids = jnp.stack([here, here ^ half])
    for bit in bits:
        ids = jnp.concatenate([ids, ids ^ bit])
    count_rows = 2 * block

    order = pick(block_order, side)
    length = pick(lengths, side)
    table = jnp.arange(ring, dtype=jnp.int32)
    place_of = jnp.sum(jnp.where(ids[:, None] == table[None, :], order[None, :], 0), axis=1)
    places = place_of[:, None] * block + jnp.arange(block, dtype=jnp.int32)[None, :]
    live_keys = (places < length).reshape(-1)
    live_rows = live_keys[:count_rows, None].astype(f32)
    extra = key_lanes(live_keys, head_dim)

    row = lax.axis_index("dp")
    owners = lax.axis_size("dp")
    devices = owners * ring
    inner = up_weight.shape[1]
    share = query_bias.shape[0]
    laid = ring == 8 and width % (8 * devices) == 0 and inner % width == 0 and block % 32 == 0
    singles = [
        query_bias,
        value_bias,
        out_bias,
        attn_gain,
        attn_shift,
        down_bias,
        ffn_gain,
        ffn_shift,
    ]
    ups = up_bias.reshape(-1, share)
    count_vectors = len(singles) + ups.shape[0]
    which = lax.broadcasted_iota(jnp.int32, (count_vectors, share), 0)
    packed = jnp.pad(ups, ((len(singles), 0), (0, 0)))
    for i, v in enumerate(singles):
        packed = jnp.where(which == i, v[None, :], packed)
    if laid:
        stream, qkv_all, vectors, queries, both = opening(
            tokens, qkv_weight, packed, owners, ring
        )
        stream = stream.reshape(-1, width)
        qkv_all = qkv_all.reshape(width, -1)
        vectors = vectors.astype(f32)
        queries = queries.reshape(-1, width)
        both = both.reshape(-1, 2 * width)
    else:
        qkv_all = gather(qkv_weight)
        vectors = gather(packed[None]).astype(f32)
        other = exchange(pick(tokens, 1 - side), half)
        stream = jnp.concatenate([pick(tokens, side), other], axis=0)
        for bit in bits:
            stream = jnp.concatenate([stream, exchange(stream, bit)], axis=0)
    rows = stream[:count_rows]
    bias = [vectors[:, i].reshape(1, width) for i in range(8)]
    up_bias_all = vectors[:, 8:].reshape(1, -1)
    if not laid:
        queries = (
            jnp.dot(rows, qkv_all[:, :width], preferred_element_type=f32) + bias[0]
        ).astype(bf16)
        kv_bias = jnp.concatenate([jnp.zeros_like(bias[1]), bias[1]], axis=1)
        both = jnp.dot(stream, qkv_all[:, width:], preferred_element_type=f32) + kv_bias
        both = both.astype(bf16)
    out_all = gather(out_weight)
    up_all = gather(up_weight)
    down_all = gather(down_weight)
    held, _ = lax.optimization_barrier((cotangent, stream))
    cot = jnp.concatenate([pick(held, side), exchange(pick(held, 1 - side), half)], axis=0)

    mixed, saved, factors = attend(queries, both, extra, head_dim)
    (
        result,
        active,
        hidden,
        grad_branch,
        grad_upper,
        grad_first,
        grad_attn,
        grad_mixed,
        deltas,
        sums,
        up_sum,
    ) = middle(
        mixed,
        stream,
        cot,
        live_rows,
        out_all,
        up_all,
        down_all,
        jnp.concatenate(bias[2:] + [jnp.zeros((2, width), f32)], axis=0),
        up_bias_all,
        head_dim,
    )
    output = arrange(result[:block], exchange(result[block:], half))

    def scatter(grad):
        return lax.psum_scatter(grad, ("dp", "ctx"), scatter_dimension=0, tiled=True)

    def spread(parts):
        return jax.tree.map(lambda v: lax.all_gather(v, "ctx", axis=0, tiled=True), parts)

    if laid:
        scattered = scatter(
            middle_grads(hidden, grad_upper, mixed, grad_attn, active, grad_branch, owners, ring)
        )
    else:
        grads = (dot(hidden, grad_upper, 0, 0), dot(active, grad_branch, 0, 0), dot(mixed, grad_attn, 0, 0))
        scattered = tuple(scatter(grad.astype(bf16)) for grad in grads)
    gathered = []
    kv_sums = []

    kv_weight = qkv_all[:, width:]
    size = 2 * block
    grad_queries = None
    shares = []

    def reduced(place, level):
        nonlocal grad_queries
        if level == len(bits):
            first = place * size
            if place == 0:
                weight, vector = (0.0, 0.0)
                for start, v in shares:
                    v = v.reshape(2 * width, size)
                    weight = weight + dot(stream[start : start + size], v, 0, 1)
                    vector = vector + jnp.sum(v[width:], axis=1, dtype=f32)
                held, weight, vector, grad_queries = lax.optimization_barrier(
                    (scattered, weight, vector, grad_queries)
                )
                kv_sums.extend([weight, vector])
                gathered.append(spread(held))
            grad_queries, grad_both = attend_back(
                queries,
                grad_mixed,
                deltas,
                saved,
                factors,
                both,
                extra,
                head_dim,
                first,
                size,
                grad_queries,
            )
            shares.append((first, grad_both))
            return dot(grad_both.reshape(2 * width, size), kv_weight, 0, 1)
        low = reduced(place + (1 << level), level + 1).astype(bf16)
        low, grad_queries = lax.optimization_barrier((low, grad_queries))
        other = exchange(low, bits[level])
        if level + 1 == len(bits):
            return reduced(place, level + 1) + other.astype(f32)
        if level + 2 < len(bits):
            return reduced(place, level + 1) + other.astype(f32)
        low = reduced(place + (1 << (level + 1)), level + 2).astype(bf16)
        low, other, grad_queries = lax.optimization_barrier((low, other, grad_queries))
        mate = exchange(low, bits[level + 1])
        return reduced(place, level + 2) + mate.astype(f32) + other.astype(f32)

    grad_stream = reduced(0, 0)
    grad_query_low = grad_queries.astype(bf16)
    grad_rows = grad_first + dot(grad_query_low, qkv_all[:, :width], 1, 1) + grad_stream
    grad_rows_low = grad_rows.astype(bf16)
    grad_rows_low, grad_queries, pieces = lax.optimization_barrier(
        (grad_rows_low, grad_queries, gathered[0])
    )
    if laid:
        pieces = pieces.astype(f32)
        each, tall = (width // devices, inner // devices)
        blocks = inner // width
        cut = blocks * each
        grad_up_weight = jnp.concatenate(
            [pieces[:, i * each : (i + 1) * each, :].reshape(share, width) for i in range(blocks)],
            axis=1,
        )
        grad_down_weight = pieces[:, cut : cut + tall, :].reshape(-1, width)
        grad_out_weight = pieces[:, cut + tall :, :].reshape(share, width)
    else:
        grad_up_weight, grad_down_weight, grad_out_weight = (v.astype(f32) for v in pieces)

    squares = jnp.sum(sums[6:9], axis=1)
    lane = jnp.arange(width)
    mine = (lane // 3) == (row * 2 + side)
    squares = jnp.where(
        lane % 3 == 0, squares[0], jnp.where(lane % 3 == 1, squares[1], squares[2])
    )
    squares = jnp.where(mine, squares, 0.0)[None, :]
    kv_weight_sum, value_sum = kv_sums
    last_share = shares[-1][1]
    small = jnp.concatenate(
        [
            jnp.zeros((1, width), f32),
            value_sum[None, :],
            sums[:6],
            squares,
            up_sum[0].reshape(-1, width),
        ],
        axis=0,
    )
    small = jnp.pad(small, ((0, -small.shape[0] % 8), (0, 0)))
    if laid:
        grad_qkv_weight, summed, other = closing(
            grad_queries,
            stream,
            last_share,
            kv_weight_sum,
            small,
            grad_rows_low[block:],
            owners,
            ring,
        )
        grad_qkv_weight = grad_qkv_weight.reshape(share, 3 * width)
    else:
        other = exchange(grad_rows_low[block:], half)
        kv_weight_sum = kv_weight_sum + dot(rows, last_share.reshape(2 * width, size), 0, 1)
        grad_qkv_weight = jnp.concatenate([dot(rows, grad_query_low, 0, 0), kv_weight_sum], axis=1)
        grad_qkv_weight = spread(scatter(grad_qkv_weight.astype(bf16))).astype(f32)
        grad_query_bias = jnp.sum(grad_query_low, axis=0, dtype=f32)
        value_sum = value_sum + jnp.sum(last_share[1], axis=1, dtype=f32)
        small = jnp.concatenate([grad_query_bias[None], value_sum[None], small[2:]], axis=0)
        summed = lax.psum(small, ("dp", "ctx"))

    grad_tokens = arrange(grad_rows_low[:block], other)
    totals = [lax.dynamic_slice_in_dim(summed[i], row * share, share) for i in range(8)]
    tall = inner // owners
    up_total = lax.dynamic_slice_in_dim(summed[9:].reshape(-1), row * tall, tall)
    seq_squares = lax.dynamic_slice_in_dim(summed[8], row * 6, 6).reshape(2, 3)
    branch_rms = jnp.sqrt(seq_squares / (lengths.astype(f32)[:, None] * width) + rms_eps)
    return (
        output,
        grad_tokens,
        grad_qkv_weight,
        totals[0],
        totals[1],
        grad_out_weight,
        totals[2],
        totals[3],
        totals[4],
        grad_up_weight,
        up_total,
        grad_down_weight,
        totals[5],
        totals[6],
        totals[7],
        branch_rms,
    )


def solution(mesh):
    in_specs = (
        P("dp", "ctx", None),
        P("dp", "ctx", None),
        P("dp"),
        P("dp", None),
        P("dp", None),
        P("dp"),
        P("dp"),
        P("dp", None),
        P("dp"),
        P("dp"),
        P("dp"),
        P("dp", None),
        P("dp"),
        P("dp", None),
        P("dp"),
        P("dp"),
        P("dp"),
    )
    out_specs = (
        P("dp", "ctx", None),
        P("dp", "ctx", None),
        P("dp", None),
        P("dp"),
        P("dp"),
        P("dp", None),
        P("dp"),
        P("dp"),
        P("dp"),
        P("dp", None),
        P("dp"),
        P("dp", None),
        P("dp"),
        P("dp"),
        P("dp"),
        P("dp", None),
    )
    return jax.shard_map(
        functools.partial(shards, mesh.shape["ctx"]),
        mesh=mesh,
        in_specs=in_specs,
        out_specs=out_specs,
        check_vma=False,
    )
```
